32 devices in a mesh: seg: 4 (over x, core), blk: 8 (over z, y).
Axes of the slice: x: 2, y: 2, z: 4, core: 2. Of those that a mesh axis runs over, the one named last changes fastest.
Arguments:
- start_vector: bfloat16 [4, 32, 128, 128], P('seg', 'blk'), may hold values from -6 to 6
- left_environment: bfloat16 [4, 32, 34, 128, 128], P('seg', 'blk'), may hold values from -0.5 to 0.5
- right_environment: bfloat16 [4, 32, 34, 128, 128], P('seg', 'blk'), may hold values from -0.5 to 0.5
- block_energy: float32 [4, 32], P('seg', 'blk'), may hold values from -2 to 2
- sector_rows: int32 [4, 32], P('seg', 'blk'), may hold values from 32 to 128, as said below
- sector_cols: int32 [4, 32], P('seg', 'blk'), may hold values from 32 to 128, as said below
- feed_block: int32 [4, 32, 34], P('seg', 'blk'), may hold values from 0 to 32, as said below
Outputs:
- coefficients: float32 [4, 6], P('seg')
- residual: float32 [4, 32, 128, 128], P('seg', 'blk')
The draws below stay inside these ranges and needn't reach their ends.
Inputs may be any that keep to these rules, and one draw needn't show every extreme that they name: `sector_rows`: the first block of every segment fills its tile. `sector_cols`: the first block of every segment fills its tile. `feed_block`: 32 marks an absent channel; absent channels come after the present ones of a block, and the first block of every segment has all 34 channels.
All inputs are finite; a program needn't handle non-finite values.
Results may differ from the reference program's by a relative error of at most 0.014.
Values may be sent and summed in bfloat16 or wider, within the bound.
No kernel may reach another device: no remote copies, remote signals or barrier semaphores. Data moves between devices by JAX's collectives and lax.ppermute only.
A program may use at most 128 MiB of HBM per device.

```python
import jax
import jax.numpy as jnp
from jax import lax

TILE = 128
NB_DEV = 4
MW = 34
STEPS = 3
NB = 32
NSEG = 4
N_BLK = 8


def draw_sector_rows(key, part):
    sizes = jax.random.randint(key, (NSEG, NB), TILE // 4, TILE + 1)
    return sizes.at[:, 0].set(TILE).astype(jnp.int32)


def draw_sector_cols(key, part):
    sizes = jax.random.randint(jax.random.fold_in(key, 7), (NSEG, NB), TILE // 4, TILE + 1)
    return sizes.at[:, 0].set(TILE).astype(jnp.int32)


def draw_feed_block(key, part):
    first_key, second_key = jax.random.split(jax.random.fold_in(key, 11))
    present = jax.random.randint(first_key, (NSEG, NB, 1), 3 * MW // 4, MW + 1)
    present = present.at[:, 0, :].set(MW)
    goals = jax.random.randint(second_key, (NSEG, NB, MW), 0, NB)
    channel = jnp.arange(MW, dtype=jnp.int32)
    return jnp.where(channel[None, None, :] < present, goals, NB).astype(jnp.int32)


def block_levels(own_key, dims, cuts, low, top_value):
    level, own = 1.0, jax.random.fold_in(own_key, 6)
    for axis_at, blocks in cuts:
        steps = jnp.exp(jax.random.uniform(jax.random.fold_in(own, axis_at), (blocks,), jnp.float32, low / len(cuts), top_value / len(cuts)))
        level = level * jnp.repeat(steps, dims[axis_at] // blocks).reshape([-1 if axis == axis_at else 1 for axis in range(len(dims))])
    return level


def bell_draw(key, dims, deviation, reach, shards=(), kind=jnp.bfloat16):
    loudness = block_levels(key, dims, shards, -0.22, 0.18) if shards else 1.0
    drawn = jax.random.normal(key, dims, jnp.float32) * deviation * loudness
    return jnp.minimum(jnp.maximum(drawn, -reach), reach).astype(kind)


def setup_inputs(seed: int = 0) -> dict:
    arg_keys = jax.random.split(jax.random.key(seed), 8)
    return {
        "start_vector": bell_draw(arg_keys[0], (NSEG, NB, TILE, TILE), 1.0, 6.0, ((0, 4), (1, 8))),
        "left_environment": bell_draw(arg_keys[1], (NSEG, NB, MW, TILE, TILE), TILE ** -0.5, 0.5, ((0, 4), (1, 8))),
        "right_environment": bell_draw(arg_keys[2], (NSEG, NB, MW, TILE, TILE), TILE ** -0.5, 0.5, ((0, 4), (1, 8))),
        "block_energy": jnp.clip(jax.random.uniform(arg_keys[3], (NSEG, NB), jnp.float32, -2.0, 2.0) * block_levels(arg_keys[3], (NSEG, NB), ((0, 4), (1, 8)), -0.4, 0.0), -2.0, 2.0),
        "sector_rows": draw_sector_rows(jax.random.fold_in(arg_keys[7], 71), 0),
        "sector_cols": draw_sector_cols(jax.random.fold_in(arg_keys[7], 71), 0),
        "feed_block": draw_feed_block(jax.random.fold_in(arg_keys[7], 71), 0),
    }


epsilon = 1e-06

def live_mask(rows_live, cols_live):
    positions = jnp.arange(TILE, dtype=jnp.int32)
    row_mask = (positions[None, :] < rows_live[:, None]).astype(jnp.float32)
    col_mask = (positions[None, :] < cols_live[:, None]).astype(jnp.float32)
    return row_mask[:, :, None] * col_mask[:, None, :]

def apply_operator(vector, left_tiles, right_tiles, energy, feeds, mask_tiles):
    low_vector = lax.optimization_barrier(vector.astype(jnp.bfloat16)).astype(jnp.float32)
    half_product = jnp.einsum('kwab,kbc->kwac', left_tiles.astype(jnp.float32), low_vector)
    half_product = lax.optimization_barrier(half_product.astype(jnp.bfloat16)).astype(jnp.float32)
    contrib = jnp.einsum('kwac,kwcd->kwad', half_product, right_tiles.astype(jnp.float32))
    contrib = contrib.reshape(N_BLK, NB_DEV * MW, TILE * TILE)
    selector = (feeds.reshape(1, NB * MW) == jnp.arange(NB, dtype=jnp.int32)[:, None]).astype(jnp.float32)
    selector = selector.reshape(NB, N_BLK, NB_DEV * MW)
    partial_value = jnp.einsum('tgp,gpe->gte', selector, contrib, precision=lax.Precision.HIGHEST)
    partial_value = lax.optimization_barrier(partial_value.astype(jnp.bfloat16)).astype(jnp.float32)
    summed = lax.optimization_barrier(jnp.sum(partial_value, axis=0)).reshape(NB, TILE, TILE)
    return mask_tiles * summed + energy[:, None, None] * vector

def lanczos(start_tiles, left_tiles, right_tiles, energy, rows_live, cols_live, feeds):
    mask_tiles = live_mask(rows_live, cols_live)
    entries = float(NB * TILE * TILE)
    vector = mask_tiles * start_tiles.astype(jnp.float32)
    vector = vector * lax.rsqrt(jnp.sum(vector * vector) / entries + epsilon)
    before = jnp.zeros_like(vector)
    coef_beta = jnp.float32(0.0)
    alphas = []
    betas = []
    image = vector
    for turn_index in range(STEPS):
        image = apply_operator(vector, left_tiles, right_tiles, energy, feeds, mask_tiles)
        coef_alpha = jnp.sum(vector * image) / entries
        image = image - coef_alpha * vector - coef_beta * before
        mean_square = jnp.sum(image * image) / entries
        coef_beta = jnp.sqrt(mean_square)
        before = vector
        vector = image * lax.rsqrt(mean_square + epsilon)
        alphas.append(coef_alpha)
        betas.append(coef_beta)
    return (jnp.stack(alphas + betas).astype(jnp.float32), image)

def reference(start_vector, left_environment, right_environment, block_energy, sector_rows, sector_cols, feed_block):

    def pick_segment(array, segment):
        return lax.dynamic_index_in_dim(array, segment, 0, keepdims=False)

    def one_segment(segment):
        earlier = jnp.maximum(segment - 1, 0).astype(jnp.int32)
        left_tiles = pick_segment(left_environment, earlier)
        left_tiles = jnp.where(segment > 0, left_tiles, jnp.zeros_like(left_tiles))
        return lanczos(pick_segment(start_vector, segment), left_tiles, pick_segment(right_environment, segment), pick_segment(block_energy, segment), pick_segment(sector_rows, segment), pick_segment(sector_cols, segment), pick_segment(feed_block, segment))
    coefficients, residual = lax.map(one_segment, jnp.arange(NSEG, dtype=jnp.int32))
    return (coefficients, residual)
```

```python
import functools

import jax
import jax.numpy as jnp
from jax import lax
from jax.experimental import pallas as pl
from jax.experimental.pallas import tpu as pltpu
from jax.sharding import PartitionSpec as P

epsilon = 1e-06
F32 = jnp.float32
BF16 = jnp.bfloat16
PAD = 16
VMEM = pltpu.VMEM
SMEM = pltpu.SMEM


def passed_along(block, axis, distance):
    devices = range(lax.axis_size(axis))
    route = [(i - distance, i) for i in devices if i - distance in devices]
    return lax.ppermute(block, axis, route)


def swapped(block, mask):
    return lax.ppermute(block, "blk", [(i, i ^ mask) for i in range(lax.axis_size("blk"))])


class Plan:
    def __init__(self, tiles, channels, tile, blk):
        self.T, self.W, self.D, self.B = tiles, channels, tile, blk
        self.Z = blk // 2
        self.Ta = tiles // 2
        self.Tb = tiles - self.Ta
        self.entries = float(tiles * blk * tile * tile)
        self.n = tiles * blk
        self.wc = next(c for c in range(max(1, channels // 2), 0, -1) if channels % c == 0)

    def slots(self, feeds, me):
        device = feeds // self.T
        tile = feeds % self.T
        zr = (device // 2) ^ (me // 2)
        yr = (device % 2) ^ (me % 2)
        a = yr * (self.Z * self.Ta) + zr * self.Ta + tile
        b = 2 * self.Z * self.Ta + zr * (2 * self.Tb) + yr * self.Tb + (tile - self.Ta)
        return jnp.where(feeds >= self.n, self.n, jnp.where(tile < self.Ta, a, b)).astype(jnp.int32)


def packed_row(scalars, tile):
    lane = lax.broadcasted_iota(jnp.int32, (1, tile), 1)
    row = jnp.zeros((1, tile), F32)
    for index, value in enumerate(scalars):
        row = row + jnp.where(lane == index, value, 0.0)
    return split_row(row, tile)


def split_row(row, tile):
    high = row.astype(BF16).astype(F32)
    middle = (row - high).astype(BF16).astype(F32)
    low = row - high - middle
    at = lax.broadcasted_iota(jnp.int32, (PAD, tile), 0)
    rows = jnp.where(at == 0, high, jnp.where(at == 1, middle, jnp.where(at == 2, low, 0.0)))
    return rows.astype(BF16)


def joined_row(rows):
    rows = rows.astype(F32)
    return rows[0:1] + rows[1:2] + rows[2:3]


def total(value):
    return jnp.sum(value, keepdims=True).reshape(1, 1)


def live_mask(plan, rows_ref, cols_ref, k):
    down = lax.broadcasted_iota(jnp.int32, (plan.D, plan.D), 0)
    across = lax.broadcasted_iota(jnp.int32, (plan.D, plan.D), 1)
    return jnp.logical_and(down < rows_ref[k], across < cols_ref[k])


def received_sums(plan, arrived):
    a_parts, b_parts = arrived[: plan.Z], arrived[plan.Z :]
    D = plan.D

    def tile(k):
        if k < plan.Ta:
            parts = [p[pl.ds(k * D, D), :].astype(F32) for p in a_parts]
        else:
            parts = [p[pl.ds((k - plan.Ta) * D, D), :].astype(F32) for p in b_parts]
        return functools.reduce(lambda x, y: x + y, parts)

    level = [joined_row(p[pl.ds(plan.Ta * D, PAD), :]) for p in a_parts]
    while len(level) > 1:
        level = [level[i] + level[i + 1] for i in range(0, len(level), 2)]
    return tile, level[0]


def lane(row, index):
    return row[:, index : index + 1]


def shift_of(plan, a, b, d, e):
    alpha = a / plan.entries
    m = jnp.maximum(b - 2.0 * alpha * d + alpha * alpha * e, 0.0) / plan.entries
    return alpha, m


def update_first(plan, ins, outs, send):
    (start, rows, cols, energy), (x_out,) = ins, outs
    norm = jnp.zeros((1, 1), F32)
    for k in range(plan.T):
        at = pl.ds(k * plan.D, plan.D)
        x = jnp.where(live_mask(plan, rows, cols, k), start[at, :].astype(F32), 0.0)
        x_out[at, :] = x
        send(k, x)
        norm = norm + total(x * x)
    return [norm]


def update_second(plan, ins, outs, send):
    (x_in, rows, cols, energy), arrived = ins[:4], ins[4:]
    q_out, h_out, known_out = outs
    tile, row = received_sums(plan, arrived)
    square = lane(row, 0)
    scale = lax.rsqrt(square / plan.entries + epsilon)
    known_out[...] = jnp.broadcast_to(scale * scale * square, known_out.shape)
    a = b = jnp.zeros((1, 1), F32)
    for k in range(plan.T):
        at = pl.ds(k * plan.D, plan.D)
        x = x_in[at, :]
        image = jnp.where(live_mask(plan, rows, cols, k), tile(k), 0.0) + energy[k] * x
        q = scale * x
        h = scale * image
        q_out[at, :] = q
        h_out[at, :] = h
        send(k, h)
        a = a + total(q * h)
        b = b + total(h * h)
    return [a, b]


def update_third(plan, ins, outs, send):
    (q_in, h_in, known, rows, cols, energy), arrived = ins[:6], ins[6:]
    q_out, h_out, z_out, coef_out = outs
    tile, row = received_sums(plan, arrived)
    a, b = lane(row, 0), lane(row, 1)
    alpha, m = shift_of(plan, a, b, a, known[0:1, 0:1])
    beta, scale = jnp.sqrt(m), lax.rsqrt(m + epsilon)
    coef_out[0:1, :] = jnp.broadcast_to(alpha, (1, plan.D))
    coef_out[1:2, :] = jnp.broadcast_to(beta, (1, plan.D))
    sums = [jnp.zeros((1, 1), F32)] * 4
    for k in range(plan.T):
        at = pl.ds(k * plan.D, plan.D)
        q0, h0 = q_in[at, :], h_in[at, :]
        image = jnp.where(live_mask(plan, rows, cols, k), tile(k), 0.0) + energy[k] * h0
        q = scale * (h0 - alpha * q0)
        h = scale * (image - alpha * h0)
        z = h - beta * q0
        q_out[at, :] = q
        h_out[at, :] = h
        z_out[at, :] = z
        send(k, z)
        sums = [s + total(p) for s, p in zip(sums, (q * h, z * z, z * q, q * q))]
    return sums


def update_last(plan, ins, outs, send):
    (q_in, h_in, z_in, rows, cols, energy), arrived = ins[:6], ins[6:]
    q_out, z_out, coef_out = outs
    tile, row = received_sums(plan, arrived)
    alpha, m = shift_of(plan, *[lane(row, i) for i in range(4)])
    beta, scale = jnp.sqrt(m), lax.rsqrt(m + epsilon)
    coef_out[0:1, :] = jnp.broadcast_to(alpha, (1, plan.D))
    coef_out[1:2, :] = jnp.broadcast_to(beta, (1, plan.D))
    sums = [jnp.zeros((1, 1), F32)] * 4
    for k in range(plan.T):
        at = pl.ds(k * plan.D, plan.D)
        q1, h1, z1 = q_in[at, :], h_in[at, :], z_in[at, :]
        image = jnp.where(live_mask(plan, rows, cols, k), tile(k), 0.0) + energy[k] * z1
        q = scale * (z1 - alpha * q1)
        h = scale * (image - alpha * h1)
        z = h - beta * q1
        q_out[at, :] = q
        z_out[at, :] = z
        sums = [s + total(p) for s, p in zip(sums, (q * h, z * z, z * q, q * q))]
    return sums


def whole(shape, space=VMEM):
    return pl.BlockSpec(shape, lambda *_: (0,) * len(shape), memory_space=space)


def message_shapes(plan):
    D = plan.D
    a = jax.ShapeDtypeStruct((plan.Z * plan.Ta * D + PAD, D), BF16)
    b = jax.ShapeDtypeStruct((2 * plan.Tb * D, D), BF16)
    return [a, a] + [b] * plan.Z


def operator_step(plan, name, update, ins, spaces, state_shapes, left, right, slots):
    D, T, wc = plan.D, plan.T, plan.wc
    per_tile = plan.W // wc
    messages = message_shapes(plan)
    n_in, n_state, n_msg = len(ins), len(state_shapes), len(messages)

    def body(*refs):
        in_refs = refs[:n_in]
        left_ref, right_ref, slot_ref = refs[n_in : n_in + 3]
        state_refs = refs[n_in + 3 : n_in + 3 + n_state]
        message_refs = refs[n_in + 3 + n_state : n_in + 3 + n_state + n_msg]
        low_ref, half_ref, sum_ref = refs[n_in + 3 + n_state + n_msg :]
        step = pl.program_id(0)

        @pl.when(step == 0)
        def _():
            def send(k, value):
                low_ref[pl.ds(k * D, D), :] = value.astype(BF16)

            scalars = update(plan, in_refs, state_refs, send)
            row = packed_row(scalars, D)
            message_refs[0][pl.ds(plan.Z * plan.Ta * D, PAD), :] = row
            message_refs[1][pl.ds(plan.Z * plan.Ta * D, PAD), :] = row
            sum_ref[...] = jnp.zeros(sum_ref.shape, F32)

        tile = step // per_tile
        low = low_ref[pl.ds(pl.multiple_of(tile * D, D), D), :]
        half_ref[...] = jnp.dot(left_ref[...], low, preferred_element_type=F32).astype(BF16)
        for w in range(wc):
            product = jnp.dot(
                half_ref[pl.ds(w * D, D), :],
                right_ref[pl.ds(w * D, D), :],
                preferred_element_type=F32,
            )
            slot = slot_ref[step * wc + w]
            at = pl.ds(pl.multiple_of(slot * D, D), D)
            sum_ref[at, :] += product

        @pl.when(step == T * per_tile - 1)
        def _():
            first = 0
            for ref in message_refs:
                rows = ref.shape[0] // D * D
                ref[pl.ds(0, rows), :] = sum_ref[pl.ds(first, rows), :].astype(BF16)
                first += rows

    stream = pl.BlockSpec((wc * D, D), lambda i: (i, 0))
    outs = list(state_shapes) + messages
    results = pl.pallas_call(
        body,
        grid=(T * per_tile,),
        in_specs=[whole(x.shape, s) for x, s in zip(ins, spaces)]
        + [stream, stream, whole(slots.shape, SMEM)],
        out_specs=[whole(s.shape) for s in outs],
        out_shape=outs,
        scratch_shapes=[
            VMEM((T * D, D), BF16),
            VMEM((wc * D, D), BF16),
            VMEM(((plan.n + 1) * D, D), F32),
        ],
        name=name,
    )(*ins, left, right, slots)
    return results[:n_state], results[n_state:]


def last_step(plan, ins, spaces, state_shapes):
    n_in = len(ins)
    row = jax.ShapeDtypeStruct((8, plan.D), F32)

    def body(*refs):
        outs = refs[n_in:-1]
        sums = update_last(plan, refs[:n_in], outs, None)
        across = lax.broadcasted_iota(jnp.int32, (8, plan.D), 1)
        packed = jnp.zeros((8, plan.D), F32)
        for index, value in enumerate(sums):
            packed = packed + jnp.where(across == index, value, 0.0)
        refs[-1][...] = packed

    outs = list(state_shapes) + [row]
    return pl.pallas_call(
        body,
        in_specs=[whole(x.shape, s) for x, s in zip(ins, spaces)],
        out_specs=[whole(s.shape) for s in outs],
        out_shape=outs,
        name="last_step",
    )(*ins)


def middle_a(plan, keep, got):
    rows = plan.Ta * plan.D

    def body(keep_ref, got_ref, *outs):
        end = pl.ds(plan.Z * rows, PAD)
        scalars = split_row(joined_row(keep_ref[end, :]) + joined_row(got_ref[end, :]), plan.D)
        for z, out in enumerate(outs):
            at = pl.ds(z * rows, rows)
            added = keep_ref[at, :].astype(F32) + got_ref[at, :].astype(F32)
            out[pl.ds(0, rows), :] = added.astype(BF16)
            out[pl.ds(rows, PAD), :] = scalars

    shape = jax.ShapeDtypeStruct((rows + PAD, plan.D), BF16)
    return pl.pallas_call(
        body,
        in_specs=[whole(keep.shape)] * 2,
        out_specs=[whole(shape.shape)] * plan.Z,
        out_shape=[shape] * plan.Z,
        name="middle_a",
    )(keep, got)


def middle_b(plan, parts):
    rows = plan.Tb * plan.D

    def body(*refs):
        outs = refs[plan.Z :]
        for y, out in enumerate(outs):
            at = pl.ds(y * rows, rows)
            added = functools.reduce(
                lambda x, z: x + z, [p[at, :].astype(F32) for p in refs[: plan.Z]]
            )
            out[...] = added.astype(out.dtype)

    shapes = [jax.ShapeDtypeStruct((rows, plan.D), d) for d in (F32, BF16)]
    return pl.pallas_call(
        body,
        in_specs=[whole(parts[0].shape)] * plan.Z,
        out_specs=[whole(s.shape) for s in shapes],
        out_shape=shapes,
        name="middle_b",
    )(*parts)


def exchanged(plan, messages):
    a_keep, a_send = messages[:2]
    b_parts = messages[2:]
    others = range(plan.Z - 1, 0, -1)
    a_got = swapped(a_send, 1)
    b_got = [swapped(b_parts[z], 2 * z) for z in others]
    a_parts = middle_a(plan, a_keep, a_got)
    a_last = [swapped(a_parts[z], 2 * z) for z in others][::-1]
    b_keep, b_send = middle_b(plan, [b_parts[0]] + b_got)
    b_last = swapped(b_send, 1)
    return [a_parts[0]] + a_last + [b_keep, b_last]


def local(
    start_vector,
    left_environment,
    right_environment,
    block_energy,
    sector_rows,
    sector_cols,
    feed_block,
):
    T, W, D = left_environment.shape[1:4]
    plan = Plan(T, W, D, lax.axis_size("blk"))
    left = passed_along(left_environment, "seg", 1).reshape(T * W * D, D)
    right = right_environment.reshape(T * W * D, D)
    slots = plan.slots(feed_block.reshape(T * W), lax.axis_index("blk"))
    sizes = [sector_rows[0], sector_cols[0], block_energy[0]]
    scalar = [SMEM] * 3
    vector = jax.ShapeDtypeStruct((T * D, D), F32)
    row = jax.ShapeDtypeStruct((8, D), F32)
    start = start_vector.reshape(T * D, D)

    (x,), messages = operator_step(
        plan, "step_0", update_first, [start] + sizes, [VMEM] + scalar, [vector], left, right, slots
    )
    arrived = exchanged(plan, messages)
    (q0, h0, known), messages = operator_step(
        plan,
        "step_1",
        update_second,
        [x] + sizes + arrived,
        [VMEM] + scalar + [VMEM] * len(arrived),
        [vector, vector, row],
        left,
        right,
        slots,
    )
    arrived = exchanged(plan, messages)
    (q1, h1, z1, first), messages = operator_step(
        plan,
        "step_2",
        update_third,
        [q0, h0, known] + sizes + arrived,
        [VMEM] * 3 + scalar + [VMEM] * len(arrived),
        [vector, vector, vector, row],
        left,
        right,
        slots,
    )
    arrived = exchanged(plan, messages)
    q2, z2, second, sums = last_step(
        plan,
        [q1, h1, z1] + sizes + arrived,
        [VMEM] * 3 + scalar + [VMEM] * len(arrived),
        [vector, vector, row],
    )
    mask = 1
    while mask < plan.B:
        sums = sums + swapped(sums, mask)
        mask *= 2
    alpha, m = shift_of(plan, *[sums[0, i] for i in range(4)])
    residual = z2 - alpha * q2
    coefficients = jnp.stack(
        [first[0, 0], second[0, 0], alpha, first[1, 0], second[1, 0], jnp.sqrt(m)]
    )
    return (coefficients[None, :], residual.reshape(1, T, D, D))


def solution(mesh):
    return jax.shard_map(
        local,
        mesh=mesh,
        in_specs=(
            P("seg", "blk", None, None),
            P("seg", "blk", None, None, None),
            P("seg", "blk", None, None, None),
            P("seg", "blk"),
            P("seg", "blk"),
            P("seg", "blk"),
            P("seg", "blk", None),
        ),
        out_specs=(P("seg", None), P("seg", "blk", None, None)),
        check_vma=False,
    )
```

```python
import functools

import jax
import jax.numpy as jnp
from jax import lax
from jax.experimental import pallas as pl
from jax.experimental.pallas import tpu as pltpu
from jax.sharding import PartitionSpec as P

epsilon = 1e-06
F32 = jnp.float32
BF16 = jnp.bfloat16
PAD = 16
VMEM = pltpu.VMEM
SMEM = pltpu.SMEM


def passed_along(block, axis, distance):
    devices = range(lax.axis_size(axis))
    route = [(i - distance, i) for i in devices if i - distance in devices]
    return lax.ppermute(block, axis, route)


def swapped(block, mask):
    return lax.ppermute(block, "blk", [(i, i ^ mask) for i in range(lax.axis_size("blk"))])


class Plan:
    def __init__(self, tiles, channels, tile, blk):
        self.T, self.W, self.D, self.B = tiles, channels, tile, blk
        self.Z = blk // 2
        self.entries = float(tiles * blk * tile * tile)
        self.n = tiles * blk
        self.part = tiles * tile
        self.half = self.Z * self.part

    def slots(self, feeds, me):
        device = feeds // self.T
        zr = (device // 2) ^ (me // 2)
        yr = (device % 2) ^ (me % 2)
        slot = (yr * self.Z + zr) * self.T + feeds % self.T
        return jnp.where(feeds >= self.n, self.n, slot).astype(jnp.int32)


def packed_row(scalars, tile):
    lane = lax.broadcasted_iota(jnp.int32, (1, tile), 1)
    row = jnp.zeros((1, tile), F32)
    for index, value in enumerate(scalars):
        row = row + jnp.where(lane == index, value, 0.0)
    return split_row(row, tile)


def split_row(row, tile):
    high = row.astype(BF16).astype(F32)
    middle = (row - high).astype(BF16).astype(F32)
    low = row - high - middle
    at = lax.broadcasted_iota(jnp.int32, (PAD, tile), 0)
    rows = jnp.where(at == 0, high, jnp.where(at == 1, middle, jnp.where(at == 2, low, 0.0)))
    return rows.astype(BF16)


def joined_row(rows):
    rows = rows.astype(F32)
    return rows[0:1] + rows[1:2] + rows[2:3]


def total(value):
    return jnp.sum(value, keepdims=True).reshape(1, 1)


def live_mask(plan, sizes, k):
    down = lax.broadcasted_iota(jnp.int32, (plan.D, plan.D), 0)
    across = lax.broadcasted_iota(jnp.int32, (plan.D, plan.D), 1)
    return jnp.logical_and(down < sizes[k], across < sizes[plan.T + k])


def received_sums(plan, parts):
    def tile(k):
        at = pl.ds(k * plan.D, plan.D)
        return functools.reduce(lambda x, y: x + y, [p[at, :].astype(F32) for p in parts])

    level = [joined_row(p[pl.ds(plan.part, PAD), :]) for p in parts]
    while len(level) > 1:
        level = [level[i] + level[i + 1] for i in range(0, len(level), 2)]
    return tile, level[0]


def lane(row, index):
    return row[:, index : index + 1]


def shift_of(plan, a, b, d, e):
    alpha = a / plan.entries
    m = jnp.maximum(b - 2.0 * alpha * d + alpha * alpha * e, 0.0) / plan.entries
    return alpha, m


def update_first(plan, ins, outs, send):
    (start, sizes, energy), (x_out,) = ins, outs
    norm = jnp.zeros((1, 1), F32)
    for k in range(plan.T):
        at = pl.ds(k * plan.D, plan.D)
        x = jnp.where(live_mask(plan, sizes, k), start[at, :].astype(F32), 0.0)
        x_out[at, :] = x
        send(k, x)
        norm = norm + total(x * x)
    return [norm]


def update_second(plan, ins, outs, send):
    (x_in, sizes, energy), arrived = ins[:3], ins[3:]
    q_out, h_out, known_out = outs
    tile, row = received_sums(plan, arrived)
    square = lane(row, 0)
    scale = lax.rsqrt(square / plan.entries + epsilon)
    known_out[...] = jnp.broadcast_to(scale * scale * square, known_out.shape)
    a = b = jnp.zeros((1, 1), F32)
    for k in range(plan.T):
        at = pl.ds(k * plan.D, plan.D)
        x = x_in[at, :]
        image = jnp.where(live_mask(plan, sizes, k), tile(k), 0.0) + energy[k] * x
        q = scale * x
        h = scale * image
        q_out[at, :] = q
        h_out[at, :] = h
        send(k, h)
        a = a + total(q * h)
        b = b + total(h * h)
    return [a, b]


def update_third(plan, ins, outs, send):
    (q_in, h_in, known, sizes, energy), arrived = ins[:5], ins[5:]
    q_out, h_out, z_out, coef_out = outs
    tile, row = received_sums(plan, arrived)
    a, b = lane(row, 0), lane(row, 1)
    alpha, m = shift_of(plan, a, b, a, known[0:1, 0:1])
    beta, scale = jnp.sqrt(m), lax.rsqrt(m + epsilon)
    coef_out[0:1, :] = jnp.broadcast_to(alpha, (1, plan.D))
    coef_out[1:2, :] = jnp.broadcast_to(beta, (1, plan.D))
    sums = [jnp.zeros((1, 1), F32)] * 4
    for k in range(plan.T):
        at = pl.ds(k * plan.D, plan.D)
        q0, h0 = q_in[at, :], h_in[at, :]
        image = jnp.where(live_mask(plan, sizes, k), tile(k), 0.0) + energy[k] * h0
        q = scale * (h0 - alpha * q0)
        h = scale * (image - alpha * h0)
        z = h - beta * q0
        q_out[at, :] = q
        h_out[at, :] = h
        z_out[at, :] = z
        send(k, z)
        sums = [s + total(p) for s, p in zip(sums, (q * h, z * z, z * q, q * q))]
    return sums


def update_last(plan, ins, outs, send):
    (q_in, h_in, z_in, sizes, energy), arrived = ins[:5], ins[5:]
    q_out, z_out, coef_out = outs
    tile, row = received_sums(plan, arrived)
    alpha, m = shift_of(plan, *[lane(row, i) for i in range(4)])
    beta, scale = jnp.sqrt(m), lax.rsqrt(m + epsilon)
    coef_out[0:1, :] = jnp.broadcast_to(alpha, (1, plan.D))
    coef_out[1:2, :] = jnp.broadcast_to(beta, (1, plan.D))
    sums = [jnp.zeros((1, 1), F32)] * 4
    for k in range(plan.T):
        at = pl.ds(k * plan.D, plan.D)
        q1, h1, z1 = q_in[at, :], h_in[at, :], z_in[at, :]
        image = jnp.where(live_mask(plan, sizes, k), tile(k), 0.0) + energy[k] * z1
        q = scale * (z1 - alpha * q1)
        h = scale * (image - alpha * h1)
        z = h - beta * q1
        q_out[at, :] = q
        z_out[at, :] = z
        sums = [s + total(p) for s, p in zip(sums, (q * h, z * z, z * q, q * q))]
    return sums


def on_chip(name, body, ins, outs, scratch=()):
    spaces = [SMEM if len(x.shape) == 1 else VMEM for x in ins]
    return pl.pallas_call(
        body,
        in_specs=[pl.BlockSpec(memory_space=s) for s in spaces],
        out_specs=[pl.BlockSpec(memory_space=VMEM)] * len(outs),
        out_shape=list(outs),
        scratch_shapes=list(scratch),
        compiler_params=pltpu.CompilerParams(vmem_limit_bytes=16 * 2**20),
        name=name,
    )(*ins)


def operator_step(plan, name, update, ins, state_shapes, left, right):
    D, T, W = plan.D, plan.T, plan.W
    pairs = T // 2
    message = jax.ShapeDtypeStruct((plan.half + PAD, D), BF16)
    n_in, n_state = len(ins), len(state_shapes)
    group = next(c for c in range(max(1, W // 2), 0, -1) if W % c == 0)

    def body(*refs):
        in_refs = refs[:n_in]
        left_ref, right_ref = refs[n_in : n_in + 2]
        state_refs = refs[n_in + 2 : n_in + 2 + n_state]
        keep_ref, send_ref, low_ref, half_ref, sum_ref = refs[n_in + 2 + n_state :]
        sizes = next(r for r in in_refs if len(r.shape) == 1 and r.dtype == jnp.int32)

        def send(k, value):
            low_ref[pl.ds(k * D, D), :] = value.astype(BF16)

        row = packed_row(update(plan, in_refs, state_refs, send), D)
        for ref in (keep_ref, send_ref):
            ref[pl.ds(plan.half, PAD), :] = row
        sum_ref[...] = jnp.zeros(sum_ref.shape, F32)
        none = jnp.zeros((D, D), BF16)

        def several(step, carry):
            for h in range(pairs):
                blocks = (h, h + pairs)
                v = [low_ref[pl.ds(k * D, D), :] for k in blocks]
                both = jnp.concatenate(
                    [jnp.concatenate([v[0], none], 1), jnp.concatenate([none, v[1]], 1)], 0
                )
                firsts = [k * W + step * group for k in blocks]
                tiles = [
                    left_ref[pl.ds(pl.multiple_of(f * D, D), group * D), :] for f in firsts
                ]
                half_ref[...] = jnp.dot(
                    jnp.concatenate(tiles, 1), both, preferred_element_type=F32
                ).astype(BF16)
                for w in range(group):
                    for side, f in enumerate(firsts):
                        product = jnp.dot(
                            half_ref[pl.ds(w * D, D), pl.ds(side * D, D)],
                            right_ref[pl.ds(pl.multiple_of((f + w) * D, D), D), :],
                            preferred_element_type=F32,
                        )
                        slot = sizes[2 * T + f + w]
                        at = pl.ds(pl.multiple_of(slot * D, D), D)
                        sum_ref[at, :] += product
            return carry

        lax.fori_loop(0, W // group, several, 0)
        for first, ref in ((0, keep_ref), (plan.half, send_ref)):
            ref[pl.ds(0, plan.half), :] = sum_ref[pl.ds(first, plan.half), :].astype(BF16)

    results = on_chip(
        name,
        body,
        list(ins) + [left, right],
        list(state_shapes) + [message] * 2,
        [
            VMEM((T * D, D), BF16),
            VMEM((group * D, 2 * D), BF16),
            VMEM(((plan.n + 1) * D, D), F32),
        ],
    )
    return results[:n_state], results[n_state:]


def row_of(plan, values):
    across = lax.broadcasted_iota(jnp.int32, (8, plan.D), 1)
    row = jnp.zeros((8, plan.D), F32)
    for index, value in enumerate(values):
        row = row + jnp.where(across == index, value, 0.0)
    return row


def last_step(plan, ins, state_shapes):
    n_in = len(ins)

    def body(*refs):
        sums = update_last(plan, refs[:n_in], refs[n_in:-1], None)
        refs[-1][...] = row_of(plan, sums)

    row = jax.ShapeDtypeStruct((8, plan.D), F32)
    return on_chip("last_step", body, ins, list(state_shapes) + [row])


def outcome(plan, q, z, first, second, *sums):
    def body(q_ref, z_ref, first_ref, second_ref, *refs):
        added = functools.reduce(lambda x, y: x + y, [r[0:1, :] for r in refs[:-2]])
        residual_ref, coef_ref = refs[-2:]
        alpha, m = shift_of(plan, *[lane(added, i) for i in range(4)])
        residual_ref[...] = z_ref[...] - alpha * q_ref[...]
        values = [first_ref[0:1, 0:1], second_ref[0:1, 0:1], alpha]
        values += [first_ref[1:2, 0:1], second_ref[1:2, 0:1], jnp.sqrt(m)]
        coef_ref[...] = row_of(plan, values)

    row = jax.ShapeDtypeStruct((8, plan.D), F32)
    return on_chip("outcome", body, [q, z, first, second, *sums], [q, row])


def middle(plan, keep, got):
    def body(keep_ref, got_ref, *outs):
        end = pl.ds(plan.half, PAD)
        scalars = split_row(joined_row(keep_ref[end, :]) + joined_row(got_ref[end, :]), plan.D)
        for z, out in enumerate(outs):
            at = pl.ds(z * plan.part, plan.part)
            added = keep_ref[at, :].astype(F32) + got_ref[at, :].astype(F32)
            out[pl.ds(0, plan.part), :] = added.astype(BF16)
            out[pl.ds(plan.part, PAD), :] = scalars

    shape = jax.ShapeDtypeStruct((plan.part + PAD, plan.D), BF16)
    return on_chip("middle", body, [keep, got], [shape] * plan.Z)


def exchanged(plan, messages):
    keep, send = messages
    parts = middle(plan, keep, swapped(send, 1))
    last = [swapped(parts[z], 2 * z) for z in range(plan.Z - 1, 0, -1)]
    return [parts[0]] + last[::-1]


def local(
    start_vector,
    left_environment,
    right_environment,
    block_energy,
    sector_rows,
    sector_cols,
    feed_block,
):
    T, W, D = left_environment.shape[1:4]
    plan = Plan(T, W, D, lax.axis_size("blk"))
    left = passed_along(left_environment, "seg", 1).reshape(T * W * D, D)
    right = right_environment.reshape(T * W * D, D)
    slots = plan.slots(feed_block.reshape(T * W), lax.axis_index("blk"))
    sizes = jnp.concatenate([sector_rows[0], sector_cols[0], slots])
    energy = block_energy[0]
    vector = jax.ShapeDtypeStruct((T * D, D), F32)
    row = jax.ShapeDtypeStruct((8, D), F32)
    start = start_vector.reshape(T * D, D)

    (x,), messages = operator_step(
        plan, "step_0", update_first, [start, sizes, energy], [vector], left, right
    )
    arrived = exchanged(plan, messages)
    (q0, h0, known), messages = operator_step(
        plan, "step_1", update_second, [x, sizes, energy] + arrived, [vector, vector, row], left, right
    )
    arrived = exchanged(plan, messages)
    (q1, h1, z1, first), messages = operator_step(
        plan,
        "step_2",
        update_third,
        [q0, h0, known, sizes, energy] + arrived,
        [vector, vector, vector, row],
        left,
        right,
    )
    arrived = exchanged(plan, messages)
    q2, z2, second, sums = last_step(
        plan, [q1, h1, z1, sizes, energy] + arrived, [vector, vector, row]
    )
    mask = 1
    while 2 * mask < plan.B:
        sums = sums + swapped(sums, mask)
        mask *= 2
    residual, coefficients = outcome(plan, q2, z2, first, second, sums, swapped(sums, mask))
    return (coefficients[:1, :6], residual.reshape(1, T, D, D))


def solution(mesh):
    return jax.shard_map(
        local,
        mesh=mesh,
        in_specs=(
            P("seg", "blk", None, None),
            P("seg", "blk", None, None, None),
            P("seg", "blk", None, None, None),
            P("seg", "blk"),
            P("seg", "blk"),
            P("seg", "blk"),
            P("seg", "blk", None),
        ),
        out_specs=(P("seg", None), P("seg", "blk", None, None)),
        check_vma=False,
    )
```

```python
import functools

import jax
import jax.numpy as jnp
from jax import lax
from jax.experimental import pallas as pl
from jax.experimental.pallas import tpu as pltpu
from jax.sharding import PartitionSpec as P

epsilon = 1e-06
F32 = jnp.float32
BF16 = jnp.bfloat16
PAD = 16
VMEM = pltpu.VMEM
SMEM = pltpu.SMEM


def passed_along(block, axis, distance):
    devices = range(lax.axis_size(axis))
    route = [(i - distance, i) for i in devices if i - distance in devices]
    return lax.ppermute(block, axis, route)


def swapped(block, mask):
    return lax.ppermute(block, "blk", [(i, i ^ mask) for i in range(lax.axis_size("blk"))])


class Plan:
    def __init__(self, tiles, channels, tile, blk):
        self.T, self.W, self.D, self.B = tiles, channels, tile, blk
        self.Z = blk // 2
        self.Ta = tiles // 2
        self.Tb = tiles - self.Ta
        self.entries = float(tiles * blk * tile * tile)
        self.n = tiles * blk
        self.a_rows = self.Ta * tile
        self.b_rows = self.Tb * tile

    def slot(self, feed, me):
        tiles = jnp.int32(self.T)
        device, tile = lax.div(feed, tiles), lax.rem(feed, tiles)
        relative = device ^ me
        zr, yr = relative >> 1, relative & 1
        a = (yr * self.Z + zr) * self.Ta + tile
        b = self.B * self.Ta + (zr * 2 + yr) * self.Tb + (tile - self.Ta)
        return jnp.where(feed >= self.n, self.n, jnp.where(tile < self.Ta, a, b))

    def messages(self):
        a = jax.ShapeDtypeStruct((self.Z * self.a_rows + PAD, self.D), BF16)
        b = jax.ShapeDtypeStruct((2 * self.b_rows, self.D), BF16)
        return [a, a] + [b] * self.Z


def packed_row(scalars, tile):
    lane = lax.broadcasted_iota(jnp.int32, (1, tile), 1)
    row = jnp.zeros((1, tile), F32)
    for index, value in enumerate(scalars):
        row = row + jnp.where(lane == index, value, 0.0)
    return split_row(row, tile)


def split_row(row, tile):
    high = row.astype(BF16).astype(F32)
    middle = (row - high).astype(BF16).astype(F32)
    low = row - high - middle
    at = lax.broadcasted_iota(jnp.int32, (PAD, tile), 0)
    rows = jnp.where(at == 0, high, jnp.where(at == 1, middle, jnp.where(at == 2, low, 0.0)))
    return rows.astype(BF16)


def joined_row(rows):
    rows = rows.astype(F32)
    return rows[0:1] + rows[1:2] + rows[2:3]


def folded(value):
    return jnp.sum(value.reshape(value.shape[0] // 8, 8, value.shape[1]), axis=0)


def total(value):
    return jnp.sum(value, keepdims=True).reshape(1, 1)


def live_mask(plan, rows, cols, k):
    down = lax.broadcasted_iota(jnp.int32, (plan.D, plan.D), 0)
    across = lax.broadcasted_iota(jnp.int32, (plan.D, plan.D), 1)
    return jnp.logical_and(down < rows[k], across < cols[k])


def received_sums(plan, arrived):
    a_parts, b_parts = arrived[: plan.Z], arrived[plan.Z :]

    def tile(k):
        parts, i = (a_parts, k) if k < plan.Ta else (b_parts, k - plan.Ta)
        at = pl.ds(i * plan.D, plan.D)
        return functools.reduce(lambda x, y: x + y, [p[at, :].astype(F32) for p in parts])

    level = [joined_row(p[pl.ds(plan.a_rows, PAD), :]) for p in a_parts]
    while len(level) > 1:
        level = [level[i] + level[i + 1] for i in range(0, len(level), 2)]
    return tile, level[0]


def lane(row, index):
    return row[:, index : index + 1]


def shift_of(plan, a, b, d, e):
    alpha = a / plan.entries
    m = jnp.maximum(b - 2.0 * alpha * d + alpha * alpha * e, 0.0) / plan.entries
    return alpha, m


def update_first(plan, ins, outs, send):
    (start, rows, cols), (x_out,) = ins, outs
    norm = jnp.zeros((8, plan.D), F32)
    for k in range(plan.T):
        at = pl.ds(k * plan.D, plan.D)
        x = jnp.where(live_mask(plan, rows, cols, k), start[at, :].astype(F32), 0.0)
        x_out[at, :] = x
        send(k, x)
        norm = norm + folded(x * x)
    return [total(norm)]


def update_second(plan, ins, outs, send):
    (x_in, rows, cols, energy), arrived = ins[:4], ins[4:]
    q_out, h_out, known_out = outs
    tile, row = received_sums(plan, arrived)
    square = lane(row, 0)
    scale = lax.rsqrt(square / plan.entries + epsilon)
    known_out[...] = jnp.broadcast_to(scale * scale * square, known_out.shape)
    a = b = jnp.zeros((8, plan.D), F32)
    for k in range(plan.T):
        at = pl.ds(k * plan.D, plan.D)
        x = x_in[at, :]
        image = jnp.where(live_mask(plan, rows, cols, k), tile(k), 0.0) + energy[k] * x
        q = scale * x
        h = scale * image
        q_out[at, :] = q
        h_out[at, :] = h
        send(k, h)
        a = a + folded(q * h)
        b = b + folded(h * h)
    return [total(a), total(b)]


def update_third(plan, ins, outs, send):
    (q_in, h_in, known, rows, cols, energy), arrived = ins[:6], ins[6:]
    q_out, h_out, z_out, coef_out = outs
    tile, row = received_sums(plan, arrived)
    a, b = lane(row, 0), lane(row, 1)
    alpha, m = shift_of(plan, a, b, a, known[0:1, 0:1])
    beta, scale = jnp.sqrt(m), lax.rsqrt(m + epsilon)
    coef_out[0:1, :] = jnp.broadcast_to(alpha, (1, plan.D))
    coef_out[1:2, :] = jnp.broadcast_to(beta, (1, plan.D))
    sums = [jnp.zeros((8, plan.D), F32)] * 4
    for k in range(plan.T):
        at = pl.ds(k * plan.D, plan.D)
        q0, h0 = q_in[at, :], h_in[at, :]
        image = jnp.where(live_mask(plan, rows, cols, k), tile(k), 0.0) + energy[k] * h0
        q = scale * (h0 - alpha * q0)
        h = scale * (image - alpha * h0)
        z = h - beta * q0
        q_out[at, :] = q
        h_out[at, :] = h
        z_out[at, :] = z
        send(k, z)
        sums = [s + folded(p) for s, p in zip(sums, (q * h, z * z, z * q, q * q))]
    return [total(s) for s in sums]


def update_last(plan, ins, outs, send):
    (q_in, h_in, z_in, rows, cols, energy), arrived = ins[:6], ins[6:]
    q_out, z_out, coef_out = outs
    tile, row = received_sums(plan, arrived)
    alpha, m = shift_of(plan, *[lane(row, i) for i in range(4)])
    beta, scale = jnp.sqrt(m), lax.rsqrt(m + epsilon)
    coef_out[0:1, :] = jnp.broadcast_to(alpha, (1, plan.D))
    coef_out[1:2, :] = jnp.broadcast_to(beta, (1, plan.D))
    sums = [jnp.zeros((8, plan.D), F32)] * 4
    for k in range(plan.T):
        at = pl.ds(k * plan.D, plan.D)
        q1, h1, z1 = q_in[at, :], h_in[at, :], z_in[at, :]
        image = jnp.where(live_mask(plan, rows, cols, k), tile(k), 0.0) + energy[k] * z1
        q = scale * (z1 - alpha * q1)
        h = scale * (image - alpha * h1)
        z = h - beta * q1
        q_out[at, :] = q
        z_out[at, :] = z
        sums = [s + folded(p) for s, p in zip(sums, (q * h, z * z, z * q, q * q))]
    return [total(s) for s in sums]


def on_chip(name, body, ins, outs, scratch=()):
    spaces = [SMEM if len(x.shape) == 1 else VMEM for x in ins]
    return pl.pallas_call(
        body,
        in_specs=[pl.BlockSpec(memory_space=s) for s in spaces],
        out_specs=[pl.BlockSpec(memory_space=VMEM)] * len(outs),
        out_shape=list(outs),
        scratch_shapes=list(scratch),
        compiler_params=pltpu.CompilerParams(vmem_limit_bytes=16 * 2**20),
        name=name,
    )(*ins)


def operator_step(plan, name, update, ins, state_shapes, left, right, slots):
    D, T, W = plan.D, plan.T, plan.W
    pairs = T // 2
    n_in, n_state = len(ins), len(state_shapes)
    group = next(c for c in range(max(1, W // 2), 0, -1) if W % c == 0)

    def body(*refs):
        in_refs = refs[:n_in]
        left_ref, right_ref, slot_ref = refs[n_in : n_in + 3]
        state_refs = refs[n_in + 3 : n_in + 3 + n_state]
        message_refs = refs[n_in + 3 + n_state : -3]
        low_ref, half_ref, sum_ref = refs[-3:]

        def send(k, value):
            low_ref[pl.ds(k * D, D), :] = value.astype(BF16)

        row = update(plan, in_refs, state_refs, send)
        if isinstance(row, list):
            row = packed_row(row, D)
        for ref in message_refs[:2]:
            ref[pl.ds(plan.Z * plan.a_rows, PAD), :] = row
        sum_ref[...] = jnp.zeros(sum_ref.shape, F32)
        none = jnp.zeros((D, D), BF16)

        def several(step, carry):
            for h in range(pairs):
                blocks = (h, h + pairs)
                v = [low_ref[pl.ds(k * D, D), :] for k in blocks]
                both = jnp.concatenate(
                    [jnp.concatenate([v[0], none], 1), jnp.concatenate([none, v[1]], 1)], 0
                )
                firsts = [k * W + step * group for k in blocks]
                tiles = [
                    left_ref[pl.ds(pl.multiple_of(f * D, D), group * D), :] for f in firsts
                ]
                half_ref[...] = jnp.dot(
                    jnp.concatenate(tiles, 1), both, preferred_element_type=F32
                ).astype(BF16)
                for w in range(group):
                    for side, f in enumerate(firsts):
                        product = jnp.dot(
                            half_ref[pl.ds(w * D, D), pl.ds(side * D, D)],
                            right_ref[pl.ds(pl.multiple_of((f + w) * D, D), D), :],
                            preferred_element_type=F32,
                        )
                        slot = slot_ref[f + w]
                        at = pl.ds(pl.multiple_of(slot * D, D), D)
                        sum_ref[at, :] += product
            return carry

        lax.fori_loop(0, W // group, several, 0)
        first = 0
        for ref in message_refs:
            rows = ref.shape[0] // D * D
            ref[pl.ds(0, rows), :] = sum_ref[pl.ds(first, rows), :].astype(BF16)
            first += rows

    results = on_chip(
        name,
        body,
        list(ins) + [left, right, slots],
        list(state_shapes) + plan.messages(),
        [
            VMEM((T * D, D), BF16),
            VMEM((group * D, 2 * D), BF16),
            VMEM(((plan.n + 1) * D, D), F32),
        ],
    )
    return results[:n_state], results[n_state:]


def row_of(plan, values):
    across = lax.broadcasted_iota(jnp.int32, (8, plan.D), 1)
    row = jnp.zeros((8, plan.D), F32)
    for index, value in enumerate(values):
        row = row + jnp.where(across == index, value, 0.0)
    return row


def last_step(plan, ins, state_shapes):
    n_in = len(ins)

    def body(*refs):
        sums = update_last(plan, refs[:n_in], refs[n_in:-1], None)
        refs[-1][...] = row_of(plan, sums)

    row = jax.ShapeDtypeStruct((8, plan.D), F32)
    return on_chip("last_step", body, ins, list(state_shapes) + [row])


def outcome(plan, q, z, first, second, *sums):
    def body(q_ref, z_ref, first_ref, second_ref, *refs):
        added = functools.reduce(lambda x, y: x + y, [r[0:1, :] for r in refs[:-2]])
        residual_ref, coef_ref = refs[-2:]
        alpha, m = shift_of(plan, *[lane(added, i) for i in range(4)])
        residual_ref[...] = z_ref[...] - alpha * q_ref[...]
        values = [first_ref[0:1, 0:1], second_ref[0:1, 0:1], alpha]
        values += [first_ref[1:2, 0:1], second_ref[1:2, 0:1], jnp.sqrt(m)]
        coef_ref[...] = row_of(plan, values)

    row = jax.ShapeDtypeStruct((8, plan.D), F32)
    return on_chip("outcome", body, [q, z, first, second, *sums], [q, row])


def middle_a(plan, keep, got):
    rows = plan.a_rows

    def body(keep_ref, got_ref, *outs):
        end = pl.ds(plan.Z * rows, PAD)
        scalars = split_row(joined_row(keep_ref[end, :]) + joined_row(got_ref[end, :]), plan.D)
        for z, out in enumerate(outs):
            at = pl.ds(z * rows, rows)
            added = keep_ref[at, :].astype(F32) + got_ref[at, :].astype(F32)
            out[pl.ds(0, rows), :] = added.astype(BF16)
            out[pl.ds(rows, PAD), :] = scalars

    shape = jax.ShapeDtypeStruct((rows + PAD, plan.D), BF16)
    return on_chip("middle_a", body, [keep, got], [shape] * plan.Z)


def middle_b(plan, parts):
    rows = plan.b_rows

    def body(*refs):
        for y, out in enumerate(refs[plan.Z :]):
            at = pl.ds(y * rows, rows)
            tiles = [p[at, :].astype(F32) for p in refs[: plan.Z]]
            out[...] = functools.reduce(lambda u, v: u + v, tiles).astype(out.dtype)

    shapes = [jax.ShapeDtypeStruct((rows, plan.D), d) for d in (F32, BF16)]
    return on_chip("middle_b", body, parts, shapes)


def exchanged(plan, messages):
    keep, send, b_parts = messages[0], messages[1], messages[2:]
    others = range(plan.Z - 1, 0, -1)
    got = swapped(send, 1)
    b_got = [swapped(b_parts[z], 2 * z) for z in others]
    a_parts = middle_a(plan, keep, got)
    a_last = [swapped(a_parts[z], 2 * z) for z in others]
    b_keep, b_send = middle_b(plan, [b_parts[0]] + b_got)
    return [a_parts[0]] + a_last[::-1] + [b_keep, swapped(b_send, 1)]


def prepared(plan, start, rows, cols, feeds, right):
    def body(start_ref, rows_ref, cols_ref, feed_ref, right_ref, *outs):
        x_ref, low_ref, row_ref, slot_ref, held_ref, done = outs
        copy = pltpu.make_async_copy(right_ref, held_ref, done)
        copy.start()
        me = lax.axis_index("blk")

        def several(w, carry):
            for k in range(plan.T):
                slot_ref[k * plan.W + w] = plan.slot(feed_ref[k, w], me)
            return carry

        lax.fori_loop(0, plan.W, several, 0)

        def send(k, value):
            low_ref[pl.ds(k * plan.D, plan.D), :] = value.astype(BF16)

        sums = update_first(plan, (start_ref, rows_ref, cols_ref), (x_ref,), send)
        row_ref[...] = packed_row(sums, plan.D)
        copy.wait()

    chip = pl.BlockSpec(memory_space=VMEM)
    scalar = pl.BlockSpec(memory_space=SMEM)
    return pl.pallas_call(
        body,
        in_specs=[chip, scalar, scalar, scalar, pl.BlockSpec(memory_space=pltpu.HBM)],
        out_specs=[chip, chip, chip, scalar, chip],
        out_shape=[
            jax.ShapeDtypeStruct(start.shape, F32),
            jax.ShapeDtypeStruct(start.shape, BF16),
            jax.ShapeDtypeStruct((PAD, plan.D), BF16),
            jax.ShapeDtypeStruct((plan.T * plan.W,), jnp.int32),
            right,
        ],
        scratch_shapes=[pltpu.SemaphoreType.DMA(())],
        compiler_params=pltpu.CompilerParams(vmem_limit_bytes=16 * 2**20),
        name="prepared",
    )(start, rows, cols, feeds, right)


def update_none(plan, ins, outs, send):
    low, row = ins
    for k in range(plan.T):
        send(k, low[pl.ds(k * plan.D, plan.D), :])
    return row[...]


def local(
    start_vector,
    left_environment,
    right_environment,
    block_energy,
    sector_rows,
    sector_cols,
    feed_block,
):
    T, W, D = left_environment.shape[1:4]
    plan = Plan(T, W, D, lax.axis_size("blk"))
    left = passed_along(left_environment, "seg", 1).reshape(T * W * D, D)
    right = right_environment.reshape(T * W * D, D)
    rows, cols, energy = sector_rows[0], sector_cols[0], block_energy[0]
    vector = jax.ShapeDtypeStruct((T * D, D), F32)
    row = jax.ShapeDtypeStruct((8, D), F32)
    start = start_vector.reshape(T * D, D)

    x, low, square, slots, right = prepared(plan, start, rows, cols, feed_block[0], right)
    _, messages = operator_step(
        plan, "step_0", update_none, [low, square], [], left, right, slots
    )
    arrived = exchanged(plan, messages)
    (q0, h0, known), messages = operator_step(
        plan,
        "step_1",
        update_second,
        [x, rows, cols, energy] + arrived,
        [vector, vector, row],
        left,
        right,
        slots,
    )
    arrived = exchanged(plan, messages)
    (q1, h1, z1, first), messages = operator_step(
        plan,
        "step_2",
        update_third,
        [q0, h0, known, rows, cols, energy] + arrived,
        [vector, vector, vector, row],
        left,
        right,
        slots,
    )
    arrived = exchanged(plan, messages)
    q2, z2, second, sums = last_step(
        plan, [q1, h1, z1, rows, cols, energy] + arrived, [vector, vector, row]
    )
    mask = 1
    while 2 * mask < plan.B:
        sums = sums + swapped(sums, mask)
        mask *= 2
    residual, coefficients = outcome(plan, q2, z2, first, second, sums, swapped(sums, mask))
    return (coefficients[:1, :6], residual.reshape(1, T, D, D))


def solution(mesh):
    return jax.shard_map(
        local,
        mesh=mesh,
        in_specs=(
            P("seg", "blk", None, None),
            P("seg", "blk", None, None, None),
            P("seg", "blk", None, None, None),
            P("seg", "blk"),
            P("seg", "blk"),
            P("seg", "blk"),
            P("seg", "blk", None),
        ),
        out_specs=(P("seg", None), P("seg", "blk", None, None)),
        check_vma=False,
    )
```

```python
import functools

import jax
import jax.numpy as jnp
from jax import lax
from jax.experimental import pallas as pl
from jax.experimental.pallas import tpu as pltpu
from jax.sharding import PartitionSpec as P


epsilon = 1e-06
F32 = jnp.float32
BF16 = jnp.bfloat16
PAD = 16
VMEM = pltpu.VMEM
SMEM = pltpu.SMEM


def handed(block, targets, distance):
    return lax.ppermute(block, "seg", [(s - distance, s) for s in targets])


def swapped(block, mask, segments):
    blk = lax.axis_size("blk")
    route = [(s * blk + i, s * blk + (i ^ mask)) for s in segments for i in range(blk)]
    return lax.ppermute(block, ("seg", "blk"), route)


class Plan:
    def __init__(self, tiles, channels, tile, blk):
        self.T, self.W, self.D, self.B = tiles, channels, tile, blk
        self.Z = blk // 2
        self.Ta = tiles // 2
        self.Tb = tiles - self.Ta
        self.entries = float(tiles * blk * tile * tile)
        self.n = tiles * blk
        self.a_rows = self.Ta * tile
        self.b_rows = self.Tb * tile
        self.H = tiles // 2
        self.group = next(
            c for c in range(max(1, channels // 2), 0, -1) if channels % c == 0
        )

    def slot(self, feed, me):
        tiles = jnp.int32(self.T)
        device, tile = lax.div(feed, tiles), lax.rem(feed, tiles)
        relative = device ^ me
        zr, yr = relative >> 1, relative & 1
        a = (yr * self.Z + zr) * self.Ta + tile
        b = self.B * self.Ta + (zr * 2 + yr) * self.Tb + (tile - self.Ta)
        return jnp.where(feed >= self.n, self.n, jnp.where(tile < self.Ta, a, b))

    def messages(self):
        a = jax.ShapeDtypeStruct((self.Z * self.a_rows + PAD, self.D), BF16)
        b = jax.ShapeDtypeStruct((2 * self.b_rows, self.D), BF16)
        return [a, a] + [b] * self.Z


def packed_row(scalars, tile):
    lane = lax.broadcasted_iota(jnp.int32, (1, tile), 1)
    row = jnp.zeros((1, tile), F32)
    for index, value in enumerate(scalars):
        row = row + jnp.where(lane == index, value, 0.0)
    return split_row(row, tile)


def split_row(row, tile):
    high = row.astype(BF16).astype(F32)
    middle = (row - high).astype(BF16).astype(F32)
    low = row - high - middle
    at = lax.broadcasted_iota(jnp.int32, (PAD, tile), 0)
    rows = jnp.where(at == 0, high, jnp.where(at == 1, middle, jnp.where(at == 2, low, 0.0)))
    return rows.astype(BF16)


def joined_row(rows):
    rows = rows.astype(F32)
    return rows[0:1] + rows[1:2] + rows[2:3]


def folded(value):
    return jnp.sum(value.reshape(value.shape[0] // 8, 8, value.shape[1]), axis=0)


def total(value):
    return jnp.sum(value, keepdims=True).reshape(1, 1)


def live_mask(plan, rows, cols, k):
    down = lax.broadcasted_iota(jnp.int32, (plan.D, plan.D), 0)
    across = lax.broadcasted_iota(jnp.int32, (plan.D, plan.D), 1)
    return jnp.logical_and(down < rows[k], across < cols[k])


def received_sums(plan, arrived):
    a_parts, b_parts = arrived[: plan.Z], arrived[plan.Z :]

    def tile(k):
        parts, i = (a_parts, k) if k < plan.Ta else (b_parts, k - plan.Ta)
        at = pl.ds(i * plan.D, plan.D)
        return functools.reduce(lambda x, y: x + y, [p[at, :].astype(F32) for p in parts])

    level = [joined_row(p[pl.ds(plan.a_rows, PAD), :]) for p in a_parts]
    while len(level) > 1:
        level = [level[i] + level[i + 1] for i in range(0, len(level), 2)]
    return tile, level[0]


def lane(row, index):
    return row[:, index : index + 1]


def shift_of(plan, a, b, d, e):
    alpha = a / plan.entries
    m = jnp.maximum(b - 2.0 * alpha * d + alpha * alpha * e, 0.0) / plan.entries
    return alpha, m


def update_first(plan, ins, outs, send):
    (start, rows, cols), (x_out,) = ins, outs
    norm = jnp.zeros((8, plan.D), F32)
    for k in range(plan.T):
        at = pl.ds(k * plan.D, plan.D)
        x = jnp.where(live_mask(plan, rows, cols, k), start[at, :].astype(F32), 0.0)
        x_out[at, :] = x
        send(k, x)
        norm = norm + folded(x * x)
    return [total(norm)]


def update_second(plan, ins, outs, send):
    (x_in, rows, cols, energy, own, own_row, helped), arrived = ins[:7], ins[7:]
    q_out, h_out, known_out = outs
    odd = in_odd_segment()
    half_tile, half_row = received_sums(plan, arrived)
    row = jnp.where(odd, own_row[0:1, :], half_row)

    def tile(k):
        at = pl.ds(k * plan.D, plan.D)
        return jnp.where(odd, own[at, :], half_tile(k) + helped[at, :].astype(F32))

    square = lane(row, 0)
    scale = lax.rsqrt(square / plan.entries + epsilon)
    known_out[...] = jnp.broadcast_to(scale * scale * square, known_out.shape)
    a = b = jnp.zeros((8, plan.D), F32)
    for k in range(plan.T):
        at = pl.ds(k * plan.D, plan.D)
        x = x_in[at, :]
        image = jnp.where(live_mask(plan, rows, cols, k), tile(k), 0.0) + energy[k] * x
        q = scale * x
        h = scale * image
        q_out[at, :] = q
        h_out[at, :] = h
        send(k, h)
        a = a + folded(q * h)
        b = b + folded(h * h)
    return [total(a), total(b)]


def update_third(plan, ins, outs, send):
    (q_in, h_in, known, rows, cols, energy), arrived = ins[:6], ins[6:]
    q_out, h_out, z_out, coef_out = outs
    tile, row = received_sums(plan, arrived)
    a, b = lane(row, 0), lane(row, 1)
    alpha, m = shift_of(plan, a, b, a, known[0:1, 0:1])
    beta, scale = jnp.sqrt(m), lax.rsqrt(m + epsilon)
    coef_out[0:1, :] = jnp.broadcast_to(alpha, (1, plan.D))
    coef_out[1:2, :] = jnp.broadcast_to(beta, (1, plan.D))
    sums = [jnp.zeros((8, plan.D), F32)] * 4
    for k in range(plan.T):
        at = pl.ds(k * plan.D, plan.D)
        q0, h0 = q_in[at, :], h_in[at, :]
        image = jnp.where(live_mask(plan, rows, cols, k), tile(k), 0.0) + energy[k] * h0
        q = scale * (h0 - alpha * q0)
        h = scale * (image - alpha * h0)
        z = h - beta * q0
        q_out[at, :] = q
        h_out[at, :] = h
        z_out[at, :] = z
        send(k, z)
        sums = [s + folded(p) for s, p in zip(sums, (q * h, z * z, z * q, q * q))]
    return [total(s) for s in sums]


def update_last(plan, ins, outs):
    (q_in, h_in, z_in, rows, cols, energy), arrived = ins[:6], ins[6:]
    q_out, z_out, coef_out = outs
    tile, row = received_sums(plan, arrived)
    alpha, m = shift_of(plan, *[lane(row, i) for i in range(4)])
    beta, scale = jnp.sqrt(m), lax.rsqrt(m + epsilon)
    coef_out[0:1, :] = jnp.broadcast_to(alpha, (1, plan.D))
    coef_out[1:2, :] = jnp.broadcast_to(beta, (1, plan.D))
    sums = [jnp.zeros((8, plan.D), F32)] * 4
    for k in range(plan.T):
        at = pl.ds(k * plan.D, plan.D)
        q1, h1, z1 = q_in[at, :], h_in[at, :], z_in[at, :]
        image = jnp.where(live_mask(plan, rows, cols, k), tile(k), 0.0) + energy[k] * z1
        q = scale * (z1 - alpha * q1)
        h = scale * (image - alpha * h1)
        z = h - beta * q1
        q_out[at, :] = q
        z_out[at, :] = z
        sums = [s + folded(p) for s, p in zip(sums, (q * h, z * z, z * q, q * q))]
    return [total(s) for s in sums]


def on_chip(body, ins, outs, scratch=()):
    spaces = [SMEM if len(x.shape) == 1 else VMEM for x in ins]
    return pl.pallas_call(
        body,
        in_specs=[pl.BlockSpec(memory_space=s) for s in spaces],
        out_specs=[pl.BlockSpec(memory_space=VMEM)] * len(outs),
        out_shape=list(outs),
        scratch_shapes=list(scratch),
        compiler_params=pltpu.CompilerParams(vmem_limit_bytes=16 * 2**20),
    )(*ins)


def in_odd_segment():
    return lax.axis_index("seg") % 2 == 1


class Block:
    def __init__(self, left, right, low, slots):
        self.left, self.right, self.low, self.slots = left, right, low, slots


def multiply(plan, pairs, half_ref, sum_ref):
    D, W, group = plan.D, plan.W, plan.group
    none = jnp.zeros((D, D), BF16)

    def rows(place, first, count):
        ref, block = place
        return ref[pl.ds(pl.multiple_of((block * W + first) * D, D), count * D), :]

    def several(step, carry):
        first = step * group
        for pair in pairs:
            v = [b.low[0][pl.ds(b.low[1] * D, D), :] for b in pair]
            both = jnp.concatenate(
                [jnp.concatenate([v[0], none], 1), jnp.concatenate([none, v[1]], 1)], 0
            )
            tiles = [rows(b.left, first, group) for b in pair]
            half_ref[...] = jnp.dot(
                jnp.concatenate(tiles, 1), both, preferred_element_type=F32
            ).astype(BF16)
            for w in range(group):
                for side, b in enumerate(pair):
                    product = jnp.dot(
                        half_ref[pl.ds(w * D, D), pl.ds(side * D, D)],
                        rows(b.right, first + w, 1),
                        preferred_element_type=F32,
                    )
                    ref, block = b.slots
                    slot = ref[block * W + first + w]
                    sum_ref[pl.ds(pl.multiple_of(slot * D, D), D), :] += product
        return carry

    lax.fori_loop(0, W // group, several, 0)


def flush(plan, row, sum_ref, message_refs):
    first = 0
    for ref in message_refs:
        rows = ref.shape[0] // plan.D * plan.D
        ref[pl.ds(0, rows), :] = sum_ref[pl.ds(first, rows), :].astype(BF16)
        first += rows
    for ref in message_refs[:2]:
        ref[pl.ds(plan.Z * plan.a_rows, PAD), :] = row


def work_space(plan):
    return [
        VMEM((plan.group * plan.D, 2 * plan.D), BF16),
        VMEM(((plan.n + 1) * plan.D, plan.D), F32),
    ]


def first_own(plan, low, row, slots, left, right):
    def body(low_ref, row_ref, slot_ref, left_ref, right_ref, *refs):
        message_refs, (half_ref, sum_ref) = refs[:-2], refs[-2:]

        @pl.when(in_odd_segment())
        def _():
            def at(k):
                return Block((left_ref, k), (right_ref, k), (low_ref, k), (slot_ref, k))

            sum_ref[...] = jnp.zeros(sum_ref.shape, F32)
            pairs = [(at(k), at(k + plan.H)) for k in range(plan.H)]
            multiply(plan, pairs, half_ref, sum_ref)
            flush(plan, row_ref[...], sum_ref, message_refs)

    ins = [low, row, slots, left, right]
    return on_chip(body, ins, plan.messages(), work_space(plan))


def first_half(plan, low, row, slots, left, right, other_low, other_slots, held, other_right):
    def body(*refs):
        low_ref, row_ref, slot_ref, left_ref, right_ref = refs[:5]
        other_low_ref, other_slot_ref, held_ref, other_right_ref = refs[5:9]
        message_refs, (half_ref, sum_ref) = refs[9:-2], refs[-2:]
        odd = in_odd_segment()

        def all_of(places):
            def at(k):
                return Block(*[(p, k) for p in places])

            sum_ref[...] = jnp.zeros(sum_ref.shape, F32)
            pairs = [(at(k), at(k + plan.H // 2)) for k in range(plan.H // 2)]
            multiply(plan, pairs, half_ref, sum_ref)
            flush(plan, row_ref[...], sum_ref, message_refs)

        @pl.when(odd)
        def _():
            all_of((held_ref, other_right_ref, other_low_ref, other_slot_ref))

        @pl.when(jnp.logical_not(odd))
        def _():
            all_of((left_ref, right_ref, low_ref, slot_ref))

    ins = [low, row, slots, left, right, other_low, other_slots, held, other_right]
    return on_chip(body, ins, plan.messages(), work_space(plan))


def operator_step(plan, update, ins, state_shapes, lefts, right, slots):
    n_in, n_state = len(ins), len(state_shapes)

    def body(*refs):
        own_ref, first_ref, last_ref, right_ref, slot_ref = refs[n_in : n_in + 5]
        state_refs = refs[n_in + 5 : n_in + 5 + n_state]
        message_refs = refs[n_in + 5 + n_state : -3]
        low_ref, half_ref, sum_ref = refs[-3:]
        odd = in_odd_segment()

        def send(k, value):
            low_ref[pl.ds(k * plan.D, plan.D), :] = value.astype(BF16)

        row = packed_row(update(plan, refs[:n_in], state_refs, send), plan.D)
        sum_ref[...] = jnp.zeros(sum_ref.shape, F32)

        def all_of(place):
            def at(k):
                return Block(place(k), (right_ref, k), (low_ref, k), (slot_ref, k))

            pairs = [(at(k), at(k + plan.H)) for k in range(plan.H)]
            multiply(plan, pairs, half_ref, sum_ref)

        @pl.when(odd)
        def _():
            all_of(lambda k: (own_ref, k))

        @pl.when(jnp.logical_not(odd))
        def _():
            all_of(lambda k: (first_ref, k) if k < plan.H else (last_ref, k - plan.H))

        flush(plan, row, sum_ref, message_refs)

    results = on_chip(
        body,
        list(ins) + list(lefts) + [right, slots],
        list(state_shapes) + plan.messages(),
        [VMEM((plan.T * plan.D, plan.D), BF16)] + work_space(plan),
    )
    return results[:n_state], results[n_state:]


def row_of(plan, values):
    across = lax.broadcasted_iota(jnp.int32, (8, plan.D), 1)
    row = jnp.zeros((8, plan.D), F32)
    for index, value in enumerate(values):
        row = row + jnp.where(across == index, value, 0.0)
    return row


def last_step(plan, ins, state_shapes):
    n_in = len(ins)

    def body(*refs):
        sums = update_last(plan, refs[:n_in], refs[n_in:-1])
        refs[-1][...] = row_of(plan, sums)

    row = jax.ShapeDtypeStruct((8, plan.D), F32)
    return on_chip(body, ins, list(state_shapes) + [row])


def outcome(plan, q, z, first, second, *sums):
    def body(q_ref, z_ref, first_ref, second_ref, *refs):
        added = functools.reduce(lambda x, y: x + y, [r[0:1, :] for r in refs[:-2]])
        residual_ref, coef_ref = refs[-2:]
        alpha, m = shift_of(plan, *[lane(added, i) for i in range(4)])
        residual_ref[...] = z_ref[...] - alpha * q_ref[...]
        values = [first_ref[0:1, 0:1], second_ref[0:1, 0:1], alpha]
        values += [first_ref[1:2, 0:1], second_ref[1:2, 0:1], jnp.sqrt(m)]
        coef_ref[...] = row_of(plan, values)

    row = jax.ShapeDtypeStruct((8, plan.D), F32)
    return on_chip(body, [q, z, first, second, *sums], [q, row])


def middle_a(plan, keep, got):
    rows = plan.a_rows

    def body(keep_ref, got_ref, *outs):
        end = pl.ds(plan.Z * rows, PAD)
        scalars = split_row(joined_row(keep_ref[end, :]) + joined_row(got_ref[end, :]), plan.D)
        for z, out in enumerate(outs):
            at = pl.ds(z * rows, rows)
            added = keep_ref[at, :].astype(F32) + got_ref[at, :].astype(F32)
            out[pl.ds(0, rows), :] = added.astype(BF16)
            out[pl.ds(rows, PAD), :] = scalars

    shape = jax.ShapeDtypeStruct((rows + PAD, plan.D), BF16)
    return on_chip(body, [keep, got], [shape] * plan.Z)


def middle_b(plan, parts):
    rows = plan.b_rows

    def body(*refs):
        for y, out in enumerate(refs[plan.Z :]):
            at = pl.ds(y * rows, rows)
            tiles = [p[at, :].astype(F32) for p in refs[: plan.Z]]
            out[...] = functools.reduce(lambda u, v: u + v, tiles).astype(out.dtype)

    shapes = [jax.ShapeDtypeStruct((rows, plan.D), d) for d in (F32, BF16)]
    return on_chip(body, parts, shapes)


def exchanged(plan, messages, segments):
    keep, send, b_parts = messages[0], messages[1], messages[2:]
    others = range(plan.Z - 1, 0, -1)
    got = swapped(send, 1, segments)
    b_got = [swapped(b_parts[z], 2 * z, segments) for z in others]
    a_parts = middle_a(plan, keep, got)
    a_last = [swapped(a_parts[z], 2 * z, segments) for z in others]
    b_keep, b_send = middle_b(plan, [b_parts[0]] + b_got)
    return [a_parts[0]] + a_last[::-1] + [b_keep, swapped(b_send, 1, segments)]


def gathered(plan, arrived, dtype):
    def body(*refs):
        tile, row = received_sums(plan, refs[:-2])
        for k in range(plan.T):
            refs[-2][pl.ds(k * plan.D, plan.D), :] = tile(k).astype(dtype)
        refs[-1][...] = jnp.broadcast_to(row, refs[-1].shape)

    sums = jax.ShapeDtypeStruct((plan.T * plan.D, plan.D), dtype)
    row = jax.ShapeDtypeStruct((8, plan.D), F32)
    return on_chip(body, arrived, [sums, row])


def copying(sources, slices):
    def body(*refs):
        n = len(sources)
        copies = []
        for i, (source, first, rows) in enumerate(slices):
            done = refs[n + len(slices)].at[i]
            from_ref = refs[source].at[pl.ds(first, rows)]
            copies.append(pltpu.make_async_copy(from_ref, refs[n + i], done))
        for copy in copies:
            copy.start()
        for copy in copies:
            copy.wait()

    return pl.pallas_call(
        body,
        in_specs=[pl.BlockSpec(memory_space=pl.ANY)] * len(sources),
        out_specs=[pl.BlockSpec(memory_space=VMEM)] * len(slices),
        out_shape=[
            jax.ShapeDtypeStruct((rows, sources[i].shape[1]), sources[i].dtype)
            for i, _, rows in slices
        ],
        scratch_shapes=[pltpu.SemaphoreType.DMA((len(slices),))],
        compiler_params=pltpu.CompilerParams(vmem_limit_bytes=16 * 2**20),
    )(*[pltpu.with_memory_space_constraint(x, pltpu.HBM) for x in sources])


def prepared(plan, start, rows, cols, feeds):
    def body(start_ref, rows_ref, cols_ref, feed_ref, *outs):
        x_ref, low_ref, row_ref, slot_ref, last_low_ref, last_slot_ref = outs
        me = lax.axis_index("blk")

        def several(w, carry):
            for k in range(plan.T):
                slot = plan.slot(feed_ref[k, w], me)
                slot_ref[k * plan.W + w] = slot
                if k >= plan.H:
                    last_slot_ref[(k - plan.H) * plan.W + w] = slot
            return carry

        lax.fori_loop(0, plan.W, several, 0)

        def send(k, value):
            low_ref[pl.ds(k * plan.D, plan.D), :] = value.astype(BF16)
            if k >= plan.H:
                last_low_ref[pl.ds((k - plan.H) * plan.D, plan.D), :] = value.astype(BF16)

        sums = update_first(plan, (start_ref, rows_ref, cols_ref), (x_ref,), send)
        row_ref[...] = packed_row(sums, plan.D)

    chip = pl.BlockSpec(memory_space=VMEM)
    scalar = pl.BlockSpec(memory_space=SMEM)
    last = plan.T - plan.H
    return pl.pallas_call(
        body,
        in_specs=[chip, scalar, scalar, scalar],
        out_specs=[chip, chip, chip, scalar, chip, scalar],
        out_shape=[
            jax.ShapeDtypeStruct(start.shape, F32),
            jax.ShapeDtypeStruct(start.shape, BF16),
            jax.ShapeDtypeStruct((PAD, plan.D), BF16),
            jax.ShapeDtypeStruct((plan.T * plan.W,), jnp.int32),
            jax.ShapeDtypeStruct((last * plan.D, plan.D), BF16),
            jax.ShapeDtypeStruct((last * plan.W,), jnp.int32),
        ],
        compiler_params=pltpu.CompilerParams(vmem_limit_bytes=16 * 2**20),
        name="prepared",
    )(start, rows, cols, feeds)


def local(
    start_vector,
    left_environment,
    right_environment,
    block_energy,
    sector_rows,
    sector_cols,
    feed_block,
):
    T, W, D = left_environment.shape[1:4]
    plan = Plan(T, W, D, lax.axis_size("blk"))
    segments = range(lax.axis_size("seg"))
    evens = [s for s in segments if s % 2 == 0]
    odds = [s for s in segments if s % 2 == 1]
    helped = [s for s in evens if s > 0]
    helpers = [s - 1 for s in helped]

    left = left_environment.reshape(T * W * D, D)
    right = right_environment.reshape(T * W * D, D)
    rows, cols, energy = sector_rows[0], sector_cols[0], block_energy[0]
    vector = jax.ShapeDtypeStruct((T * D, D), F32)
    row = jax.ShapeDtypeStruct((8, D), F32)
    start = start_vector.reshape(T * D, D)

    first_rows = plan.H * W * D
    last_rows = T * W * D - first_rows
    sent_left, sent_right = copying([left, right], [(0, 0, first_rows), (1, first_rows, last_rows)])
    left_first = handed(sent_left, helped, 1)
    right_last = handed(sent_right, helpers, -1)
    left_own = handed(left_environment, odds, 1).reshape(T * W * D, D)
    held_left, held_right = copying([left, right], [(0, first_rows, last_rows), (1, 0, T * W * D)])
    left_last = handed(held_left, helped, 1)
    x, low, square, slots, last_low, last_slots = prepared(
        plan, start, rows, cols, feed_block[0]
    )
    other_low = handed(last_low, helpers, -1)
    other_slots = handed(last_slots, helpers, -1)

    messages = first_own(plan, low, square, slots, left_own, held_right)
    arrived = exchanged(plan, messages, odds)
    own, own_row = gathered(plan, arrived, F32)
    messages = first_half(
        plan,
        low,
        square,
        slots,
        left_first,
        held_right,
        other_low,
        other_slots,
        held_left,
        right_last,
    )
    half = exchanged(plan, messages, evens + helpers)
    help_sum, _ = gathered(plan, half, BF16)
    help_sum = handed(help_sum, helped, 1)
    lefts = [left_own, left_first, left_last]
    (q0, h0, known), messages = operator_step(
        plan,
        update_second,
        [x, rows, cols, energy, own, own_row, help_sum] + half,
        [vector, vector, row],
        lefts,
        held_right,
        slots,
    )
    arrived = exchanged(plan, messages, segments)
    (q1, h1, z1, first), messages = operator_step(
        plan,
        update_third,
        [q0, h0, known, rows, cols, energy] + arrived,
        [vector, vector, vector, row],
        lefts,
        held_right,
        slots,
    )
    arrived = exchanged(plan, messages, segments)
    q2, z2, second, sums = last_step(
        plan, [q1, h1, z1, rows, cols, energy] + arrived, [vector, vector, row]
    )
    mask = 1
    while 2 * mask < plan.B:
        sums = sums + swapped(sums, mask, segments)
        mask *= 2
    last = swapped(sums, mask, segments)
    residual, coefficients = outcome(plan, q2, z2, first, second, sums, last)
    return (coefficients[:1, :6], residual.reshape(1, T, D, D))


def solution(mesh):
    return jax.shard_map(
        local,
        mesh=mesh,
        in_specs=(
            P("seg", "blk", None, None),
            P("seg", "blk", None, None, None),
            P("seg", "blk", None, None, None),
            P("seg", "blk"),
            P("seg", "blk"),
            P("seg", "blk"),
            P("seg", "blk", None),
        ),
        out_specs=(P("seg", None), P("seg", "blk", None, None)),
        check_vma=False,
    )
```

```python
import functools

import jax
import jax.numpy as jnp
from jax import lax
from jax.experimental import pallas as pl
from jax.experimental.pallas import tpu as pltpu
from jax.sharding import PartitionSpec as P


epsilon = 1e-06
F32 = jnp.float32
BF16 = jnp.bfloat16
PAD = 16
VMEM = pltpu.VMEM
SMEM = pltpu.SMEM


def handed(block, targets, distance):
    return lax.ppermute(block, "seg", [(s - distance, s) for s in targets])


def swapped(block, mask, axis="blk"):
    return lax.ppermute(block, axis, [(i, i ^ mask) for i in range(lax.axis_size(axis))])


class Plan:
    def __init__(self, tiles, channels, tile, blk):
        self.T, self.W, self.D, self.B = tiles, channels, tile, blk
        self.Z = blk // 2
        self.Ta = tiles // 2
        self.Tb = tiles - self.Ta
        self.entries = float(tiles * blk * tile * tile)
        self.n = tiles * blk
        self.a_rows = self.Ta * tile
        self.b_rows = self.Tb * tile
        self.H = tiles // 2
        self.group = next(
            c for c in range(max(1, channels // 2), 0, -1) if channels % c == 0
        )

    def slot(self, feed, me):
        tiles = jnp.int32(self.T)
        device, tile = lax.div(feed, tiles), lax.rem(feed, tiles)
        relative = device ^ me
        zr, yr = relative >> 1, relative & 1
        a = (yr * self.Z + zr) * self.Ta + tile
        b = self.B * self.Ta + (zr * 2 + yr) * self.Tb + (tile - self.Ta)
        return jnp.where(feed >= self.n, self.n, jnp.where(tile < self.Ta, a, b))

    def messages(self):
        a = jax.ShapeDtypeStruct((self.Z * self.a_rows + PAD, self.D), BF16)
        b = jax.ShapeDtypeStruct((2 * self.b_rows, self.D), BF16)
        return [a, a] + [b] * self.Z


def packed_row(scalars, tile):
    lane = lax.broadcasted_iota(jnp.int32, (1, tile), 1)
    row = jnp.zeros((1, tile), F32)
    for index, value in enumerate(scalars):
        row = row + jnp.where(lane == index, value, 0.0)
    return split_row(row, tile)


def split_row(row, tile):
    high = row.astype(BF16).astype(F32)
    middle = (row - high).astype(BF16).astype(F32)
    low = row - high - middle
    at = lax.broadcasted_iota(jnp.int32, (PAD, tile), 0)
    rows = jnp.where(at == 0, high, jnp.where(at == 1, middle, jnp.where(at == 2, low, 0.0)))
    return rows.astype(BF16)


def joined_row(rows):
    rows = rows.astype(F32)
    return rows[0:1] + rows[1:2] + rows[2:3]


def folded(value):
    return jnp.sum(value.reshape(value.shape[0] // 8, 8, value.shape[1]), axis=0)


def total(value):
    return jnp.sum(value, keepdims=True).reshape(1, 1)


def live_mask(plan, rows, cols, k):
    down = lax.broadcasted_iota(jnp.int32, (plan.D, plan.D), 0)
    across = lax.broadcasted_iota(jnp.int32, (plan.D, plan.D), 1)
    return jnp.logical_and(down < rows[k], across < cols[k])


def received_sums(plan, arrived):
    a_parts, b_parts = arrived[: plan.Z], arrived[plan.Z :]

    def tile(k):
        parts, i = (a_parts, k) if k < plan.Ta else (b_parts, k - plan.Ta)
        at = pl.ds(i * plan.D, plan.D)
        return functools.reduce(lambda x, y: x + y, [p[at, :].astype(F32) for p in parts])

    level = [joined_row(p[pl.ds(plan.a_rows, PAD), :]) for p in a_parts]
    while len(level) > 1:
        level = [level[i] + level[i + 1] for i in range(0, len(level), 2)]
    return tile, level[0]


def lane(row, index):
    return row[:, index : index + 1]


def shift_of(plan, a, b, d, e):
    alpha = a / plan.entries
    m = jnp.maximum(b - 2.0 * alpha * d + alpha * alpha * e, 0.0) / plan.entries
    return alpha, m


def update_first(plan, ins, outs, send):
    (start, rows, cols), (x_out,) = ins, outs
    norm = jnp.zeros((8, plan.D), F32)
    for k in range(plan.T):
        at = pl.ds(k * plan.D, plan.D)
        x = jnp.where(live_mask(plan, rows, cols, k), start[at, :].astype(F32), 0.0)
        x_out[at, :] = x
        send(k, x)
        norm = norm + folded(x * x)
    return [total(norm)]


def update_second(plan, ins, outs, send):
    (x_in, rows, cols, energy, own, own_row, helped), arrived = ins[:7], ins[7:]
    q_out, h_out, known_out = outs
    odd = in_odd_segment()
    half_tile, half_row = received_sums(plan, arrived)
    row = jnp.where(odd, own_row[0:1, :], half_row)

    def tile(k):
        at = pl.ds(k * plan.D, plan.D)
        return jnp.where(odd, own[at, :], half_tile(k) + helped[at, :].astype(F32))

    square = lane(row, 0)
    scale = lax.rsqrt(square / plan.entries + epsilon)
    known_out[...] = jnp.broadcast_to(scale * scale * square, known_out.shape)
    a = b = jnp.zeros((8, plan.D), F32)
    for k in range(plan.T):
        at = pl.ds(k * plan.D, plan.D)
        x = x_in[at, :]
        image = jnp.where(live_mask(plan, rows, cols, k), tile(k), 0.0) + energy[k] * x
        q = scale * x
        h = scale * image
        q_out[at, :] = q
        h_out[at, :] = h
        send(k, h)
        a = a + folded(q * h)
        b = b + folded(h * h)
    return [total(a), total(b)]


def update_third(plan, ins, outs, send):
    (q_in, h_in, known, rows, cols, energy), arrived = ins[:6], ins[6:]
    q_out, h_out, z_out, coef_out = outs
    tile, row = received_sums(plan, arrived)
    a, b = lane(row, 0), lane(row, 1)
    alpha, m = shift_of(plan, a, b, a, known[0:1, 0:1])
    beta, scale = jnp.sqrt(m), lax.rsqrt(m + epsilon)
    coef_out[0:1, :] = jnp.broadcast_to(alpha, (1, plan.D))
    coef_out[1:2, :] = jnp.broadcast_to(beta, (1, plan.D))
    sums = [jnp.zeros((8, plan.D), F32)] * 4
    for k in range(plan.T):
        at = pl.ds(k * plan.D, plan.D)
        q0, h0 = q_in[at, :], h_in[at, :]
        image = jnp.where(live_mask(plan, rows, cols, k), tile(k), 0.0) + energy[k] * h0
        q = scale * (h0 - alpha * q0)
        h = scale * (image - alpha * h0)
        z = h - beta * q0
        q_out[at, :] = q
        h_out[at, :] = h
        z_out[at, :] = z
        send(k, z)
        sums = [s + folded(p) for s, p in zip(sums, (q * h, z * z, z * q, q * q))]
    return [total(s) for s in sums]


def update_last(plan, ins, outs):
    (q_in, h_in, z_in, rows, cols, energy), arrived = ins[:6], ins[6:]
    q_out, z_out, coef_out = outs
    tile, row = received_sums(plan, arrived)
    alpha, m = shift_of(plan, *[lane(row, i) for i in range(4)])
    beta, scale = jnp.sqrt(m), lax.rsqrt(m + epsilon)
    coef_out[0:1, :] = jnp.broadcast_to(alpha, (1, plan.D))
    coef_out[1:2, :] = jnp.broadcast_to(beta, (1, plan.D))
    sums = [jnp.zeros((8, plan.D), F32)] * 4
    for k in range(plan.T):
        at = pl.ds(k * plan.D, plan.D)
        q1, h1, z1 = q_in[at, :], h_in[at, :], z_in[at, :]
        image = jnp.where(live_mask(plan, rows, cols, k), tile(k), 0.0) + energy[k] * z1
        q = scale * (z1 - alpha * q1)
        h = scale * (image - alpha * h1)
        z = h - beta * q1
        q_out[at, :] = q
        z_out[at, :] = z
        sums = [s + folded(p) for s, p in zip(sums, (q * h, z * z, z * q, q * q))]
    return [total(s) for s in sums]


def on_chip(body, ins, outs, scratch=()):
    spaces = [SMEM if len(x.shape) == 1 else VMEM for x in ins]
    return pl.pallas_call(
        body,
        in_specs=[pl.BlockSpec(memory_space=s) for s in spaces],
        out_specs=[pl.BlockSpec(memory_space=VMEM)] * len(outs),
        out_shape=list(outs),
        scratch_shapes=list(scratch),
        compiler_params=pltpu.CompilerParams(vmem_limit_bytes=16 * 2**20),
    )(*ins)


def in_odd_segment():
    return lax.axis_index("seg") % 2 == 1


class Block:
    def __init__(self, left, right, low, slots):
        self.left, self.right, self.low, self.slots = left, right, low, slots


def multiply(plan, pairs, half_ref, sum_ref):
    D, W, group = plan.D, plan.W, plan.group
    none = jnp.zeros((D, D), BF16)

    def rows(place, first, count):
        ref, block = place
        return ref[pl.ds(pl.multiple_of((block * W + first) * D, D), count * D), :]

    def several(step, carry):
        first = step * group
        for pair in pairs:
            v = [b.low[0][pl.ds(b.low[1] * D, D), :] for b in pair]
            both = jnp.concatenate(
                [jnp.concatenate([v[0], none], 1), jnp.concatenate([none, v[1]], 1)], 0
            )
            tiles = [rows(b.left, first, group) for b in pair]
            half_ref[...] = jnp.dot(
                jnp.concatenate(tiles, 1), both, preferred_element_type=F32
            ).astype(BF16)
            for w in range(group):
                for side, b in enumerate(pair):
                    product = jnp.dot(
                        half_ref[pl.ds(w * D, D), pl.ds(side * D, D)],
                        rows(b.right, first + w, 1),
                        preferred_element_type=F32,
                    )
                    ref, block = b.slots
                    slot = ref[block * W + first + w]
                    sum_ref[pl.ds(pl.multiple_of(slot * D, D), D), :] += product
        return carry

    lax.fori_loop(0, W // group, several, 0)


def scalars(plan, row, message_refs):
    for ref in message_refs[:2]:
        ref[pl.ds(plan.Z * plan.a_rows, PAD), :] = row


def flush(plan, sum_ref, message_refs):
    first = 0
    for ref in message_refs:
        rows = ref.shape[0] // plan.D * plan.D
        ref[pl.ds(0, rows), :] = sum_ref[pl.ds(first, rows), :].astype(BF16)
        first += rows


def work_space(plan):
    return [
        VMEM((plan.group * plan.D, 2 * plan.D), BF16),
        VMEM(((plan.n + 1) * plan.D, plan.D), F32),
    ]


def first_next(plan, row, left, right, low, slots):
    def body(row_ref, left_ref, right_ref, low_ref, slot_ref, *refs):
        message_refs, (half_ref, sum_ref) = refs[:-2], refs[-2:]

        @pl.when(jnp.logical_not(in_odd_segment()))
        def _():
            def at(k):
                return Block((left_ref, k), (right_ref, k), (low_ref, k), (slot_ref, k))

            sum_ref[...] = jnp.zeros(sum_ref.shape, F32)
            pairs = [(at(k), at(k + plan.H)) for k in range(plan.H)]
            multiply(plan, pairs, half_ref, sum_ref)
            flush(plan, sum_ref, message_refs)

        scalars(plan, row_ref[...], message_refs)

    ins = [row, left, right, low, slots]
    return on_chip(body, ins, plan.messages(), work_space(plan))


def first_half(plan, row, crossed, own, other):
    n_own = len(own)

    def body(row_ref, crossed_ref, *refs):
        right_ref, low_ref, slot_ref = refs[:n_own]
        held_ref, other_low_ref, other_slot_ref = refs[n_own : n_own + 3]
        message_refs, (half_ref, sum_ref) = refs[n_own + 3 : -2], refs[-2:]
        odd = in_odd_segment()

        def all_of(places):
            def at(k):
                return Block(*[(p, k) for p in places])

            sum_ref[...] = jnp.zeros(sum_ref.shape, F32)
            pairs = [(at(k), at(k + plan.H // 2)) for k in range(plan.H // 2)]
            multiply(plan, pairs, half_ref, sum_ref)
            flush(plan, sum_ref, message_refs)

        @pl.when(odd)
        def _():
            all_of((held_ref, crossed_ref, other_low_ref, other_slot_ref))

        @pl.when(jnp.logical_not(odd))
        def _():
            all_of((crossed_ref, right_ref, low_ref, slot_ref))

        scalars(plan, row_ref[...], message_refs)

    ins = [row, crossed] + own + other
    return on_chip(body, ins, plan.messages(), work_space(plan))


def operator_step(plan, update, ins, state_shapes, lefts, right, slots):
    n_in, n_state = len(ins), len(state_shapes)

    def body(*refs):
        own_ref, first_ref, last_ref, right_ref, slot_ref = refs[n_in : n_in + 5]
        state_refs = refs[n_in + 5 : n_in + 5 + n_state]
        message_refs = refs[n_in + 5 + n_state : -3]
        low_ref, half_ref, sum_ref = refs[-3:]
        odd = in_odd_segment()

        def send(k, value):
            low_ref[pl.ds(k * plan.D, plan.D), :] = value.astype(BF16)

        row = packed_row(update(plan, refs[:n_in], state_refs, send), plan.D)
        sum_ref[...] = jnp.zeros(sum_ref.shape, F32)

        def all_of(place):
            def at(k):
                return Block(place(k), (right_ref, k), (low_ref, k), (slot_ref, k))

            pairs = [(at(k), at(k + plan.H)) for k in range(plan.H)]
            multiply(plan, pairs, half_ref, sum_ref)

        @pl.when(odd)
        def _():
            all_of(lambda k: (own_ref, k))

        @pl.when(jnp.logical_not(odd))
        def _():
            all_of(lambda k: (first_ref, k) if k < plan.H else (last_ref, k - plan.H))

        flush(plan, sum_ref, message_refs)
        scalars(plan, row, message_refs)

    results = on_chip(
        body,
        list(ins) + list(lefts) + [right, slots],
        list(state_shapes) + plan.messages(),
        [VMEM((plan.T * plan.D, plan.D), BF16)] + work_space(plan),
    )
    return results[:n_state], results[n_state:]


def row_of(plan, values):
    across = lax.broadcasted_iota(jnp.int32, (8, plan.D), 1)
    row = jnp.zeros((8, plan.D), F32)
    for index, value in enumerate(values):
        row = row + jnp.where(across == index, value, 0.0)
    return row


def last_step(plan, ins, state_shapes):
    n_in = len(ins)

    def body(*refs):
        sums = update_last(plan, refs[:n_in], refs[n_in:-1])
        refs[-1][...] = row_of(plan, sums)

    row = jax.ShapeDtypeStruct((8, plan.D), F32)
    return on_chip(body, ins, list(state_shapes) + [row])


def outcome(plan, q, z, first, second, *sums):
    def body(q_ref, z_ref, first_ref, second_ref, *refs):
        added = functools.reduce(lambda x, y: x + y, [r[0:1, :] for r in refs[:-2]])
        residual_ref, coef_ref = refs[-2:]
        alpha, m = shift_of(plan, *[lane(added, i) for i in range(4)])
        residual_ref[...] = z_ref[...] - alpha * q_ref[...]
        values = [first_ref[0:1, 0:1], second_ref[0:1, 0:1], alpha]
        values += [first_ref[1:2, 0:1], second_ref[1:2, 0:1], jnp.sqrt(m)]
        coef_ref[...] = row_of(plan, values)

    row = jax.ShapeDtypeStruct((8, plan.D), F32)
    return on_chip(body, [q, z, first, second, *sums], [q, row])


def middle_a(plan, keep, got):
    rows = plan.a_rows

    def body(keep_ref, got_ref, *outs):
        end = pl.ds(plan.Z * rows, PAD)
        row = split_row(joined_row(keep_ref[end, :]) + joined_row(got_ref[end, :]), plan.D)
        for z, out in enumerate(outs):
            at = pl.ds(z * rows, rows)
            added = keep_ref[at, :].astype(F32) + got_ref[at, :].astype(F32)
            out[pl.ds(0, rows), :] = added.astype(BF16)
            out[pl.ds(rows, PAD), :] = row

    shape = jax.ShapeDtypeStruct((rows + PAD, plan.D), BF16)
    return on_chip(body, [keep, got], [shape] * plan.Z)


def middle_b(plan, parts):
    rows = plan.b_rows

    def body(*refs):
        for y, out in enumerate(refs[plan.Z :]):
            at = pl.ds(y * rows, rows)
            tiles = [p[at, :].astype(F32) for p in refs[: plan.Z]]
            out[...] = functools.reduce(lambda u, v: u + v, tiles).astype(out.dtype)

    shapes = [jax.ShapeDtypeStruct((rows, plan.D), d) for d in (F32, BF16)]
    return on_chip(body, parts, shapes)


def exchanged(plan, messages):
    keep, send, b_parts = messages[0], messages[1], messages[2:]
    others = range(plan.Z - 1, 0, -1)
    got = swapped(send, 1)
    b_got = [swapped(b_parts[z], 2 * z) for z in others]
    a_parts = middle_a(plan, keep, got)
    a_last = [swapped(a_parts[z], 2 * z) for z in others]
    b_keep, b_send = middle_b(plan, [b_parts[0]] + b_got)
    return [a_parts[0]] + a_last[::-1] + [b_keep, swapped(b_send, 1)]


def gathered(plan, arrived, dtype):
    def body(*refs):
        tile, row = received_sums(plan, refs[:-2])
        for k in range(plan.T):
            refs[-2][pl.ds(k * plan.D, plan.D), :] = tile(k).astype(dtype)
        refs[-1][...] = jnp.broadcast_to(row, refs[-1].shape)

    sums = jax.ShapeDtypeStruct((plan.T * plan.D, plan.D), dtype)
    row = jax.ShapeDtypeStruct((8, plan.D), F32)
    return on_chip(body, arrived, [sums, row])


def copying(sources, slices):
    n, m = len(sources), len(slices)

    def body(*refs):
        odd = in_odd_segment()

        def all_of(side):
            copies = []
            for i, choice in enumerate(slices):
                source, first = choice[side]
                from_ref = refs[source].at[pl.ds(first, choice[2])]
                copies.append(pltpu.make_async_copy(from_ref, refs[n + i], refs[n + m].at[i]))
            for copy in copies:
                copy.start()
            for copy in copies:
                copy.wait()

        pl.when(jnp.logical_not(odd))(lambda: all_of(0))
        pl.when(odd)(lambda: all_of(1))

    return pl.pallas_call(
        body,
        in_specs=[pl.BlockSpec(memory_space=pl.ANY)] * n,
        out_specs=[pl.BlockSpec(memory_space=VMEM)] * m,
        out_shape=[
            jax.ShapeDtypeStruct((c[2], sources[c[0][0]].shape[1]), sources[c[0][0]].dtype)
            for c in slices
        ],
        scratch_shapes=[pltpu.SemaphoreType.DMA((m,))],
        compiler_params=pltpu.CompilerParams(vmem_limit_bytes=16 * 2**20),
    )(*[pltpu.with_memory_space_constraint(x, pltpu.HBM) for x in sources])


def prepared(plan, start, rows, cols, feeds):
    def body(start_ref, rows_ref, cols_ref, feed_ref, *outs):
        x_ref, low_ref, row_ref, slot_ref, last_low_ref, last_slot_ref = outs
        me = lax.axis_index("blk")

        def several(w, carry):
            for k in range(plan.T):
                slot = plan.slot(feed_ref[k, w], me)
                slot_ref[k * plan.W + w] = slot
                if k >= plan.H:
                    last_slot_ref[(k - plan.H) * plan.W + w] = slot
            return carry

        lax.fori_loop(0, plan.W, several, 0)

        def send(k, value):
            low_ref[pl.ds(k * plan.D, plan.D), :] = value.astype(BF16)
            if k >= plan.H:
                last_low_ref[pl.ds((k - plan.H) * plan.D, plan.D), :] = value.astype(BF16)

        sums = update_first(plan, (start_ref, rows_ref, cols_ref), (x_ref,), send)
        row_ref[...] = packed_row(sums, plan.D)

    chip = pl.BlockSpec(memory_space=VMEM)
    scalar = pl.BlockSpec(memory_space=SMEM)
    last = plan.T - plan.H
    return pl.pallas_call(
        body,
        in_specs=[chip, scalar, scalar, scalar],
        out_specs=[chip, chip, chip, scalar, chip, scalar],
        out_shape=[
            jax.ShapeDtypeStruct(start.shape, F32),
            jax.ShapeDtypeStruct(start.shape, BF16),
            jax.ShapeDtypeStruct((PAD, plan.D), BF16),
            jax.ShapeDtypeStruct((plan.T * plan.W,), jnp.int32),
            jax.ShapeDtypeStruct((last * plan.D, plan.D), BF16),
            jax.ShapeDtypeStruct((last * plan.W,), jnp.int32),
        ],
        compiler_params=pltpu.CompilerParams(vmem_limit_bytes=16 * 2**20),
        name="prepared",
    )(start, rows, cols, feeds)


def local(
    start_vector,
    left_environment,
    right_environment,
    block_energy,
    sector_rows,
    sector_cols,
    feed_block,
):
    T, W, D = left_environment.shape[1:4]
    plan = Plan(T, W, D, lax.axis_size("blk"))
    helped = [s for s in range(1, lax.axis_size("seg")) if s % 2 == 0]
    helpers = [s - 1 for s in helped]

    left = left_environment.reshape(T * W * D, D)
    right = right_environment.reshape(T * W * D, D)
    rows, cols, energy = sector_rows[0], sector_cols[0], block_energy[0]
    vector = jax.ShapeDtypeStruct((T * D, D), F32)
    row = jax.ShapeDtypeStruct((8, D), F32)
    start = start_vector.reshape(T * D, D)
    every = T * W * D
    half_rows = every // 2

    (sent,) = copying([left, right], [((1, half_rows), (0, 0), half_rows)])
    pairs = list(zip(helpers, helped)) + list(zip(helped, helpers))
    crossed = lax.ppermute(sent, "seg", pairs)
    (own_side,) = copying([left, right], [((0, 0), (1, 0), every)])
    partner = swapped(own_side, 1, "seg")
    held_left, held_right = copying(
        [left, right], [((0, half_rows), (0, half_rows), half_rows), ((1, 0), (1, 0), every)]
    )
    x, low, square, slots, last_low, last_slots = prepared(
        plan, start, rows, cols, feed_block[0]
    )
    partner_low = swapped(low, 1, "seg")
    partner_slots = swapped(slots, 1, "seg")
    other_low = handed(last_low, helpers, -1)
    other_slots = handed(last_slots, helpers, -1)

    messages = first_next(plan, square, own_side, partner, partner_low, partner_slots)
    arrived = exchanged(plan, messages)
    own, own_row = gathered(plan, arrived, F32)
    own = swapped(own, 1, "seg")
    left_last = handed(held_left, helped, 1)
    messages = first_half(
        plan,
        square,
        crossed,
        [held_right, low, slots],
        [held_left, other_low, other_slots],
    )
    half = exchanged(plan, messages)
    help_sum, _ = gathered(plan, half, BF16)
    help_sum = handed(help_sum, helped, 1)
    lefts = [partner, crossed, left_last]
    (q0, h0, known), messages = operator_step(
        plan,
        update_second,
        [x, rows, cols, energy, own, own_row, help_sum] + half,
        [vector, vector, row],
        lefts,
        held_right,
        slots,
    )
    arrived = exchanged(plan, messages)
    (q1, h1, z1, first), messages = operator_step(
        plan,
        update_third,
        [q0, h0, known, rows, cols, energy] + arrived,
        [vector, vector, vector, row],
        lefts,
        held_right,
        slots,
    )
    arrived = exchanged(plan, messages)
    q2, z2, second, sums = last_step(
        plan, [q1, h1, z1, rows, cols, energy] + arrived, [vector, vector, row]
    )
    mask = 1
    while 2 * mask < plan.B:
        sums = sums + swapped(sums, mask)
        mask *= 2
    last = swapped(sums, mask)
    residual, coefficients = outcome(plan, q2, z2, first, second, sums, last)
    return (coefficients[:1, :6], residual.reshape(1, T, D, D))


def solution(mesh):
    return jax.shard_map(
        local,
        mesh=mesh,
        in_specs=(
            P("seg", "blk", None, None),
            P("seg", "blk", None, None, None),
            P("seg", "blk", None, None, None),
            P("seg", "blk"),
            P("seg", "blk"),
            P("seg", "blk"),
            P("seg", "blk", None),
        ),
        out_specs=(P("seg", None), P("seg", "blk", None, None)),
        check_vma=False,
    )
```

```python
import functools

import jax
import jax.numpy as jnp
from jax import lax
from jax.experimental import pallas as pl
from jax.experimental.pallas import tpu as pltpu
from jax.sharding import PartitionSpec as P


epsilon = 1e-06
F32 = jnp.float32
BF16 = jnp.bfloat16
PAD = 16
VMEM = pltpu.VMEM
SMEM = pltpu.SMEM


def handed(block, targets, distance):
    return lax.ppermute(block, "seg", [(s - distance, s) for s in targets])


def swapped(block, mask, axis="blk"):
    return lax.ppermute(block, axis, [(i, i ^ mask) for i in range(lax.axis_size(axis))])


class Plan:
    def __init__(self, tiles, channels, tile, blk, segments):
        self.T, self.W, self.D, self.B = tiles, channels, tile, blk
        self.Z = blk // 2
        self.Ta = tiles // 2
        self.Tb = tiles - self.Ta
        self.entries = float(tiles * blk * tile * tile)
        self.n = tiles * blk
        self.a_rows = self.Ta * tile
        self.b_rows = self.Tb * tile
        self.H = tiles // 2
        self.shared = segments == 4
        self.helped = 2
        self.group = next(
            c for c in range(max(1, channels // 2), 0, -1) if channels % c == 0
        )

    def slot(self, feed, me):
        tiles = jnp.int32(self.T)
        device, tile = lax.div(feed, tiles), lax.rem(feed, tiles)
        relative = device ^ me
        zr, yr = relative >> 1, relative & 1
        a = (yr * self.Z + zr) * self.Ta + tile
        b = self.B * self.Ta + (zr * 2 + yr) * self.Tb + (tile - self.Ta)
        return jnp.where(feed >= self.n, self.n, jnp.where(tile < self.Ta, a, b))

    def works_for_next(self):
        return lax.axis_index("seg") < self.helped

    def messages(self):
        a = jax.ShapeDtypeStruct((self.Z * self.a_rows + PAD, self.D), BF16)
        b = jax.ShapeDtypeStruct((2 * self.b_rows, self.D), BF16)
        return [a, a] + [b] * self.Z


def packed_row(scalars, tile):
    lane = lax.broadcasted_iota(jnp.int32, (1, tile), 1)
    row = jnp.zeros((1, tile), F32)
    for index, value in enumerate(scalars):
        row = row + jnp.where(lane == index, value, 0.0)
    return split_row(row, tile)


def split_row(row, tile):
    high = row.astype(BF16).astype(F32)
    middle = (row - high).astype(BF16).astype(F32)
    low = row - high - middle
    at = lax.broadcasted_iota(jnp.int32, (PAD, tile), 0)
    rows = jnp.where(at == 0, high, jnp.where(at == 1, middle, jnp.where(at == 2, low, 0.0)))
    return rows.astype(BF16)


def joined_row(rows):
    rows = rows.astype(F32)
    return rows[0:1] + rows[1:2] + rows[2:3]


def folded(value):
    return jnp.sum(value.reshape(value.shape[0] // 8, 8, value.shape[1]), axis=0)


def total(value):
    return jnp.sum(value, keepdims=True).reshape(1, 1)


def live_mask(plan, rows, cols, k):
    down = lax.broadcasted_iota(jnp.int32, (plan.D, plan.D), 0)
    across = lax.broadcasted_iota(jnp.int32, (plan.D, plan.D), 1)
    return jnp.logical_and(down < rows[k], across < cols[k])


def received_sums(plan, arrived):
    a_parts, b_parts = arrived[: plan.Z], arrived[plan.Z :]

    def tile(k):
        parts, i = (a_parts, k) if k < plan.Ta else (b_parts, k - plan.Ta)
        at = pl.ds(i * plan.D, plan.D)
        return functools.reduce(lambda x, y: x + y, [p[at, :].astype(F32) for p in parts])

    level = [joined_row(p[pl.ds(plan.a_rows, PAD), :]) for p in a_parts]
    while len(level) > 1:
        level = [level[i] + level[i + 1] for i in range(0, len(level), 2)]
    return tile, level[0]


def lane(row, index):
    return row[:, index : index + 1]


def shift_of(plan, a, b, d, e):
    alpha = a / plan.entries
    m = jnp.maximum(b - 2.0 * alpha * d + alpha * alpha * e, 0.0) / plan.entries
    return alpha, m


def update_first(plan, ins, outs, send):
    (start, rows, cols), (x_out,) = ins, outs
    norm = jnp.zeros((8, plan.D), F32)
    for k in range(plan.T):
        at = pl.ds(k * plan.D, plan.D)
        x = jnp.where(live_mask(plan, rows, cols, k), start[at, :].astype(F32), 0.0)
        x_out[at, :] = x
        send(k, x)
        norm = norm + folded(x * x)
    return [total(norm)]


def update_second(plan, ins, outs, send):
    (x_in, rows, cols, energy), arrived = ins[:4], ins[4:]
    q_out, h_out, known_out = outs
    if plan.shared:
        handed_on, arrived = arrived[0], arrived[1:]
    own_tile, row = received_sums(plan, arrived)

    def tile(k):
        if not plan.shared:
            return own_tile(k)
        kept = jnp.where(plan.works_for_next(), 0.0, own_tile(k))
        return kept + handed_on[pl.ds(k * plan.D, plan.D), :].astype(F32)

    square = lane(row, 0)
    scale = lax.rsqrt(square / plan.entries + epsilon)
    known_out[...] = jnp.broadcast_to(scale * scale * square, known_out.shape)
    a = b = jnp.zeros((8, plan.D), F32)
    for k in range(plan.T):
        at = pl.ds(k * plan.D, plan.D)
        x = x_in[at, :]
        image = jnp.where(live_mask(plan, rows, cols, k), tile(k), 0.0) + energy[k] * x
        q = scale * x
        h = scale * image
        q_out[at, :] = q
        h_out[at, :] = h
        send(k, h)
        a = a + folded(q * h)
        b = b + folded(h * h)
    return [total(a), total(b)]


def update_third(plan, ins, outs, send):
    (q_in, h_in, known, rows, cols, energy), arrived = ins[:6], ins[6:]
    q_out, h_out, z_out, coef_out = outs
    tile, row = received_sums(plan, arrived)
    a, b = lane(row, 0), lane(row, 1)
    alpha, m = shift_of(plan, a, b, a, known[0:1, 0:1])
    beta, scale = jnp.sqrt(m), lax.rsqrt(m + epsilon)
    coef_out[0:1, :] = jnp.broadcast_to(alpha, (1, plan.D))
    coef_out[1:2, :] = jnp.broadcast_to(beta, (1, plan.D))
    sums = [jnp.zeros((8, plan.D), F32)] * 4
    for k in range(plan.T):
        at = pl.ds(k * plan.D, plan.D)
        q0, h0 = q_in[at, :], h_in[at, :]
        image = jnp.where(live_mask(plan, rows, cols, k), tile(k), 0.0) + energy[k] * h0
        q = scale * (h0 - alpha * q0)
        h = scale * (image - alpha * h0)
        z = h - beta * q0
        q_out[at, :] = q
        h_out[at, :] = h
        z_out[at, :] = z
        send(k, z)
        sums = [s + folded(p) for s, p in zip(sums, (q * h, z * z, z * q, q * q))]
    return [total(s) for s in sums]


def update_last(plan, ins, outs):
    (q_in, h_in, z_in, rows, cols, energy), arrived = ins[:6], ins[6:]
    q_out, z_out, coef_out = outs
    tile, row = received_sums(plan, arrived)
    alpha, m = shift_of(plan, *[lane(row, i) for i in range(4)])
    beta, scale = jnp.sqrt(m), lax.rsqrt(m + epsilon)
    coef_out[0:1, :] = jnp.broadcast_to(alpha, (1, plan.D))
    coef_out[1:2, :] = jnp.broadcast_to(beta, (1, plan.D))
    sums = [jnp.zeros((8, plan.D), F32)] * 4
    for k in range(plan.T):
        at = pl.ds(k * plan.D, plan.D)
        q1, h1, z1 = q_in[at, :], h_in[at, :], z_in[at, :]
        image = jnp.where(live_mask(plan, rows, cols, k), tile(k), 0.0) + energy[k] * z1
        q = scale * (z1 - alpha * q1)
        h = scale * (image - alpha * h1)
        z = h - beta * q1
        q_out[at, :] = q
        z_out[at, :] = z
        sums = [s + folded(p) for s, p in zip(sums, (q * h, z * z, z * q, q * q))]
    return [total(s) for s in sums]


def on_chip(body, ins, outs, scratch=()):
    spaces = [SMEM if len(x.shape) == 1 else VMEM for x in ins]
    return pl.pallas_call(
        body,
        in_specs=[pl.BlockSpec(memory_space=s) for s in spaces],
        out_specs=[pl.BlockSpec(memory_space=VMEM)] * len(outs),
        out_shape=list(outs),
        scratch_shapes=list(scratch),
        compiler_params=pltpu.CompilerParams(vmem_limit_bytes=16 * 2**20),
    )(*ins)


def in_odd_segment():
    return lax.axis_index("seg") % 2 == 1


class Block:
    def __init__(self, left, right, low, slots):
        self.left, self.right, self.low, self.slots = left, right, low, slots


def multiply(plan, pairs, half_ref, sum_ref):
    D, W, group = plan.D, plan.W, plan.group
    none = jnp.zeros((D, D), BF16)

    def rows(place, first, count):
        ref, block = place
        return ref[pl.ds(pl.multiple_of((block * W + first) * D, D), count * D), :]

    def several(step, carry):
        first = step * group
        for pair in pairs:
            v = [b.low[0][pl.ds(b.low[1] * D, D), :] for b in pair]
            both = jnp.concatenate(
                [jnp.concatenate([v[0], none], 1), jnp.concatenate([none, v[1]], 1)], 0
            )
            tiles = [rows(b.left, first, group) for b in pair]
            half_ref[...] = jnp.dot(
                jnp.concatenate(tiles, 1), both, preferred_element_type=F32
            ).astype(BF16)
            for w in range(group):
                for side, b in enumerate(pair):
                    product = jnp.dot(
                        half_ref[pl.ds(w * D, D), pl.ds(side * D, D)],
                        rows(b.right, first + w, 1),
                        preferred_element_type=F32,
                    )
                    ref, block = b.slots
                    slot = ref[block * W + first + w]
                    sum_ref[pl.ds(pl.multiple_of(slot * D, D), D), :] += product
        return carry

    lax.fori_loop(0, W // group, several, 0)


def scalars(plan, row, message_refs):
    for ref in message_refs[:2]:
        ref[pl.ds(plan.Z * plan.a_rows, PAD), :] = row


def flush(plan, sum_ref, message_refs):
    first = 0
    for ref in message_refs:
        rows = ref.shape[0] // plan.D * plan.D
        ref[pl.ds(0, rows), :] = sum_ref[pl.ds(first, rows), :].astype(BF16)
        first += rows


def work_space(plan):
    return [
        VMEM((plan.group * plan.D, 2 * plan.D), BF16),
        VMEM(((plan.n + 1) * plan.D, plan.D), F32),
    ]


def first_step(plan, row, roles):
    ins, places = [row], []
    for _, arrays in roles:
        for array in arrays:
            if all(array is not known for known in ins):
                ins.append(array)
        places.append([next(i for i, a in enumerate(ins) if a is array) for array in arrays])

    def body(*refs):
        n = len(ins)
        message_refs, (half_ref, sum_ref) = refs[n:-2], refs[-2:]

        def work(place):
            def at(k):
                return Block(*[(refs[i], k) for i in place])

            blocks = refs[place[0]].shape[0] // (plan.W * plan.D)
            sum_ref[...] = jnp.zeros(sum_ref.shape, F32)
            pairs = [(at(k), at(k + blocks // 2)) for k in range(blocks // 2)]
            multiply(plan, pairs, half_ref, sum_ref)

        for (segment, _), place in zip(roles, places):
            if segment is None:
                work(place)
            else:
                pl.when(lax.axis_index("seg") == segment)(functools.partial(work, place))
        flush(plan, sum_ref, message_refs)
        scalars(plan, refs[0][...], message_refs)

    return on_chip(body, ins, plan.messages(), work_space(plan))


def operator_step(plan, update, ins, state_shapes, lefts, right, slots):
    n_in, n_state = len(ins), len(state_shapes)

    def body(*refs):
        left_refs = refs[n_in : n_in + len(lefts)]
        n = n_in + len(lefts)
        right_ref, slot_ref = refs[n : n + 2]
        state_refs = refs[n + 2 : n + 2 + n_state]
        message_refs = refs[n + 2 + n_state : -3]
        low_ref, half_ref, sum_ref = refs[-3:]
        odd = in_odd_segment()

        def send(k, value):
            low_ref[pl.ds(k * plan.D, plan.D), :] = value.astype(BF16)

        row = packed_row(update(plan, refs[:n_in], state_refs, send), plan.D)
        sum_ref[...] = jnp.zeros(sum_ref.shape, F32)

        def all_of(place):
            def at(k):
                return Block(place(k), (right_ref, k), (low_ref, k), (slot_ref, k))

            pairs = [(at(k), at(k + plan.H)) for k in range(plan.H)]
            multiply(plan, pairs, half_ref, sum_ref)

        def in_halves(k):
            return (left_refs[1], k) if k < plan.H else (left_refs[2], k - plan.H)

        if plan.shared:
            pl.when(odd)(lambda: all_of(lambda k: (left_refs[0], k)))
            pl.when(jnp.logical_not(odd))(lambda: all_of(in_halves))
        else:
            all_of(lambda k: (left_refs[0], k))

        flush(plan, sum_ref, message_refs)
        scalars(plan, row, message_refs)

    results = on_chip(
        body,
        list(ins) + list(lefts) + [right, slots],
        list(state_shapes) + plan.messages(),
        [VMEM((plan.T * plan.D, plan.D), BF16)] + work_space(plan),
    )
    return results[:n_state], results[n_state:]


def row_of(plan, values):
    across = lax.broadcasted_iota(jnp.int32, (8, plan.D), 1)
    row = jnp.zeros((8, plan.D), F32)
    for index, value in enumerate(values):
        row = row + jnp.where(across == index, value, 0.0)
    return row


def last_step(plan, ins, state_shapes):
    n_in = len(ins)

    def body(*refs):
        sums = update_last(plan, refs[:n_in], refs[n_in:-1])
        refs[-1][...] = row_of(plan, sums)

    row = jax.ShapeDtypeStruct((8, plan.D), F32)
    return on_chip(body, ins, list(state_shapes) + [row])


def outcome(plan, q, z, first, second, *sums):
    def body(q_ref, z_ref, first_ref, second_ref, *refs):
        added = functools.reduce(lambda x, y: x + y, [r[0:1, :] for r in refs[:-2]])
        residual_ref, coef_ref = refs[-2:]
        alpha, m = shift_of(plan, *[lane(added, i) for i in range(4)])
        residual_ref[...] = z_ref[...] - alpha * q_ref[...]
        values = [first_ref[0:1, 0:1], second_ref[0:1, 0:1], alpha]
        values += [first_ref[1:2, 0:1], second_ref[1:2, 0:1], jnp.sqrt(m)]
        coef_ref[...] = row_of(plan, values)

    row = jax.ShapeDtypeStruct((8, plan.D), F32)
    return on_chip(body, [q, z, first, second, *sums], [q, row])


def middle_a(plan, keep, got):
    rows = plan.a_rows

    def body(keep_ref, got_ref, *outs):
        end = pl.ds(plan.Z * rows, PAD)
        row = split_row(joined_row(keep_ref[end, :]) + joined_row(got_ref[end, :]), plan.D)
        for z, out in enumerate(outs):
            at = pl.ds(z * rows, rows)
            added = keep_ref[at, :].astype(F32) + got_ref[at, :].astype(F32)
            out[pl.ds(0, rows), :] = added.astype(BF16)
            out[pl.ds(rows, PAD), :] = row

    shape = jax.ShapeDtypeStruct((rows + PAD, plan.D), BF16)
    return on_chip(body, [keep, got], [shape] * plan.Z)


def middle_b(plan, parts):
    rows = plan.b_rows

    def body(*refs):
        for y, out in enumerate(refs[plan.Z :]):
            at = pl.ds(y * rows, rows)
            tiles = [p[at, :].astype(F32) for p in refs[: plan.Z]]
            out[...] = functools.reduce(lambda u, v: u + v, tiles).astype(out.dtype)

    shapes = [jax.ShapeDtypeStruct((rows, plan.D), d) for d in (F32, BF16)]
    return on_chip(body, parts, shapes)


def exchanged(plan, messages):
    keep, send, b_parts = messages[0], messages[1], messages[2:]
    others = range(plan.Z - 1, 0, -1)
    got = swapped(send, 1)
    b_got = [swapped(b_parts[z], 2 * z) for z in others]
    a_parts = middle_a(plan, keep, got)
    a_last = [swapped(a_parts[z], 2 * z) for z in others]
    b_keep, b_send = middle_b(plan, [b_parts[0]] + b_got)
    return [a_parts[0]] + a_last[::-1] + [b_keep, swapped(b_send, 1)]


def gathered(plan, arrived, dtype):
    def body(*refs):
        tile, _ = received_sums(plan, refs[:-1])
        for k in range(plan.T):
            refs[-1][pl.ds(k * plan.D, plan.D), :] = tile(k).astype(dtype)

    sums = jax.ShapeDtypeStruct((plan.T * plan.D, plan.D), dtype)
    return on_chip(body, arrived, [sums])[0]


def copying(sources, slices):
    n, m = len(sources), len(slices)

    def body(*refs):
        odd = in_odd_segment()

        def all_of(side):
            copies = []
            for i, choice in enumerate(slices):
                source, first = choice[side]
                from_ref = refs[source].at[pl.ds(first, choice[2])]
                copies.append(pltpu.make_async_copy(from_ref, refs[n + i], refs[n + m].at[i]))
            for copy in copies:
                copy.start()
            for copy in copies:
                copy.wait()

        pl.when(jnp.logical_not(odd))(lambda: all_of(0))
        pl.when(odd)(lambda: all_of(1))

    return pl.pallas_call(
        body,
        in_specs=[pl.BlockSpec(memory_space=pl.ANY)] * n,
        out_specs=[pl.BlockSpec(memory_space=VMEM)] * m,
        out_shape=[
            jax.ShapeDtypeStruct((c[2], sources[c[0][0]].shape[1]), sources[c[0][0]].dtype)
            for c in slices
        ],
        scratch_shapes=[pltpu.SemaphoreType.DMA((m,))],
        compiler_params=pltpu.CompilerParams(vmem_limit_bytes=16 * 2**20),
    )(*[pltpu.with_memory_space_constraint(x, pltpu.HBM) for x in sources])


def prepared(plan, start, rows, cols, feeds):
    def body(start_ref, rows_ref, cols_ref, feed_ref, *outs):
        x_ref, low_ref, row_ref, slot_ref, last_low_ref, last_slot_ref = outs
        me = lax.axis_index("blk")

        def several(w, carry):
            for k in range(plan.T):
                slot = plan.slot(feed_ref[k, w], me)
                slot_ref[k * plan.W + w] = slot
                if k >= plan.H:
                    last_slot_ref[(k - plan.H) * plan.W + w] = slot
            return carry

        lax.fori_loop(0, plan.W, several, 0)

        def send(k, value):
            low_ref[pl.ds(k * plan.D, plan.D), :] = value.astype(BF16)
            if k >= plan.H:
                last_low_ref[pl.ds((k - plan.H) * plan.D, plan.D), :] = value.astype(BF16)

        sums = update_first(plan, (start_ref, rows_ref, cols_ref), (x_ref,), send)
        row_ref[...] = packed_row(sums, plan.D)

    chip = pl.BlockSpec(memory_space=VMEM)
    scalar = pl.BlockSpec(memory_space=SMEM)
    last = plan.T - plan.H
    return pl.pallas_call(
        body,
        in_specs=[chip, scalar, scalar, scalar],
        out_specs=[chip, chip, chip, scalar, chip, scalar],
        out_shape=[
            jax.ShapeDtypeStruct(start.shape, F32),
            jax.ShapeDtypeStruct(start.shape, BF16),
            jax.ShapeDtypeStruct((PAD, plan.D), BF16),
            jax.ShapeDtypeStruct((plan.T * plan.W,), jnp.int32),
            jax.ShapeDtypeStruct((last * plan.D, plan.D), BF16),
            jax.ShapeDtypeStruct((last * plan.W,), jnp.int32),
        ],
        compiler_params=pltpu.CompilerParams(vmem_limit_bytes=16 * 2**20),
        name="prepared",
    )(start, rows, cols, feeds)


def plain_start(plan, left, right, start, rows, cols, feeds):
    segments = range(1, lax.axis_size("seg"))
    left = handed(left, segments, 1)
    every = right.shape[0]
    (held_right,) = copying([right], [((0, 0), (0, 0), every)])
    x, low, square, slots, _, _ = prepared(plan, start, rows, cols, feeds)
    messages = first_step(plan, square, [(None, [left, held_right, low, slots])])
    return x, slots, [left], held_right, exchanged(plan, messages)


def shared_start(plan, left, right, start, rows, cols, feeds):
    every = right.shape[0]
    half = every // 2
    helped, helper = plan.helped, plan.helped - 1

    (sent,) = copying([left, right], [((1, half), (0, 0), half)])
    crossed = lax.ppermute(sent, "seg", [(helper, helped), (helped, helper)])
    (own_side,) = copying([left, right], [((0, 0), (1, 0), every)])
    partner = swapped(own_side, 1, "seg")
    x, low, square, slots, last_low, last_slots = prepared(plan, start, rows, cols, feeds)
    partner_low = swapped(low, 1, "seg")
    partner_slots = swapped(slots, 1, "seg")
    other_low = handed(last_low, [helper], -1)
    other_slots = handed(last_slots, [helper], -1)
    held_left, held_right = copying(
        [left, right], [((0, half), (0, half), half), ((1, 0), (1, 0), every)]
    )
    left_last = handed(held_left, [helped], 1)

    roles = [
        (helper - 1, [own_side, partner, partner_low, partner_slots]),
        (helper, [held_left, crossed, other_low, other_slots]),
        (helped, [crossed, held_right, low, slots]),
        (helped + 1, [partner, held_right, low, slots]),
    ]
    messages = first_step(plan, square, roles)
    arrived = exchanged(plan, messages)
    sums = gathered(plan, arrived, BF16)
    got = handed(sums, [helper, helped], 1)
    return x, slots, [partner, crossed, left_last], held_right, [got] + arrived


def local(
    start_vector,
    left_environment,
    right_environment,
    block_energy,
    sector_rows,
    sector_cols,
    feed_block,
):
    T, W, D = left_environment.shape[1:4]
    plan = Plan(T, W, D, lax.axis_size("blk"), lax.axis_size("seg"))
    left = left_environment.reshape(T * W * D, D)
    right = right_environment.reshape(T * W * D, D)
    rows, cols, energy = sector_rows[0], sector_cols[0], block_energy[0]
    vector = jax.ShapeDtypeStruct((T * D, D), F32)
    row = jax.ShapeDtypeStruct((8, D), F32)
    start = start_vector.reshape(T * D, D)
    first = shared_start if plan.shared else plain_start
    x, slots, lefts, held_right, arrived = first(
        plan, left, right, start, rows, cols, feed_block[0]
    )
    (q0, h0, known), messages = operator_step(
        plan,
        update_second,
        [x, rows, cols, energy] + arrived,
        [vector, vector, row],
        lefts,
        held_right,
        slots,
    )
    arrived = exchanged(plan, messages)
    (q1, h1, z1, first), messages = operator_step(
        plan,
        update_third,
        [q0, h0, known, rows, cols, energy] + arrived,
        [vector, vector, vector, row],
        lefts,
        held_right,
        slots,
    )
    arrived = exchanged(plan, messages)
    q2, z2, second, sums = last_step(
        plan, [q1, h1, z1, rows, cols, energy] + arrived, [vector, vector, row]
    )
    mask = 1
    while 2 * mask < plan.B:
        sums = sums + swapped(sums, mask)
        mask *= 2
    last = swapped(sums, mask)
    residual, coefficients = outcome(plan, q2, z2, first, second, sums, last)
    return (coefficients[:1, :6], residual.reshape(1, T, D, D))


def solution(mesh):
    return jax.shard_map(
        local,
        mesh=mesh,
        in_specs=(
            P("seg", "blk", None, None),
            P("seg", "blk", None, None, None),
            P("seg", "blk", None, None, None),
            P("seg", "blk"),
            P("seg", "blk"),
            P("seg", "blk"),
            P("seg", "blk", None),
        ),
        out_specs=(P("seg", None), P("seg", "blk", None, None)),
        check_vma=False,
    )
```

```python
import functools

import jax
import jax.numpy as jnp
from jax import lax
from jax.experimental import pallas as pl
from jax.experimental.pallas import tpu as pltpu
from jax.sharding import PartitionSpec as P


epsilon = 1e-06
F32 = jnp.float32
BF16 = jnp.bfloat16
PAD = 16
VMEM = pltpu.VMEM
SMEM = pltpu.SMEM


def handed(block, targets, distance):
    return lax.ppermute(block, "seg", [(s - distance, s) for s in targets])


def swapped(block, mask, axis="blk"):
    return lax.ppermute(block, axis, [(i, i ^ mask) for i in range(lax.axis_size(axis))])


class Plan:
    def __init__(self, tiles, channels, tile, blk, segments):
        self.T, self.W, self.D, self.B = tiles, channels, tile, blk
        self.Z = blk // 2
        self.Ta = tiles // 2
        self.Tb = tiles - self.Ta
        self.entries = float(tiles * blk * tile * tile)
        self.n = tiles * blk
        self.a_rows = self.Ta * tile
        self.b_rows = self.Tb * tile
        self.H = tiles // 2
        self.shared = segments == 4
        self.helped = 2
        self.group = next(
            c for c in range(max(1, channels // 2), 0, -1) if channels % c == 0
        )

    def slot(self, feed, me):
        tiles = jnp.int32(self.T)
        device, tile = lax.div(feed, tiles), lax.rem(feed, tiles)
        relative = device ^ me
        zr, yr = relative >> 1, relative & 1
        a = (yr * self.Z + zr) * self.Ta + tile
        b = self.B * self.Ta + (zr * 2 + yr) * self.Tb + (tile - self.Ta)
        return jnp.where(feed >= self.n, self.n, jnp.where(tile < self.Ta, a, b))

    def works_for_next(self):
        return lax.axis_index("seg") < self.helped

    def messages(self):
        a = jax.ShapeDtypeStruct((self.Z * self.a_rows + PAD, self.D), BF16)
        b = jax.ShapeDtypeStruct((2 * self.b_rows, self.D), BF16)
        return [a, a] + [b] * self.Z


def packed_row(scalars, tile):
    lane = lax.broadcasted_iota(jnp.int32, (1, tile), 1)
    row = jnp.zeros((1, tile), F32)
    for index, value in enumerate(scalars):
        row = row + jnp.where(lane == index, value, 0.0)
    return split_row(row, tile)


def split_row(row, tile):
    high = row.astype(BF16).astype(F32)
    middle = (row - high).astype(BF16).astype(F32)
    low = row - high - middle
    at = lax.broadcasted_iota(jnp.int32, (PAD, tile), 0)
    rows = jnp.where(at == 0, high, jnp.where(at == 1, middle, jnp.where(at == 2, low, 0.0)))
    return rows.astype(BF16)


def joined_row(rows):
    rows = rows.astype(F32)
    return rows[0:1] + rows[1:2] + rows[2:3]


def folded(value):
    return jnp.sum(value.reshape(value.shape[0] // 8, 8, value.shape[1]), axis=0)


def total(value):
    return jnp.sum(value, keepdims=True).reshape(1, 1)


def live_mask(plan, rows, cols, k):
    down = lax.broadcasted_iota(jnp.int32, (plan.D, plan.D), 0)
    across = lax.broadcasted_iota(jnp.int32, (plan.D, plan.D), 1)
    return jnp.logical_and(down < rows[k], across < cols[k])


def received_sums(plan, arrived):
    a_parts, b_parts = arrived[: plan.Z], arrived[plan.Z :]

    def tile(k):
        parts, i = (a_parts, k) if k < plan.Ta else (b_parts, k - plan.Ta)
        at = pl.ds(i * plan.D, plan.D)
        return functools.reduce(lambda x, y: x + y, [p[at, :].astype(F32) for p in parts])

    level = [joined_row(p[pl.ds(plan.a_rows, PAD), :]) for p in a_parts]
    while len(level) > 1:
        level = [level[i] + level[i + 1] for i in range(0, len(level), 2)]
    return tile, level[0]


def lane(row, index):
    return row[:, index : index + 1]


def shift_of(plan, a, b, d, e):
    alpha = a / plan.entries
    m = jnp.maximum(b - 2.0 * alpha * d + alpha * alpha * e, 0.0) / plan.entries
    return alpha, m


def update_first(plan, ins, outs, send):
    (start, rows, cols), (x_out,) = ins, outs
    norm = jnp.zeros((8, plan.D), F32)
    for k in range(plan.T):
        at = pl.ds(k * plan.D, plan.D)
        x = jnp.where(live_mask(plan, rows, cols, k), start[at, :].astype(F32), 0.0)
        x_out[at, :] = x
        send(k, x)
        norm = norm + folded(x * x)
    return [total(norm)]


def update_second(plan, ins, outs, send):
    (x_in, rows, cols, energy), arrived = ins[:4], ins[4:]
    q_out, h_out, known_out = outs
    if plan.shared:
        handed_on, arrived = arrived[0], arrived[1:]
    own_tile, row = received_sums(plan, arrived)

    def tile(k):
        if not plan.shared:
            return own_tile(k)
        kept = jnp.where(plan.works_for_next(), 0.0, own_tile(k))
        return kept + handed_on[pl.ds(k * plan.D, plan.D), :].astype(F32)

    square = lane(row, 0)
    scale = lax.rsqrt(square / plan.entries + epsilon)
    known_out[...] = jnp.broadcast_to(scale * scale * square, known_out.shape)
    a = b = jnp.zeros((8, plan.D), F32)
    for k in range(plan.T):
        at = pl.ds(k * plan.D, plan.D)
        x = x_in[at, :]
        image = jnp.where(live_mask(plan, rows, cols, k), tile(k), 0.0) + energy[k] * x
        q = scale * x
        h = scale * image
        q_out[at, :] = q
        h_out[at, :] = h
        send(k, h)
        a = a + folded(q * h)
        b = b + folded(h * h)
    return [total(a), total(b)]


def update_third(plan, ins, outs, send):
    (q_in, h_in, known, rows, cols, energy), arrived = ins[:6], ins[6:]
    q_out, h_out, z_out, coef_out = outs
    tile, row = received_sums(plan, arrived)
    a, b = lane(row, 0), lane(row, 1)
    alpha, m = shift_of(plan, a, b, a, known[0:1, 0:1])
    beta, scale = jnp.sqrt(m), lax.rsqrt(m + epsilon)
    coef_out[0:1, :] = jnp.broadcast_to(alpha, (1, plan.D))
    coef_out[1:2, :] = jnp.broadcast_to(beta, (1, plan.D))
    sums = [jnp.zeros((8, plan.D), F32)] * 4
    for k in range(plan.T):
        at = pl.ds(k * plan.D, plan.D)
        q0, h0 = q_in[at, :], h_in[at, :]
        image = jnp.where(live_mask(plan, rows, cols, k), tile(k), 0.0) + energy[k] * h0
        q = scale * (h0 - alpha * q0)
        h = scale * (image - alpha * h0)
        z = h - beta * q0
        q_out[at, :] = q
        h_out[at, :] = h
        z_out[at, :] = z
        send(k, z)
        sums = [s + folded(p) for s, p in zip(sums, (q * h, z * z, z * q, q * q))]
    return [total(s) for s in sums]


def update_last(plan, ins, outs):
    (q_in, h_in, z_in, rows, cols, energy), arrived = ins[:6], ins[6:]
    q_out, z_out, coef_out = outs
    tile, row = received_sums(plan, arrived)
    alpha, m = shift_of(plan, *[lane(row, i) for i in range(4)])
    beta, scale = jnp.sqrt(m), lax.rsqrt(m + epsilon)
    coef_out[0:1, :] = jnp.broadcast_to(alpha, (1, plan.D))
    coef_out[1:2, :] = jnp.broadcast_to(beta, (1, plan.D))
    sums = [jnp.zeros((8, plan.D), F32)] * 4
    for k in range(plan.T):
        at = pl.ds(k * plan.D, plan.D)
        q1, h1, z1 = q_in[at, :], h_in[at, :], z_in[at, :]
        image = jnp.where(live_mask(plan, rows, cols, k), tile(k), 0.0) + energy[k] * z1
        q = scale * (z1 - alpha * q1)
        h = scale * (image - alpha * h1)
        z = h - beta * q1
        q_out[at, :] = q
        z_out[at, :] = z
        sums = [s + folded(p) for s, p in zip(sums, (q * h, z * z, z * q, q * q))]
    return [total(s) for s in sums]


def on_chip(body, ins, outs, scratch=()):
    spaces = [SMEM if len(x.shape) == 1 else VMEM for x in ins]
    return pl.pallas_call(
        body,
        in_specs=[pl.BlockSpec(memory_space=s) for s in spaces],
        out_specs=[pl.BlockSpec(memory_space=VMEM)] * len(outs),
        out_shape=list(outs),
        scratch_shapes=list(scratch),
        compiler_params=pltpu.CompilerParams(vmem_limit_bytes=16 * 2**20),
    )(*ins)


def in_odd_segment():
    return lax.axis_index("seg") % 2 == 1


class Block:
    def __init__(self, left, right, low, slots):
        self.left, self.right, self.low, self.slots = left, right, low, slots


def multiply(plan, pairs, half_ref, sum_ref):
    D, W, group = plan.D, plan.W, plan.group
    none = jnp.zeros((D, D), BF16)

    def rows(place, first, count):
        ref, block = place
        return ref[pl.ds(pl.multiple_of((block * W + first) * D, D), count * D), :]

    def several(step, carry):
        first = step * group
        for pair in pairs:
            v = [b.low[0][pl.ds(b.low[1] * D, D), :] for b in pair]
            both = jnp.concatenate(
                [jnp.concatenate([v[0], none], 1), jnp.concatenate([none, v[1]], 1)], 0
            )
            tiles = [rows(b.left, first, group) for b in pair]
            half_ref[...] = jnp.dot(
                jnp.concatenate(tiles, 1), both, preferred_element_type=F32
            ).astype(BF16)
            for w in range(group):
                for side, b in enumerate(pair):
                    product = jnp.dot(
                        half_ref[pl.ds(w * D, D), pl.ds(side * D, D)],
                        rows(b.right, first + w, 1),
                        preferred_element_type=F32,
                    )
                    ref, block = b.slots
                    slot = ref[block * W + first + w]
                    sum_ref[pl.ds(pl.multiple_of(slot * D, D), D), :] += product
        return carry

    lax.fori_loop(0, W // group, several, 0)


def scalars(plan, row, message_refs):
    for ref in message_refs[:2]:
        ref[pl.ds(plan.Z * plan.a_rows, PAD), :] = row


def flush(plan, sum_ref, message_refs):
    first = 0
    for ref in message_refs:
        rows = ref.shape[0] // plan.D * plan.D
        ref[pl.ds(0, rows), :] = sum_ref[pl.ds(first, rows), :].astype(BF16)
        first += rows


def work_space(plan):
    return [
        VMEM((plan.group * plan.D, 2 * plan.D), BF16),
        VMEM(((plan.n + 1) * plan.D, plan.D), F32),
    ]


def first_step(plan, row, roles):
    ins, places = [row], []
    for _, arrays in roles:
        for array in arrays:
            if all(array is not known for known in ins):
                ins.append(array)
        places.append([next(i for i, a in enumerate(ins) if a is array) for array in arrays])

    def body(*refs):
        n = len(ins)
        message_refs, (half_ref, sum_ref) = refs[n:-2], refs[-2:]

        def work(place):
            def at(k):
                return Block(*[(refs[i], k) for i in place])

            blocks = refs[place[0]].shape[0] // (plan.W * plan.D)
            sum_ref[...] = jnp.zeros(sum_ref.shape, F32)
            pairs = [(at(k), at(k + blocks // 2)) for k in range(blocks // 2)]
            multiply(plan, pairs, half_ref, sum_ref)

        for (segment, _), place in zip(roles, places):
            if segment is None:
                work(place)
            else:
                pl.when(lax.axis_index("seg") == segment)(functools.partial(work, place))
        flush(plan, sum_ref, message_refs)
        scalars(plan, refs[0][...], message_refs)

    return on_chip(body, ins, plan.messages(), work_space(plan))


def operator_step(plan, update, ins, state_shapes, lefts, rights, slots):
    n_in, n_state = len(ins), len(state_shapes)

    def body(*refs):
        left_refs = refs[n_in : n_in + len(lefts)]
        n = n_in + len(lefts)
        right_refs = refs[n : n + len(rights)]
        n += len(rights)
        slot_ref = refs[n]
        state_refs = refs[n + 1 : n + 1 + n_state]
        message_refs = refs[n + 1 + n_state : -3]
        low_ref, half_ref, sum_ref = refs[-3:]
        odd = in_odd_segment()

        def send(k, value):
            low_ref[pl.ds(k * plan.D, plan.D), :] = value.astype(BF16)

        row = packed_row(update(plan, refs[:n_in], state_refs, send), plan.D)
        sum_ref[...] = jnp.zeros(sum_ref.shape, F32)

        def all_of(place, right_ref):
            def at(k):
                return Block(place(k), (right_ref, k), (low_ref, k), (slot_ref, k))

            pairs = [(at(k), at(k + plan.H)) for k in range(plan.H)]
            multiply(plan, pairs, half_ref, sum_ref)

        def in_halves(k):
            return (left_refs[1], k) if k < plan.H else (left_refs[2], k - plan.H)

        if plan.shared:
            pl.when(odd)(lambda: all_of(lambda k: (left_refs[0], k), right_refs[0]))
            pl.when(jnp.logical_not(odd))(lambda: all_of(in_halves, right_refs[1]))
        else:
            all_of(lambda k: (left_refs[0], k), right_refs[0])

        flush(plan, sum_ref, message_refs)
        scalars(plan, row, message_refs)

    results = on_chip(
        body,
        list(ins) + list(lefts) + list(rights) + [slots],
        list(state_shapes) + plan.messages(),
        [VMEM((plan.T * plan.D, plan.D), BF16)] + work_space(plan),
    )
    return results[:n_state], results[n_state:]


def row_of(plan, values):
    across = lax.broadcasted_iota(jnp.int32, (8, plan.D), 1)
    row = jnp.zeros((8, plan.D), F32)
    for index, value in enumerate(values):
        row = row + jnp.where(across == index, value, 0.0)
    return row


def last_step(plan, ins, state_shapes):
    n_in = len(ins)

    def body(*refs):
        sums = update_last(plan, refs[:n_in], refs[n_in:-1])
        refs[-1][...] = row_of(plan, sums)

    row = jax.ShapeDtypeStruct((8, plan.D), F32)
    return on_chip(body, ins, list(state_shapes) + [row])


def outcome(plan, q, z, first, second, *sums):
    def body(q_ref, z_ref, first_ref, second_ref, *refs):
        added = functools.reduce(lambda x, y: x + y, [r[0:1, :] for r in refs[:-2]])
        residual_ref, coef_ref = refs[-2:]
        alpha, m = shift_of(plan, *[lane(added, i) for i in range(4)])
        residual_ref[...] = z_ref[...] - alpha * q_ref[...]
        values = [first_ref[0:1, 0:1], second_ref[0:1, 0:1], alpha]
        values += [first_ref[1:2, 0:1], second_ref[1:2, 0:1], jnp.sqrt(m)]
        coef_ref[...] = row_of(plan, values)[0:1, 0 : len(values)]

    row = jax.ShapeDtypeStruct((1, 6), F32)
    return on_chip(body, [q, z, first, second, *sums], [q, row])


def middle_a(plan, keep, got):
    rows = plan.a_rows

    def body(keep_ref, got_ref, *outs):
        end = pl.ds(plan.Z * rows, PAD)
        row = split_row(joined_row(keep_ref[end, :]) + joined_row(got_ref[end, :]), plan.D)
        for z, out in enumerate(outs):
            at = pl.ds(z * rows, rows)
            added = keep_ref[at, :].astype(F32) + got_ref[at, :].astype(F32)
            out[pl.ds(0, rows), :] = added.astype(BF16)
            out[pl.ds(rows, PAD), :] = row

    shape = jax.ShapeDtypeStruct((rows + PAD, plan.D), BF16)
    return on_chip(body, [keep, got], [shape] * plan.Z)


def middle_b(plan, parts):
    rows = plan.b_rows

    def body(*refs):
        for y, out in enumerate(refs[plan.Z :]):
            at = pl.ds(y * rows, rows)
            tiles = [p[at, :].astype(F32) for p in refs[: plan.Z]]
            out[...] = functools.reduce(lambda u, v: u + v, tiles).astype(out.dtype)

    shapes = [jax.ShapeDtypeStruct((rows, plan.D), d) for d in (F32, BF16)]
    return on_chip(body, parts, shapes)


def exchanged(plan, messages):
    keep, send, b_parts = messages[0], messages[1], messages[2:]
    others = range(plan.Z - 1, 0, -1)
    got = swapped(send, 1)
    b_got = [swapped(b_parts[z], 2 * z) for z in others]
    a_parts = middle_a(plan, keep, got)
    a_last = [swapped(a_parts[z], 2 * z) for z in others]
    b_keep, b_send = middle_b(plan, [b_parts[0]] + b_got)
    return [a_parts[0]] + a_last[::-1] + [b_keep, swapped(b_send, 1)]


def gathered(plan, arrived, dtype):
    def body(*refs):
        tile, _ = received_sums(plan, refs[:-1])
        for k in range(plan.T):
            refs[-1][pl.ds(k * plan.D, plan.D), :] = tile(k).astype(dtype)

    sums = jax.ShapeDtypeStruct((plan.T * plan.D, plan.D), dtype)
    return on_chip(body, arrived, [sums])[0]


PIECES = 4


def pieces_of(source, first, target, done, rows):
    piece = rows // PIECES
    return [
        pltpu.make_async_copy(
            source.at[pl.ds(first + i * piece, piece)], target.at[pl.ds(i * piece, piece)], done.at[i]
        )
        for i in range(PIECES)
    ]


def run(copies, after=None):
    for copy in copies:
        copy.start()
    if after is not None:
        after()
    for copy in copies:
        copy.wait()


def in_hbm(x):
    return pltpu.with_memory_space_constraint(x, pltpu.HBM)


def copying(sources, even, odd, rows):
    n = len(sources)

    def body(*refs):
        def one(choice):
            source, first = choice
            run(pieces_of(refs[source], first, refs[n], refs[n + 1], rows))

        pl.when(jnp.logical_not(in_odd_segment()))(lambda: one(even))
        pl.when(in_odd_segment())(lambda: one(odd))

    return pl.pallas_call(
        body,
        in_specs=[pl.BlockSpec(memory_space=pl.ANY)] * n,
        out_specs=pl.BlockSpec(memory_space=VMEM),
        out_shape=jax.ShapeDtypeStruct((rows, sources[0].shape[1]), sources[0].dtype),
        scratch_shapes=[pltpu.SemaphoreType.DMA((PIECES,))],
        compiler_params=pltpu.CompilerParams(vmem_limit_bytes=16 * 2**20),
    )(*[in_hbm(x) for x in sources])


def prepared(plan, start, rows, cols, feeds, left, right):
    every = right.shape[0]
    half = every // 2

    def body(start_ref, rows_ref, cols_ref, feed_ref, left_ref, right_ref, *outs):
        x_ref, low_ref, row_ref, slot_ref, last_low_ref, last_slot_ref = outs[:6]
        held_left_ref, held_right_ref, done = outs[6:]
        me = lax.axis_index("blk")

        def send(k, value):
            low_ref[pl.ds(k * plan.D, plan.D), :] = value.astype(BF16)
            if k >= plan.H:
                last_low_ref[pl.ds((k - plan.H) * plan.D, plan.D), :] = value.astype(BF16)

        def several(w, carry):
            for k in range(plan.T):
                slot = plan.slot(feed_ref[k, w], me)
                slot_ref[k * plan.W + w] = slot
                if k >= plan.H:
                    last_slot_ref[(k - plan.H) * plan.W + w] = slot
            return carry

        def compute():
            lax.fori_loop(0, plan.W, several, 0)
            sums = update_first(plan, (start_ref, rows_ref, cols_ref), (x_ref,), send)
            row_ref[...] = packed_row(sums, plan.D)

        def all_right():
            run(pieces_of(right_ref, 0, held_right_ref, done, every), compute)

        def last_left():
            run(pieces_of(left_ref, half, held_left_ref, done, half), compute)

        if plan.shared:
            pl.when(jnp.logical_not(in_odd_segment()))(all_right)
            pl.when(in_odd_segment())(last_left)
        else:
            all_right()

    chip = pl.BlockSpec(memory_space=VMEM)
    scalar = pl.BlockSpec(memory_space=SMEM)
    anywhere = pl.BlockSpec(memory_space=pl.ANY)
    last = plan.T - plan.H
    return pl.pallas_call(
        body,
        in_specs=[chip, scalar, scalar, scalar, anywhere, anywhere],
        out_specs=[chip, chip, chip, scalar, chip, scalar, chip, chip],
        out_shape=[
            jax.ShapeDtypeStruct(start.shape, F32),
            jax.ShapeDtypeStruct(start.shape, BF16),
            jax.ShapeDtypeStruct((PAD, plan.D), BF16),
            jax.ShapeDtypeStruct((plan.T * plan.W,), jnp.int32),
            jax.ShapeDtypeStruct((last * plan.D, plan.D), BF16),
            jax.ShapeDtypeStruct((last * plan.W,), jnp.int32),
            jax.ShapeDtypeStruct((half, plan.D), BF16),
            jax.ShapeDtypeStruct((every, plan.D), BF16),
        ],
        scratch_shapes=[pltpu.SemaphoreType.DMA((PIECES,))],
        compiler_params=pltpu.CompilerParams(vmem_limit_bytes=16 * 2**20),
        name="prepared",
    )(start, rows, cols, feeds, in_hbm(left), in_hbm(right))


def plain_start(plan, left, right, start, rows, cols, feeds):
    segments = range(1, lax.axis_size("seg"))
    arrived_left = handed(left, segments, 1)
    x, low, square, slots, _, _, _, held_right = prepared(
        plan, start, rows, cols, feeds, left, right
    )
    messages = first_step(plan, square, [(None, [arrived_left, held_right, low, slots])])
    return x, slots, [arrived_left], [held_right], exchanged(plan, messages)


def shared_start(plan, left, right, start, rows, cols, feeds):
    every = right.shape[0]
    half = every // 2
    helped, helper = plan.helped, plan.helped - 1

    sent = copying([left, right], (1, half), (0, 0), half)
    crossed = lax.ppermute(sent, "seg", [(helper, helped), (helped, helper)])
    own_side = copying([left, right], (0, 0), (1, 0), every)
    partner = swapped(own_side, 1, "seg")
    x, low, square, slots, last_low, last_slots, held_left, held_right = prepared(
        plan, start, rows, cols, feeds, left, right
    )
    other_low = handed(last_low, [helper], -1)
    other_slots = handed(last_slots, [helper], -1)
    partner_low = handed(low, [helper - 1], -1)
    partner_slots = handed(slots, [helper - 1], -1)
    left_last = handed(held_left, [helped], 1)

    roles = [
        (helper - 1, [own_side, partner, partner_low, partner_slots]),
        (helper, [held_left, crossed, other_low, other_slots]),
        (helped, [crossed, held_right, low, slots]),
        (helped + 1, [partner, own_side, low, slots]),
    ]
    messages = first_step(plan, square, roles)
    arrived = exchanged(plan, messages)
    sums = gathered(plan, arrived, BF16)
    got = handed(sums, [helper, helped], 1)
    lefts, rights = [partner, crossed, left_last], [own_side, held_right]
    return x, slots, lefts, rights, [got] + arrived


def local(
    start_vector,
    left_environment,
    right_environment,
    block_energy,
    sector_rows,
    sector_cols,
    feed_block,
):
    T, W, D = left_environment.shape[1:4]
    plan = Plan(T, W, D, lax.axis_size("blk"), lax.axis_size("seg"))
    left = left_environment.reshape(T * W * D, D)
    right = right_environment.reshape(T * W * D, D)
    rows, cols, energy = sector_rows[0], sector_cols[0], block_energy[0]
    vector = jax.ShapeDtypeStruct((T * D, D), F32)
    row = jax.ShapeDtypeStruct((8, D), F32)
    start = start_vector.reshape(T * D, D)
    first = shared_start if plan.shared else plain_start
    x, slots, lefts, rights, arrived = first(
        plan, left, right, start, rows, cols, feed_block[0]
    )
    (q0, h0, known), messages = operator_step(
        plan,
        update_second,
        [x, rows, cols, energy] + arrived,
        [vector, vector, row],
        lefts,
        rights,
        slots,
    )
    arrived = exchanged(plan, messages)
    (q1, h1, z1, first), messages = operator_step(
        plan,
        update_third,
        [q0, h0, known, rows, cols, energy] + arrived,
        [vector, vector, vector, row],
        lefts,
        rights,
        slots,
    )
    arrived = exchanged(plan, messages)
    q2, z2, second, sums = last_step(
        plan, [q1, h1, z1, rows, cols, energy] + arrived, [vector, vector, row]
    )
    mask = 1
    while 2 * mask < plan.B:
        sums = sums + swapped(sums, mask)
        mask *= 2
    last = swapped(sums, mask)
    residual, coefficients = outcome(plan, q2, z2, first, second, sums, last)
    return (coefficients, residual.reshape(1, T, D, D))


def solution(mesh):
    return jax.shard_map(
        local,
        mesh=mesh,
        in_specs=(
            P("seg", "blk", None, None),
            P("seg", "blk", None, None, None),
            P("seg", "blk", None, None, None),
            P("seg", "blk"),
            P("seg", "blk"),
            P("seg", "blk"),
            P("seg", "blk", None),
        ),
        out_specs=(P("seg", None), P("seg", "blk", None, None)),
        check_vma=False,
    )
```

```python
import functools

import jax
import jax.numpy as jnp
from jax import lax
from jax.experimental import pallas as pl
from jax.experimental.pallas import tpu as pltpu
from jax.sharding import PartitionSpec as P


epsilon = 1e-06
F32 = jnp.float32
BF16 = jnp.bfloat16
PAD = 16
VMEM = pltpu.VMEM
SMEM = pltpu.SMEM


def handed(block, targets, distance):
    return lax.ppermute(block, "seg", [(s - distance, s) for s in targets])


def swapped(block, mask, axis="blk"):
    return lax.ppermute(block, axis, [(i, i ^ mask) for i in range(lax.axis_size(axis))])


class Plan:
    def __init__(self, tiles, channels, tile, blk, segments):
        self.T, self.W, self.D, self.B = tiles, channels, tile, blk
        self.Z = blk // 2
        self.Ta = tiles // 2
        self.Tb = tiles - self.Ta
        self.entries = float(tiles * blk * tile * tile)
        self.n = tiles * blk
        self.a_rows = self.Ta * tile
        self.b_rows = self.Tb * tile
        self.H = tiles // 2
        self.shared = segments == 4
        self.helped = 2
        self.group = channels

    def slot(self, feed, me):
        tiles = jnp.int32(self.T)
        device, tile = lax.div(feed, tiles), lax.rem(feed, tiles)
        relative = device ^ me
        zr, yr = relative >> 1, relative & 1
        a = (yr * self.Z + zr) * self.Ta + tile
        b = self.B * self.Ta + (zr * 2 + yr) * self.Tb + (tile - self.Ta)
        return jnp.where(feed >= self.n, self.n, jnp.where(tile < self.Ta, a, b))

    def works_for_next(self):
        return lax.axis_index("seg") < self.helped

    def messages(self):
        a = jax.ShapeDtypeStruct((self.Z * self.a_rows + PAD, self.D), BF16)
        b = jax.ShapeDtypeStruct((2 * self.b_rows, self.D), BF16)
        return [a, a] + [b] * self.Z


def packed_row(scalars, tile):
    lane = lax.broadcasted_iota(jnp.int32, (1, tile), 1)
    row = jnp.zeros((1, tile), F32)
    for index, value in enumerate(scalars):
        row = row + jnp.where(lane == index, value, 0.0)
    return split_row(row, tile)


def split_row(row, tile):
    high = row.astype(BF16).astype(F32)
    middle = (row - high).astype(BF16).astype(F32)
    low = row - high - middle
    at = lax.broadcasted_iota(jnp.int32, (PAD, tile), 0)
    rows = jnp.where(at == 0, high, jnp.where(at == 1, middle, jnp.where(at == 2, low, 0.0)))
    return rows.astype(BF16)


def joined_row(rows):
    rows = rows.astype(F32)
    return rows[0:1] + rows[1:2] + rows[2:3]


def folded(value):
    return jnp.sum(value.reshape(value.shape[0] // 8, 8, value.shape[1]), axis=0)


def total(value):
    return jnp.sum(value, keepdims=True).reshape(1, 1)


def live_mask(plan, rows, cols, k):
    down = lax.broadcasted_iota(jnp.int32, (plan.D, plan.D), 0)
    across = lax.broadcasted_iota(jnp.int32, (plan.D, plan.D), 1)
    return jnp.logical_and(down < rows[k], across < cols[k])


def received_sums(plan, arrived):
    a_parts, b_parts = arrived[: plan.Z], arrived[plan.Z :]

    def tile(k):
        parts, i = (a_parts, k) if k < plan.Ta else (b_parts, k - plan.Ta)
        at = pl.ds(i * plan.D, plan.D)
        return functools.reduce(lambda x, y: x + y, [p[at, :].astype(F32) for p in parts])

    level = [joined_row(p[pl.ds(plan.a_rows, PAD), :]) for p in a_parts]
    while len(level) > 1:
        level = [level[i] + level[i + 1] for i in range(0, len(level), 2)]
    return tile, level[0]


def lane(row, index):
    return row[:, index : index + 1]


def shift_of(plan, a, b, d, e):
    alpha = a / plan.entries
    m = jnp.maximum(b - 2.0 * alpha * d + alpha * alpha * e, 0.0) / plan.entries
    return alpha, m


def update_first(plan, ins, outs, send):
    (start, rows, cols), (x_out,) = ins, outs
    norm = jnp.zeros((8, plan.D), F32)
    for k in range(plan.T):
        at = pl.ds(k * plan.D, plan.D)
        x = jnp.where(live_mask(plan, rows, cols, k), start[at, :].astype(F32), 0.0)
        x_out[at, :] = x
        send(k, x)
        norm = norm + folded(x * x)
    return [total(norm)]


def update_second(plan, ins, outs, send):
    (x_in, rows, cols, energy), arrived = ins[:4], ins[4:]
    q_out, h_out, known_out = outs
    if plan.shared:
        handed_on, arrived = arrived[0], arrived[1:]
    own_tile, row = received_sums(plan, arrived)

    def tile(k):
        if not plan.shared:
            return own_tile(k)
        kept = jnp.where(plan.works_for_next(), 0.0, own_tile(k))
        return kept + handed_on[pl.ds(k * plan.D, plan.D), :].astype(F32)

    square = lane(row, 0)
    scale = lax.rsqrt(square / plan.entries + epsilon)
    known_out[...] = jnp.broadcast_to(scale * scale * square, known_out.shape)
    a = b = jnp.zeros((8, plan.D), F32)
    for k in range(plan.T):
        at = pl.ds(k * plan.D, plan.D)
        x = x_in[at, :]
        image = jnp.where(live_mask(plan, rows, cols, k), tile(k), 0.0) + energy[k] * x
        q = scale * x
        h = scale * image
        q_out[at, :] = q
        h_out[at, :] = h
        send(k, h)
        a = a + folded(q * h)
        b = b + folded(h * h)
    return [total(a), total(b)]


def update_third(plan, ins, outs, send):
    (q_in, h_in, known, rows, cols, energy), arrived = ins[:6], ins[6:]
    q_out, h_out, z_out, coef_out = outs
    tile, row = received_sums(plan, arrived)
    a, b = lane(row, 0), lane(row, 1)
    alpha, m = shift_of(plan, a, b, a, known[0:1, 0:1])
    beta, scale = jnp.sqrt(m), lax.rsqrt(m + epsilon)
    coef_out[0:1, :] = jnp.broadcast_to(alpha, (1, plan.D))
    coef_out[1:2, :] = jnp.broadcast_to(beta, (1, plan.D))
    sums = [jnp.zeros((8, plan.D), F32)] * 4
    for k in range(plan.T):
        at = pl.ds(k * plan.D, plan.D)
        q0, h0 = q_in[at, :], h_in[at, :]
        image = jnp.where(live_mask(plan, rows, cols, k), tile(k), 0.0) + energy[k] * h0
        q = scale * (h0 - alpha * q0)
        h = scale * (image - alpha * h0)
        z = h - beta * q0
        q_out[at, :] = q
        h_out[at, :] = h
        z_out[at, :] = z
        send(k, z)
        sums = [s + folded(p) for s, p in zip(sums, (q * h, z * z, z * q, q * q))]
    return [total(s) for s in sums]


def update_last(plan, ins, outs):
    (q_in, h_in, z_in, rows, cols, energy), arrived = ins[:6], ins[6:]
    q_out, z_out, coef_out = outs
    tile, row = received_sums(plan, arrived)
    alpha, m = shift_of(plan, *[lane(row, i) for i in range(4)])
    beta, scale = jnp.sqrt(m), lax.rsqrt(m + epsilon)
    coef_out[0:1, :] = jnp.broadcast_to(alpha, (1, plan.D))
    coef_out[1:2, :] = jnp.broadcast_to(beta, (1, plan.D))
    sums = [jnp.zeros((8, plan.D), F32)] * 4
    for k in range(plan.T):
        at = pl.ds(k * plan.D, plan.D)
        q1, h1, z1 = q_in[at, :], h_in[at, :], z_in[at, :]
        image = jnp.where(live_mask(plan, rows, cols, k), tile(k), 0.0) + energy[k] * z1
        q = scale * (z1 - alpha * q1)
        h = scale * (image - alpha * h1)
        z = h - beta * q1
        q_out[at, :] = q
        z_out[at, :] = z
        sums = [s + folded(p) for s, p in zip(sums, (q * h, z * z, z * q, q * q))]
    return [total(s) for s in sums]


def on_chip(body, ins, outs, scratch=()):
    spaces = [SMEM if len(x.shape) == 1 else VMEM for x in ins]
    return pl.pallas_call(
        body,
        in_specs=[pl.BlockSpec(memory_space=s) for s in spaces],
        out_specs=[pl.BlockSpec(memory_space=VMEM)] * len(outs),
        out_shape=list(outs),
        scratch_shapes=list(scratch),
        compiler_params=pltpu.CompilerParams(vmem_limit_bytes=16 * 2**20),
    )(*ins)


def in_odd_segment():
    return lax.axis_index("seg") % 2 == 1


class Block:
    def __init__(self, left, right, low, slots):
        self.left, self.right, self.low, self.slots = left, right, low, slots


def multiply(plan, pairs, half_ref, sum_ref):
    D, W, group = plan.D, plan.W, plan.group
    none = jnp.zeros((D, D), BF16)

    def rows(place, first, count):
        ref, block = place
        return ref[pl.ds(pl.multiple_of((block * W + first) * D, D), count * D), :]

    def several(step, carry):
        first = step * group
        for pair in pairs:
            v = [b.low[0][pl.ds(b.low[1] * D, D), :] for b in pair]
            both = jnp.concatenate(
                [jnp.concatenate([v[0], none], 1), jnp.concatenate([none, v[1]], 1)], 0
            )
            tiles = [rows(b.left, first, group) for b in pair]
            half_ref[...] = jnp.dot(
                jnp.concatenate(tiles, 1), both, preferred_element_type=F32
            ).astype(BF16)
            for w in range(group):
                r = [rows(b.right, first + w, 1) for b in pair]
                both = jnp.concatenate(
                    [jnp.concatenate([r[0], none], 1), jnp.concatenate([none, r[1]], 1)], 0
                )
                product = jnp.dot(
                    half_ref[pl.ds(w * D, D), :], both, preferred_element_type=F32
                )
                for side, b in enumerate(pair):
                    ref, block = b.slots
                    at = pl.ds(pl.multiple_of(ref[block * W + first + w] * D, D), D)
                    sum_ref[at, :] += product[:, side * D : (side + 1) * D]
        return carry

    lax.fori_loop(0, W // group, several, 0)


def scalars(plan, row, message_refs):
    for ref in message_refs[:2]:
        ref[pl.ds(plan.Z * plan.a_rows, PAD), :] = row


def flush(plan, sum_ref, message_refs):
    first = 0
    for ref in message_refs:
        rows = ref.shape[0] // plan.D * plan.D
        ref[pl.ds(0, rows), :] = sum_ref[pl.ds(first, rows), :].astype(BF16)
        first += rows


def work_space(plan):
    return [
        VMEM((plan.group * plan.D, 2 * plan.D), BF16),
        VMEM(((plan.n + 1) * plan.D, plan.D), F32),
    ]


def first_step(plan, row, roles):
    ins, places = [row], []
    for _, arrays in roles:
        for array in arrays:
            if all(array is not known for known in ins):
                ins.append(array)
        places.append([next(i for i, a in enumerate(ins) if a is array) for array in arrays])

    def body(*refs):
        n = len(ins)
        message_refs, (half_ref, sum_ref) = refs[n:-2], refs[-2:]

        def work(place):
            def at(k):
                return Block(*[(refs[i], k) for i in place])

            blocks = refs[place[0]].shape[0] // (plan.W * plan.D)
            sum_ref[...] = jnp.zeros(sum_ref.shape, F32)
            pairs = [(at(k), at(k + blocks // 2)) for k in range(blocks // 2)]
            multiply(plan, pairs, half_ref, sum_ref)

        for (segment, _), place in zip(roles, places):
            if segment is None:
                work(place)
            else:
                pl.when(lax.axis_index("seg") == segment)(functools.partial(work, place))
        flush(plan, sum_ref, message_refs)
        scalars(plan, refs[0][...], message_refs)

    return on_chip(body, ins, plan.messages(), work_space(plan))


def operator_step(plan, update, ins, state_shapes, lefts, rights, slots):
    n_in, n_state = len(ins), len(state_shapes)

    def body(*refs):
        left_refs = refs[n_in : n_in + len(lefts)]
        n = n_in + len(lefts)
        right_refs = refs[n : n + len(rights)]
        n += len(rights)
        slot_ref = refs[n]
        state_refs = refs[n + 1 : n + 1 + n_state]
        message_refs = refs[n + 1 + n_state : -3]
        low_ref, half_ref, sum_ref = refs[-3:]
        odd = in_odd_segment()

        def send(k, value):
            low_ref[pl.ds(k * plan.D, plan.D), :] = value.astype(BF16)

        row = packed_row(update(plan, refs[:n_in], state_refs, send), plan.D)
        sum_ref[...] = jnp.zeros(sum_ref.shape, F32)

        def all_of(place, right_ref):
            def at(k):
                return Block(place(k), (right_ref, k), (low_ref, k), (slot_ref, k))

            pairs = [(at(k), at(k + plan.H)) for k in range(plan.H)]
            multiply(plan, pairs, half_ref, sum_ref)

        def in_halves(k):
            return (left_refs[1], k) if k < plan.H else (left_refs[2], k - plan.H)

        if plan.shared:
            pl.when(odd)(lambda: all_of(lambda k: (left_refs[0], k), right_refs[0]))
            pl.when(jnp.logical_not(odd))(lambda: all_of(in_halves, right_refs[1]))
        else:
            all_of(lambda k: (left_refs[0], k), right_refs[0])

        flush(plan, sum_ref, message_refs)
        scalars(plan, row, message_refs)

    results = on_chip(
        body,
        list(ins) + list(lefts) + list(rights) + [slots],
        list(state_shapes) + plan.messages(),
        [VMEM((plan.T * plan.D, plan.D), BF16)] + work_space(plan),
    )
    return results[:n_state], results[n_state:]


def row_of(plan, values):
    across = lax.broadcasted_iota(jnp.int32, (8, plan.D), 1)
    row = jnp.zeros((8, plan.D), F32)
    for index, value in enumerate(values):
        row = row + jnp.where(across == index, value, 0.0)
    return row


def last_step(plan, ins, state_shapes):
    n_in = len(ins)

    def body(*refs):
        sums = update_last(plan, refs[:n_in], refs[n_in:-1])
        refs[-1][...] = row_of(plan, sums)

    row = jax.ShapeDtypeStruct((8, plan.D), F32)
    return on_chip(body, ins, list(state_shapes) + [row])


def outcome(plan, q, z, first, second, *sums):
    def body(q_ref, z_ref, first_ref, second_ref, *refs):
        added = functools.reduce(lambda x, y: x + y, [r[0:1, :] for r in refs[:-2]])
        residual_ref, coef_ref = refs[-2:]
        alpha, m = shift_of(plan, *[lane(added, i) for i in range(4)])
        residual_ref[...] = z_ref[...] - alpha * q_ref[...]
        values = [first_ref[0:1, 0:1], second_ref[0:1, 0:1], alpha]
        values += [first_ref[1:2, 0:1], second_ref[1:2, 0:1], jnp.sqrt(m)]
        coef_ref[...] = row_of(plan, values)[0:1, 0 : len(values)]

    row = jax.ShapeDtypeStruct((1, 6), F32)
    return on_chip(body, [q, z, first, second, *sums], [q, row])


def middle_a(plan, keep, got):
    rows = plan.a_rows

    def body(keep_ref, got_ref, *outs):
        end = pl.ds(plan.Z * rows, PAD)
        row = split_row(joined_row(keep_ref[end, :]) + joined_row(got_ref[end, :]), plan.D)
        for z, out in enumerate(outs):
            at = pl.ds(z * rows, rows)
            added = keep_ref[at, :].astype(F32) + got_ref[at, :].astype(F32)
            out[pl.ds(0, rows), :] = added.astype(BF16)
            out[pl.ds(rows, PAD), :] = row

    shape = jax.ShapeDtypeStruct((rows + PAD, plan.D), BF16)
    return on_chip(body, [keep, got], [shape] * plan.Z)


def middle_b(plan, parts):
    rows = plan.b_rows

    def body(*refs):
        for y, out in enumerate(refs[plan.Z :]):
            at = pl.ds(y * rows, rows)
            tiles = [p[at, :].astype(F32) for p in refs[: plan.Z]]
            out[...] = functools.reduce(lambda u, v: u + v, tiles).astype(out.dtype)

    shapes = [jax.ShapeDtypeStruct((rows, plan.D), d) for d in (F32, BF16)]
    return on_chip(body, parts, shapes)


def exchanged(plan, messages):
    keep, send, b_parts = messages[0], messages[1], messages[2:]
    others = range(plan.Z - 1, 0, -1)
    got = swapped(send, 1)
    b_got = [swapped(b_parts[z], 2 * z) for z in others]
    a_parts = middle_a(plan, keep, got)
    a_last = [swapped(a_parts[z], 2 * z) for z in others]
    b_keep, b_send = middle_b(plan, [b_parts[0]] + b_got)
    b_last = swapped(b_send, 1)
    return [a_parts[0]] + a_last[::-1] + [b_keep, b_last]


def gathered(plan, arrived, dtype):
    def body(*refs):
        tile, _ = received_sums(plan, refs[:-1])
        for k in range(plan.T):
            refs[-1][pl.ds(k * plan.D, plan.D), :] = tile(k).astype(dtype)

    sums = jax.ShapeDtypeStruct((plan.T * plan.D, plan.D), dtype)
    return on_chip(body, arrived, [sums])[0]


PIECES = 4


def pieces_of(source, first, target, done, rows):
    piece = rows // PIECES
    return [
        pltpu.make_async_copy(
            source.at[pl.ds(first + i * piece, piece)], target.at[pl.ds(i * piece, piece)], done.at[i]
        )
        for i in range(PIECES)
    ]


def run(copies, after=None):
    for copy in copies:
        copy.start()
    if after is not None:
        after()
    for copy in copies:
        copy.wait()


def in_hbm(x):
    return pltpu.with_memory_space_constraint(x, pltpu.HBM)


def copying(sources, even, odd, rows):
    n = len(sources)

    def body(*refs):
        def one(choice):
            source, first = choice
            run(pieces_of(refs[source], first, refs[n], refs[n + 1], rows))

        pl.when(jnp.logical_not(in_odd_segment()))(lambda: one(even))
        pl.when(in_odd_segment())(lambda: one(odd))

    return pl.pallas_call(
        body,
        in_specs=[pl.BlockSpec(memory_space=pl.ANY)] * n,
        out_specs=pl.BlockSpec(memory_space=VMEM),
        out_shape=jax.ShapeDtypeStruct((rows, sources[0].shape[1]), sources[0].dtype),
        scratch_shapes=[pltpu.SemaphoreType.DMA((PIECES,))],
        compiler_params=pltpu.CompilerParams(vmem_limit_bytes=16 * 2**20),
    )(*[in_hbm(x) for x in sources])


def prepared(plan, start, rows, cols, feeds, left, right):
    every = right.shape[0]
    half = every // 2

    def body(start_ref, rows_ref, cols_ref, feed_ref, left_ref, right_ref, *outs):
        x_ref, low_ref, row_ref, slot_ref, last_low_ref, last_slot_ref = outs[:6]
        held_left_ref, held_right_ref, done = outs[6:]
        me = lax.axis_index("blk")

        def send(k, value):
            low_ref[pl.ds(k * plan.D, plan.D), :] = value.astype(BF16)
            if k >= plan.H:
                last_low_ref[pl.ds((k - plan.H) * plan.D, plan.D), :] = value.astype(BF16)

        def several(w, carry):
            for k in range(plan.T):
                slot = plan.slot(feed_ref[k, w], me)
                slot_ref[k * plan.W + w] = slot
                if k >= plan.H:
                    last_slot_ref[(k - plan.H) * plan.W + w] = slot
            return carry

        def compute():
            lax.fori_loop(0, plan.W, several, 0)
            sums = update_first(plan, (start_ref, rows_ref, cols_ref), (x_ref,), send)
            row_ref[...] = packed_row(sums, plan.D)

        def all_right():
            run(pieces_of(right_ref, 0, held_right_ref, done, every), compute)

        def last_left():
            run(pieces_of(left_ref, half, held_left_ref, done, half), compute)

        if plan.shared:
            pl.when(jnp.logical_not(in_odd_segment()))(all_right)
            pl.when(in_odd_segment())(last_left)
        else:
            all_right()

    chip = pl.BlockSpec(memory_space=VMEM)
    scalar = pl.BlockSpec(memory_space=SMEM)
    anywhere = pl.BlockSpec(memory_space=pl.ANY)
    last = plan.T - plan.H
    return pl.pallas_call(
        body,
        in_specs=[chip, scalar, scalar, scalar, anywhere, anywhere],
        out_specs=[chip, chip, chip, scalar, chip, scalar, chip, chip],
        out_shape=[
            jax.ShapeDtypeStruct(start.shape, F32),
            jax.ShapeDtypeStruct(start.shape, BF16),
            jax.ShapeDtypeStruct((PAD, plan.D), BF16),
            jax.ShapeDtypeStruct((plan.T * plan.W,), jnp.int32),
            jax.ShapeDtypeStruct((last * plan.D, plan.D), BF16),
            jax.ShapeDtypeStruct((last * plan.W,), jnp.int32),
            jax.ShapeDtypeStruct((half, plan.D), BF16),
            jax.ShapeDtypeStruct((every, plan.D), BF16),
        ],
        scratch_shapes=[pltpu.SemaphoreType.DMA((PIECES,))],
        compiler_params=pltpu.CompilerParams(vmem_limit_bytes=16 * 2**20),
        name="prepared",
    )(start, rows, cols, feeds, in_hbm(left), in_hbm(right))


def plain_start(plan, left, right, start, rows, cols, feeds):
    segments = range(1, lax.axis_size("seg"))
    arrived_left = handed(left, segments, 1)
    x, low, square, slots, _, _, _, held_right = prepared(
        plan, start, rows, cols, feeds, left, right
    )
    messages = first_step(plan, square, [(None, [arrived_left, held_right, low, slots])])
    return x, slots, [arrived_left], [held_right], exchanged(plan, messages)


def shared_start(plan, left, right, start, rows, cols, feeds):
    every = right.shape[0]
    half = every // 2
    helped, helper = plan.helped, plan.helped - 1

    sent = copying([left, right], (1, half), (0, 0), half)
    crossed = lax.ppermute(sent, "seg", [(helper, helped), (helped, helper)])
    own_side = copying([left, right], (0, 0), (1, 0), every)
    partner = swapped(own_side, 1, "seg")
    x, low, square, slots, last_low, last_slots, held_left, held_right = prepared(
        plan, start, rows, cols, feeds, left, right
    )
    other_low = handed(last_low, [helper], -1)
    other_slots = handed(last_slots, [helper], -1)
    partner_low = handed(low, [helper - 1], -1)
    partner_slots = handed(slots, [helper - 1], -1)
    left_last = handed(held_left, [helped], 1)

    roles = [
        (helper - 1, [own_side, partner, partner_low, partner_slots]),
        (helper, [held_left, crossed, other_low, other_slots]),
        (helped, [crossed, held_right, low, slots]),
        (helped + 1, [partner, own_side, low, slots]),
    ]
    messages = first_step(plan, square, roles)
    arrived = exchanged(plan, messages)
    sums = gathered(plan, arrived, BF16)
    got = handed(sums, [helper, helped], 1)
    lefts, rights = [partner, crossed, left_last], [own_side, held_right]
    return x, slots, lefts, rights, [got] + arrived


def local(
    start_vector,
    left_environment,
    right_environment,
    block_energy,
    sector_rows,
    sector_cols,
    feed_block,
):
    T, W, D = left_environment.shape[1:4]
    plan = Plan(T, W, D, lax.axis_size("blk"), lax.axis_size("seg"))
    left = left_environment.reshape(T * W * D, D)
    right = right_environment.reshape(T * W * D, D)
    rows, cols, energy = sector_rows[0], sector_cols[0], block_energy[0]
    vector = jax.ShapeDtypeStruct((T * D, D), F32)
    row = jax.ShapeDtypeStruct((8, D), F32)
    start = start_vector.reshape(T * D, D)
    first = shared_start if plan.shared else plain_start
    x, slots, lefts, rights, arrived = first(
        plan, left, right, start, rows, cols, feed_block[0]
    )
    (q0, h0, known), messages = operator_step(
        plan,
        update_second,
        [x, rows, cols, energy] + arrived,
        [vector, vector, row],
        lefts,
        rights,
        slots,
    )
    arrived = exchanged(plan, messages)
    (q1, h1, z1, first), messages = operator_step(
        plan,
        update_third,
        [q0, h0, known, rows, cols, energy] + arrived,
        [vector, vector, vector, row],
        lefts,
        rights,
        slots,
    )
    arrived = exchanged(plan, messages)
    q2, z2, second, sums = last_step(
        plan, [q1, h1, z1, rows, cols, energy] + arrived, [vector, vector, row]
    )
    mask = 1
    while 2 * mask < plan.B:
        sums = sums + swapped(sums, mask)
        mask *= 2
    last = swapped(sums, mask)
    residual, coefficients = outcome(plan, q2, z2, first, second, sums, last)
    return (coefficients, residual.reshape(1, T, D, D))


def solution(mesh):
    return jax.shard_map(
        local,
        mesh=mesh,
        in_specs=(
            P("seg", "blk", None, None),
            P("seg", "blk", None, None, None),
            P("seg", "blk", None, None, None),
            P("seg", "blk"),
            P("seg", "blk"),
            P("seg", "blk"),
            P("seg", "blk", None),
        ),
        out_specs=(P("seg", None), P("seg", "blk", None, None)),
        check_vma=False,
    )
```

```python
import functools

import jax
import jax.numpy as jnp
from jax import lax
from jax.experimental import pallas as pl
from jax.experimental.pallas import tpu as pltpu
from jax.sharding import PartitionSpec as P


epsilon = 1e-06
F32 = jnp.float32
BF16 = jnp.bfloat16
PAD = 16
VMEM = pltpu.VMEM
SMEM = pltpu.SMEM


def handed(block, targets, distance):
    return lax.ppermute(block, "seg", [(s - distance, s) for s in targets])


def swapped(block, mask, axis="blk"):
    return lax.ppermute(block, axis, [(i, i ^ mask) for i in range(lax.axis_size(axis))])


def swapped_but_first(block, mask):
    blk, segments = lax.axis_size("blk"), lax.axis_size("seg")
    route = [
        (s * blk + i, s * blk + (i ^ (mask if s else 1))) for s in range(segments) for i in range(blk)
    ]
    return lax.ppermute(block, ("seg", "blk"), route)


class Plan:
    def __init__(self, tiles, channels, tile, blk, segments):
        self.T, self.W, self.D, self.B = tiles, channels, tile, blk
        self.Z = blk // 2
        self.Ta = tiles // 2
        self.Tb = tiles - self.Ta
        self.entries = float(tiles * blk * tile * tile)
        self.n = tiles * blk
        self.a_rows = self.Ta * tile
        self.b_rows = self.Tb * tile
        self.H = tiles // 2
        self.shared = segments == 4
        self.helped = 2
        self.group = next(
            c for c in range(max(1, channels // 2), 0, -1) if channels % c == 0
        )

    def slot(self, feed, me):
        tiles = jnp.int32(self.T)
        device, tile = lax.div(feed, tiles), lax.rem(feed, tiles)
        relative = device ^ me
        zr, yr = relative >> 1, relative & 1
        a = (yr * self.Z + zr) * self.Ta + tile
        b = self.B * self.Ta + (zr * 2 + yr) * self.Tb + (tile - self.Ta)
        return jnp.where(feed >= self.n, self.n, jnp.where(tile < self.Ta, a, b))

    def works_for_next(self):
        return lax.axis_index("seg") < self.helped

    def messages(self):
        a = jax.ShapeDtypeStruct((self.Z * self.a_rows + PAD, self.D), BF16)
        b = jax.ShapeDtypeStruct((2 * self.b_rows, self.D), BF16)
        return [a, a] + [b] * self.Z


def packed_row(scalars, tile):
    lane = lax.broadcasted_iota(jnp.int32, (1, tile), 1)
    row = jnp.zeros((1, tile), F32)
    for index, value in enumerate(scalars):
        row = row + jnp.where(lane == index, value, 0.0)
    return split_row(row, tile)


def split_row(row, tile):
    high = row.astype(BF16).astype(F32)
    middle = (row - high).astype(BF16).astype(F32)
    low = row - high - middle
    at = lax.broadcasted_iota(jnp.int32, (PAD, tile), 0)
    rows = jnp.where(at == 0, high, jnp.where(at == 1, middle, jnp.where(at == 2, low, 0.0)))
    return rows.astype(BF16)


def joined_row(rows):
    rows = rows.astype(F32)
    return rows[0:1] + rows[1:2] + rows[2:3]


def folded(value):
    return jnp.sum(value.reshape(value.shape[0] // 8, 8, value.shape[1]), axis=0)


def total(value):
    return jnp.sum(value, keepdims=True).reshape(1, 1)


def live_mask(plan, rows, cols, k):
    down = lax.broadcasted_iota(jnp.int32, (plan.D, plan.D), 0)
    across = lax.broadcasted_iota(jnp.int32, (plan.D, plan.D), 1)
    return jnp.logical_and(down < rows[k], across < cols[k])


def received_sums(plan, arrived):
    a_parts, b_parts = arrived[: plan.Z], arrived[plan.Z :]

    def tile(k):
        parts, i = (a_parts, k) if k < plan.Ta else (b_parts, k - plan.Ta)
        at = pl.ds(i * plan.D, plan.D)
        return functools.reduce(lambda x, y: x + y, [p[at, :].astype(F32) for p in parts])

    level = [joined_row(p[pl.ds(plan.a_rows, PAD), :]) for p in a_parts]
    while len(level) > 1:
        level = [level[i] + level[i + 1] for i in range(0, len(level), 2)]
    return tile, level[0]


def lane(row, index):
    return row[:, index : index + 1]


def shift_of(plan, a, b, d, e):
    alpha = a / plan.entries
    m = jnp.maximum(b - 2.0 * alpha * d + alpha * alpha * e, 0.0) / plan.entries
    return alpha, m


def update_first(plan, ins, outs, send):
    (start, rows, cols), (x_out,) = ins, outs
    norm = jnp.zeros((8, plan.D), F32)
    for k in range(plan.T):
        at = pl.ds(k * plan.D, plan.D)
        x = jnp.where(live_mask(plan, rows, cols, k), start[at, :].astype(F32), 0.0)
        x_out[at, :] = x
        send(k, x)
        norm = norm + folded(x * x)
    return [total(norm)]


def update_second(plan, ins, outs, send):
    (x_in, rows, cols, energy), arrived = ins[:4], ins[4:]
    q_out, h_out, known_out = outs
    if plan.shared:
        handed_on, arrived = arrived[0], arrived[1:]
    own_tile, row = received_sums(plan, arrived)

    def tile(k):
        if not plan.shared:
            return own_tile(k)
        kept = jnp.where(plan.works_for_next(), 0.0, own_tile(k))
        return kept + handed_on[pl.ds(k * plan.D, plan.D), :].astype(F32)

    square = lane(row, 0)
    scale = lax.rsqrt(square / plan.entries + epsilon)
    known_out[...] = jnp.broadcast_to(scale * scale * square, known_out.shape)
    a = b = jnp.zeros((8, plan.D), F32)
    for k in range(plan.T):
        at = pl.ds(k * plan.D, plan.D)
        x = x_in[at, :]
        image = jnp.where(live_mask(plan, rows, cols, k), tile(k), 0.0) + energy[k] * x
        q = scale * x
        h = scale * image
        q_out[at, :] = q
        h_out[at, :] = h
        send(k, h)
        a = a + folded(q * h)
        b = b + folded(h * h)
    return [total(a), total(b)]


def update_third(plan, ins, outs, send):
    (q_in, h_in, known, rows, cols, energy), arrived = ins[:6], ins[6:]
    q_out, h_out, z_out, coef_out = outs
    tile, row = received_sums(plan, arrived)
    a, b = lane(row, 0), lane(row, 1)
    alpha, m = shift_of(plan, a, b, a, known[0:1, 0:1])
    beta, scale = jnp.sqrt(m), lax.rsqrt(m + epsilon)
    coef_out[0:1, :] = jnp.broadcast_to(alpha, (1, plan.D))
    coef_out[1:2, :] = jnp.broadcast_to(beta, (1, plan.D))
    sums = [jnp.zeros((8, plan.D), F32)] * 4
    for k in range(plan.T):
        at = pl.ds(k * plan.D, plan.D)
        q0, h0 = q_in[at, :], h_in[at, :]
        image = jnp.where(live_mask(plan, rows, cols, k), tile(k), 0.0) + energy[k] * h0
        q = scale * (h0 - alpha * q0)
        h = scale * (image - alpha * h0)
        z = h - beta * q0
        q_out[at, :] = q
        h_out[at, :] = h
        z_out[at, :] = z
        send(k, z)
        sums = [s + folded(p) for s, p in zip(sums, (q * h, z * z, z * q, q * q))]
    return [total(s) for s in sums]


def update_last(plan, ins, outs):
    (q_in, h_in, z_in, rows, cols, energy), arrived = ins[:6], ins[6:]
    q_out, z_out, coef_out = outs
    tile, row = received_sums(plan, arrived)
    alpha, m = shift_of(plan, *[lane(row, i) for i in range(4)])
    beta, scale = jnp.sqrt(m), lax.rsqrt(m + epsilon)
    coef_out[0:1, :] = jnp.broadcast_to(alpha, (1, plan.D))
    coef_out[1:2, :] = jnp.broadcast_to(beta, (1, plan.D))
    sums = [jnp.zeros((8, plan.D), F32)] * 4
    for k in range(plan.T):
        at = pl.ds(k * plan.D, plan.D)
        q1, h1, z1 = q_in[at, :], h_in[at, :], z_in[at, :]
        image = jnp.where(live_mask(plan, rows, cols, k), tile(k), 0.0) + energy[k] * z1
        q = scale * (z1 - alpha * q1)
        h = scale * (image - alpha * h1)
        z = h - beta * q1
        q_out[at, :] = q
        z_out[at, :] = z
        sums = [s + folded(p) for s, p in zip(sums, (q * h, z * z, z * q, q * q))]
    return [total(s) for s in sums]


def on_chip(body, ins, outs, scratch=()):
    spaces = [SMEM if len(x.shape) == 1 else VMEM for x in ins]
    return pl.pallas_call(
        body,
        in_specs=[pl.BlockSpec(memory_space=s) for s in spaces],
        out_specs=[pl.BlockSpec(memory_space=VMEM)] * len(outs),
        out_shape=list(outs),
        scratch_shapes=list(scratch),
        compiler_params=pltpu.CompilerParams(vmem_limit_bytes=16 * 2**20),
    )(*ins)


def in_odd_segment():
    return lax.axis_index("seg") % 2 == 1


class Block:
    def __init__(self, left, right, low, slots):
        self.left, self.right, self.low, self.slots = left, right, low, slots


def multiply(plan, pairs, half_ref, sum_ref):
    D, W, group = plan.D, plan.W, plan.group
    none = jnp.zeros((D, D), BF16)

    def rows(place, first, count):
        ref, block = place
        return ref[pl.ds(pl.multiple_of((block * W + first) * D, D), count * D), :]

    def several(step, carry):
        first = step * group
        for pair in pairs:
            v = [b.low[0][pl.ds(b.low[1] * D, D), :] for b in pair]
            both = jnp.concatenate(
                [jnp.concatenate([v[0], none], 1), jnp.concatenate([none, v[1]], 1)], 0
            )
            tiles = [rows(b.left, first, group) for b in pair]
            half_ref[...] = jnp.dot(
                jnp.concatenate(tiles, 1), both, preferred_element_type=F32
            ).astype(BF16)
            for w in range(group):
                r = [rows(b.right, first + w, 1) for b in pair]
                both = jnp.concatenate(
                    [jnp.concatenate([r[0], none], 1), jnp.concatenate([none, r[1]], 1)], 0
                )
                product = jnp.dot(
                    half_ref[pl.ds(w * D, D), :], both, preferred_element_type=F32
                )
                for side, b in enumerate(pair):
                    ref, block = b.slots
                    at = pl.ds(pl.multiple_of(ref[block * W + first + w] * D, D), D)
                    sum_ref[at, :] += product[:, side * D : (side + 1) * D]
        return carry

    lax.fori_loop(0, W // group, several, 0)


def scalars(plan, row, message_refs):
    for ref in message_refs[:2]:
        ref[pl.ds(plan.Z * plan.a_rows, PAD), :] = row


def flush(plan, sum_ref, message_refs):
    first = 0
    for ref in message_refs:
        rows = ref.shape[0] // plan.D * plan.D
        ref[pl.ds(0, rows), :] = sum_ref[pl.ds(first, rows), :].astype(BF16)
        first += rows


def work_space(plan):
    return [
        VMEM((plan.group * plan.D, 2 * plan.D), BF16),
        VMEM(((plan.n + 1) * plan.D, plan.D), F32),
    ]


def first_step(plan, row, roles):
    ins, places = [row], []
    for _, arrays in roles:
        for array in arrays:
            if all(array is not known for known in ins):
                ins.append(array)
        places.append([next(i for i, a in enumerate(ins) if a is array) for array in arrays])

    def body(*refs):
        n = len(ins)
        message_refs, (half_ref, sum_ref) = refs[n:-2], refs[-2:]

        def work(place):
            def at(k):
                return Block(*[(refs[i], k) for i in place])

            blocks = refs[place[0]].shape[0] // (plan.W * plan.D)
            sum_ref[...] = jnp.zeros(sum_ref.shape, F32)
            pairs = [(at(k), at(k + blocks // 2)) for k in range(blocks // 2)]
            multiply(plan, pairs, half_ref, sum_ref)

        for (segment, _), place in zip(roles, places):
            if segment is None:
                work(place)
            else:
                pl.when(lax.axis_index("seg") == segment)(functools.partial(work, place))
        flush(plan, sum_ref, message_refs)
        scalars(plan, refs[0][...], message_refs)

    return on_chip(body, ins, plan.messages(), work_space(plan))


def operator_step(plan, update, ins, state_shapes, lefts, rights, slots):
    n_in, n_state = len(ins), len(state_shapes)

    def body(*refs):
        left_refs = refs[n_in : n_in + len(lefts)]
        n = n_in + len(lefts)
        right_refs = refs[n : n + len(rights)]
        n += len(rights)
        slot_ref = refs[n]
        state_refs = refs[n + 1 : n + 1 + n_state]
        message_refs = refs[n + 1 + n_state : -3]
        low_ref, half_ref, sum_ref = refs[-3:]
        odd = in_odd_segment()

        def send(k, value):
            low_ref[pl.ds(k * plan.D, plan.D), :] = value.astype(BF16)

        row = packed_row(update(plan, refs[:n_in], state_refs, send), plan.D)
        sum_ref[...] = jnp.zeros(sum_ref.shape, F32)

        def all_of(place, right_ref):
            def at(k):
                return Block(place(k), (right_ref, k), (low_ref, k), (slot_ref, k))

            pairs = [(at(k), at(k + plan.H)) for k in range(plan.H)]
            multiply(plan, pairs, half_ref, sum_ref)

        def in_halves(k):
            return (left_refs[1], k) if k < plan.H else (left_refs[2], k - plan.H)

        if plan.shared:
            pl.when(odd)(lambda: all_of(lambda k: (left_refs[0], k), right_refs[0]))
            pl.when(jnp.logical_not(odd))(lambda: all_of(in_halves, right_refs[1]))
        else:
            all_of(lambda k: (left_refs[0], k), right_refs[0])

        flush(plan, sum_ref, message_refs)
        scalars(plan, row, message_refs)

    results = on_chip(
        body,
        list(ins) + list(lefts) + list(rights) + [slots],
        list(state_shapes) + plan.messages(),
        [VMEM((plan.T * plan.D, plan.D), BF16)] + work_space(plan),
    )
    return results[:n_state], results[n_state:]


def row_of(plan, values):
    across = lax.broadcasted_iota(jnp.int32, (8, plan.D), 1)
    row = jnp.zeros((8, plan.D), F32)
    for index, value in enumerate(values):
        row = row + jnp.where(across == index, value, 0.0)
    return row


def last_step(plan, ins, state_shapes):
    n_in = len(ins)

    def body(*refs):
        sums = update_last(plan, refs[:n_in], refs[n_in:-1])
        refs[-1][...] = row_of(plan, sums)

    row = jax.ShapeDtypeStruct((8, plan.D), F32)
    return on_chip(body, ins, list(state_shapes) + [row])


def outcome(plan, q, z, first, second, *sums):
    def body(q_ref, z_ref, first_ref, second_ref, *refs):
        added = functools.reduce(lambda x, y: x + y, [r[0:1, :] for r in refs[:-2]])
        residual_ref, coef_ref = refs[-2:]
        alpha, m = shift_of(plan, *[lane(added, i) for i in range(4)])
        residual_ref[...] = z_ref[...] - alpha * q_ref[...]
        values = [first_ref[0:1, 0:1], second_ref[0:1, 0:1], alpha]
        values += [first_ref[1:2, 0:1], second_ref[1:2, 0:1], jnp.sqrt(m)]
        coef_ref[...] = row_of(plan, values)[0:1, 0 : len(values)]

    row = jax.ShapeDtypeStruct((1, 6), F32)
    return on_chip(body, [q, z, first, second, *sums], [q, row])


def middle_a(plan, keep, got):
    rows = plan.a_rows

    def body(keep_ref, got_ref, *outs):
        end = pl.ds(plan.Z * rows, PAD)
        row = split_row(joined_row(keep_ref[end, :]) + joined_row(got_ref[end, :]), plan.D)
        for z, out in enumerate(outs):
            at = pl.ds(z * rows, rows)
            added = keep_ref[at, :].astype(F32) + got_ref[at, :].astype(F32)
            out[pl.ds(0, rows), :] = added.astype(BF16)
            out[pl.ds(rows, PAD), :] = row

    shape = jax.ShapeDtypeStruct((rows + PAD, plan.D), BF16)
    return on_chip(body, [keep, got], [shape] * plan.Z)


def middle_b(plan, parts):
    rows = plan.b_rows

    def body(*refs):
        for y, out in enumerate(refs[plan.Z :]):
            at = pl.ds(y * rows, rows)
            tiles = [p[at, :].astype(F32) for p in refs[: plan.Z]]
            out[...] = functools.reduce(lambda u, v: u + v, tiles).astype(out.dtype)

    shapes = [jax.ShapeDtypeStruct((rows, plan.D), d) for d in (F32, BF16)]
    return on_chip(body, parts, shapes)


def exchanged(plan, messages, turn):
    keep, send, b_parts = messages[0], messages[1], messages[2:]
    others = range(plan.Z - 1, 0, -1)
    got = swapped(send, 1)
    swap = swapped_but_first if turn else swapped
    b_got = [swap(b_parts[z], 2 * z) for z in others]
    a_parts = middle_a(plan, keep, got)
    a_last = [swapped(a_parts[z], 2 * z) for z in others]
    b_keep, b_send = middle_b(plan, [b_parts[0]] + b_got)
    b_last = swapped(b_send, 1)
    return [a_parts[0]] + a_last[::-1] + [b_keep, b_last]


def gathered(plan, arrived, dtype):
    def body(*refs):
        tile, _ = received_sums(plan, refs[:-1])
        for k in range(plan.T):
            refs[-1][pl.ds(k * plan.D, plan.D), :] = tile(k).astype(dtype)

    sums = jax.ShapeDtypeStruct((plan.T * plan.D, plan.D), dtype)
    return on_chip(body, arrived, [sums])[0]


PIECES = 4


def pieces_of(source, first, target, done, rows):
    piece = rows // PIECES
    return [
        pltpu.make_async_copy(
            source.at[pl.ds(first + i * piece, piece)], target.at[pl.ds(i * piece, piece)], done.at[i]
        )
        for i in range(PIECES)
    ]


def run(copies, after=None):
    for copy in copies:
        copy.start()
    if after is not None:
        after()
    for copy in copies:
        copy.wait()


def in_hbm(x):
    return pltpu.with_memory_space_constraint(x, pltpu.HBM)


def copying(sources, even, odd, rows):
    n = len(sources)

    def body(*refs):
        def one(choice):
            source, first = choice
            run(pieces_of(refs[source], first, refs[n], refs[n + 1], rows))

        pl.when(jnp.logical_not(in_odd_segment()))(lambda: one(even))
        pl.when(in_odd_segment())(lambda: one(odd))

    return pl.pallas_call(
        body,
        in_specs=[pl.BlockSpec(memory_space=pl.ANY)] * n,
        out_specs=pl.BlockSpec(memory_space=VMEM),
        out_shape=jax.ShapeDtypeStruct((rows, sources[0].shape[1]), sources[0].dtype),
        scratch_shapes=[pltpu.SemaphoreType.DMA((PIECES,))],
        compiler_params=pltpu.CompilerParams(vmem_limit_bytes=16 * 2**20),
    )(*[in_hbm(x) for x in sources])


def prepared(plan, start, rows, cols, feeds, left, right):
    every = right.shape[0]
    half = every // 2

    def body(start_ref, rows_ref, cols_ref, feed_ref, left_ref, right_ref, *outs):
        x_ref, low_ref, row_ref, slot_ref, last_low_ref, last_slot_ref = outs[:6]
        held_left_ref, held_right_ref, done = outs[6:]
        me = lax.axis_index("blk")

        def send(k, value):
            low_ref[pl.ds(k * plan.D, plan.D), :] = value.astype(BF16)
            if k >= plan.H:
                last_low_ref[pl.ds((k - plan.H) * plan.D, plan.D), :] = value.astype(BF16)

        def several(w, carry):
            for k in range(plan.T):
                slot = plan.slot(feed_ref[k, w], me)
                slot_ref[k * plan.W + w] = slot
                if k >= plan.H:
                    last_slot_ref[(k - plan.H) * plan.W + w] = slot
            return carry

        def compute():
            lax.fori_loop(0, plan.W, several, 0)
            sums = update_first(plan, (start_ref, rows_ref, cols_ref), (x_ref,), send)
            row_ref[...] = packed_row(sums, plan.D)

        def all_right():
            run(pieces_of(right_ref, 0, held_right_ref, done, every), compute)

        def last_left():
            run(pieces_of(left_ref, half, held_left_ref, done, half), compute)

        if plan.shared:
            pl.when(jnp.logical_not(in_odd_segment()))(all_right)
            pl.when(in_odd_segment())(last_left)
        else:
            all_right()

    chip = pl.BlockSpec(memory_space=VMEM)
    scalar = pl.BlockSpec(memory_space=SMEM)
    anywhere = pl.BlockSpec(memory_space=pl.ANY)
    last = plan.T - plan.H
    return pl.pallas_call(
        body,
        in_specs=[chip, scalar, scalar, scalar, anywhere, anywhere],
        out_specs=[chip, chip, chip, scalar, chip, scalar, chip, chip],
        out_shape=[
            jax.ShapeDtypeStruct(start.shape, F32),
            jax.ShapeDtypeStruct(start.shape, BF16),
            jax.ShapeDtypeStruct((PAD, plan.D), BF16),
            jax.ShapeDtypeStruct((plan.T * plan.W,), jnp.int32),
            jax.ShapeDtypeStruct((last * plan.D, plan.D), BF16),
            jax.ShapeDtypeStruct((last * plan.W,), jnp.int32),
            jax.ShapeDtypeStruct((half, plan.D), BF16),
            jax.ShapeDtypeStruct((every, plan.D), BF16),
        ],
        scratch_shapes=[pltpu.SemaphoreType.DMA((PIECES,))],
        compiler_params=pltpu.CompilerParams(vmem_limit_bytes=16 * 2**20),
        name="prepared",
    )(start, rows, cols, feeds, in_hbm(left), in_hbm(right))


def plain_start(plan, left, right, start, rows, cols, feeds):
    segments = range(1, lax.axis_size("seg"))
    arrived_left = handed(left, segments, 1)
    x, low, square, slots, _, _, _, held_right = prepared(
        plan, start, rows, cols, feeds, left, right
    )
    messages = first_step(plan, square, [(None, [arrived_left, held_right, low, slots])])
    return x, slots, [arrived_left], [held_right], exchanged(plan, messages, 0)


def shared_start(plan, left, right, start, rows, cols, feeds):
    every = right.shape[0]
    half = every // 2
    helped, helper = plan.helped, plan.helped - 1

    sent = copying([left, right], (1, half), (0, 0), half)
    crossed = lax.ppermute(sent, "seg", [(helper, helped), (helped, helper)])
    own_side = copying([left, right], (0, 0), (1, 0), every)
    partner = swapped(own_side, 1, "seg")
    x, low, square, slots, last_low, last_slots, held_left, held_right = prepared(
        plan, start, rows, cols, feeds, left, right
    )
    other_low = handed(last_low, [helper], -1)
    other_slots = handed(last_slots, [helper], -1)
    partner_low = handed(low, [helper - 1], -1)
    partner_slots = handed(slots, [helper - 1], -1)
    left_last = handed(held_left, [helped], 1)

    roles = [
        (helper - 1, [own_side, partner, partner_low, partner_slots]),
        (helper, [held_left, crossed, other_low, other_slots]),
        (helped, [crossed, held_right, low, slots]),
        (helped + 1, [partner, own_side, low, slots]),
    ]
    messages = first_step(plan, square, roles)
    arrived = exchanged(plan, messages, 0)
    sums = gathered(plan, arrived, BF16)
    got = handed(sums, [helper, helped], 1)
    lefts, rights = [partner, crossed, left_last], [own_side, held_right]
    return x, slots, lefts, rights, [got] + arrived


def local(
    start_vector,
    left_environment,
    right_environment,
    block_energy,
    sector_rows,
    sector_cols,
    feed_block,
):
    T, W, D = left_environment.shape[1:4]
    plan = Plan(T, W, D, lax.axis_size("blk"), lax.axis_size("seg"))
    left = left_environment.reshape(T * W * D, D)
    right = right_environment.reshape(T * W * D, D)
    rows, cols, energy = sector_rows[0], sector_cols[0], block_energy[0]
    vector = jax.ShapeDtypeStruct((T * D, D), F32)
    row = jax.ShapeDtypeStruct((8, D), F32)
    start = start_vector.reshape(T * D, D)
    first = shared_start if plan.shared else plain_start
    x, slots, lefts, rights, arrived = first(
        plan, left, right, start, rows, cols, feed_block[0]
    )
    (q0, h0, known), messages = operator_step(
        plan,
        update_second,
        [x, rows, cols, energy] + arrived,
        [vector, vector, row],
        lefts,
        rights,
        slots,
    )
    arrived = exchanged(plan, messages, 1)
    (q1, h1, z1, first), messages = operator_step(
        plan,
        update_third,
        [q0, h0, known, rows, cols, energy] + arrived,
        [vector, vector, vector, row],
        lefts,
        rights,
        slots,
    )
    arrived = exchanged(plan, messages, 2)
    q2, z2, second, sums = last_step(
        plan, [q1, h1, z1, rows, cols, energy] + arrived, [vector, vector, row]
    )
    mask = 1
    while 2 * mask < plan.B:
        sums = sums + swapped(sums, mask)
        mask *= 2
    last = swapped(sums, mask)
    residual, coefficients = outcome(plan, q2, z2, first, second, sums, last)
    return (coefficients, residual.reshape(1, T, D, D))


def solution(mesh):
    return jax.shard_map(
        local,
        mesh=mesh,
        in_specs=(
            P("seg", "blk", None, None),
            P("seg", "blk", None, None, None),
            P("seg", "blk", None, None, None),
            P("seg", "blk"),
            P("seg", "blk"),
            P("seg", "blk"),
            P("seg", "blk", None),
        ),
        out_specs=(P("seg", None), P("seg", "blk", None, None)),
        check_vma=False,
    )
```
